32 devices in a mesh: group: 2 (over y), tm: 8 (over z, core), pix: 2 (over x), sub: 1.
Axes of the slice: x: 2, y: 2, z: 4, core: 2. Of those that a mesh axis runs over, the one named last changes fastest.
Arguments:
- anomaly: bfloat16 [512, 65536], P('tm', ('group', 'pix', 'sub')), parts along dimension 1, may hold values from -6 to 6
- offsets: int32 [32], replicated, may hold values from 0 to 256, as said below
- taper_index: int32 [32], replicated, may hold values from 0 to 3
Outputs:
- spectral_gram: float32 [256, 64, 64], P(('group', 'tm')), parts along dimension 0
- leading_energy: float32 [256], P(('group', 'tm')), parts along dimension 0
The draws below stay inside these ranges and needn't reach their ends.
There are 2 independent parts, one for each index of `group`. The reference program is written for one: setup_inputs(seed, part) draws one part's arguments, and reference() takes and returns one part's arrays. A program takes and returns all parts, laid end to end along the dimension named above; an argument that names none is the same for every part. Nothing has to cross between parts.
Inputs may be any that keep to these rules, and one draw needn't show every extreme that they name: `offsets`: block starts never fall; the first block starts at day 0 and the last at day 512 - 256.
All inputs are finite; a program needn't handle non-finite values.
Results may differ from the reference program's by a relative error of at most 0.0034.
Values may be sent and summed in bfloat16 or wider, within the bound.
A program may use at most 128 MiB of HBM per device.

```python
import math
import jax
import jax.numpy as jnp
from jax import lax

NFFT = 256
NB = 32
POWER = 8
PIX_DEV = 16384
NF = 128
DAYS = 512
PIXELS = 32768


def draw_offsets(key, part):
    stride = (DAYS - NFFT) // (NB - 1)
    jitter = jax.random.randint(key, (NB,), 0, stride // 2 + 1)
    blocks = jnp.arange(NB, dtype=jnp.int32)
    starts = blocks * stride + jitter.astype(jnp.int32)
    starts = jnp.where(blocks == 0, 0, starts)
    starts = jnp.where(blocks == NB - 1, DAYS - NFFT, starts)
    return starts.astype(jnp.int32)


def set_ends(values, rng, smallest, top_value):
    dims = values.shape
    place = [jax.random.randint(jax.random.fold_in(rng, axis), (), 0, dims[axis]) for axis in range(len(dims))]
    values = values.at[tuple(place)].set(smallest)
    longest = dims.index(max(dims))
    place[longest] = (place[longest] + 1) % dims[longest]
    return values.at[tuple(place)].set(top_value)


def levels(key, extent, pieces, smallest, largest):
    def one(position, blocks):
        steps = jax.random.uniform(jax.random.fold_in(jax.random.fold_in(key, 6), position), (blocks,), jnp.float32, smallest / len(pieces), largest / len(pieces))
        return jnp.repeat(jnp.exp(steps), extent[position] // blocks).reshape((-1,) + (1,) * (len(extent) - position - 1))

    loudness = one(*pieces[0])
    for cut in pieces[1:]:
        loudness = loudness * one(*cut)
    return loudness


def scatter_about(rng, shape, scale, bound, pieces=(), kind=jnp.bfloat16):
    result = scale * jax.random.normal(rng, shape, jnp.float32)
    if pieces:
        result = result * levels(rng, shape, pieces, -0.22, 0.18)
    return jnp.clip(result, -bound, bound).astype(kind)


def setup_inputs(seed: int = 0, part: int = 0) -> dict:
    streams_of = jax.random.split(jax.random.key(seed), 4)
    part_keys = jax.random.split(jax.random.fold_in(streams_of[3], part), 4)
    anomaly = scatter_about(part_keys[0], (DAYS, PIXELS), 1.0, 6.0, ((0, 8), (1, 2)))
    offsets = draw_offsets(jax.random.fold_in(streams_of[3], 71), part)
    taper_index = set_ends(jax.random.randint(streams_of[2], (NB,), 0, 4), jax.random.fold_in(streams_of[2], 1), 0, 3).astype(jnp.int32)
    return dict(anomaly=anomaly, offsets=offsets, taper_index=taper_index)


power_eps = 1e-06

def window_rows(taper_index, length):
    steps_t = jnp.arange(length, dtype=jnp.float32)
    phase = steps_t * (2.0 * math.pi / length)
    center = (steps_t + 0.5) * (math.pi / length)
    hann = jnp.sin(center) ** 2
    hamming = 0.54 - 0.46 * jnp.cos(phase)
    blackman = 0.42 - 0.5 * jnp.cos(phase) + 0.08 * jnp.cos(2.0 * phase)
    sine_win = jnp.sin(center)
    table_rows = jnp.stack([hann, hamming, blackman, sine_win])
    chosen = jnp.zeros((taper_index.shape[0], length), jnp.float32)
    for which in range(4):
        chosen = chosen + jnp.where(taper_index[:, None] == which, table_rows[which][None, :], jnp.float32(0.0))
    return chosen

def dft_table(length, kept):
    freqs = jnp.arange(kept, dtype=jnp.int32)
    times = jnp.arange(length, dtype=jnp.int32)
    product = freqs[:, None] * times[None, :] % length
    angle = product.astype(jnp.float32) * (2.0 * math.pi / length)
    return jnp.stack([jnp.cos(angle), -jnp.sin(angle)]).astype(jnp.bfloat16)

def reference(anomaly, offsets, taper_index):
    windows = window_rows(taper_index, NFFT)
    energy = 1.0 / jnp.sqrt(lax.optimization_barrier(jnp.sum(windows * windows, axis=1)))
    transform = dft_table(NFFT, NF).astype(jnp.float32)
    spans = PIXELS // PIX_DEV

    def one_span(running, span_index):
        columns = lax.dynamic_slice_in_dim(anomaly, (span_index * PIX_DEV).astype(jnp.int32), PIX_DEV, 1)
        segments = jax.vmap(lambda first_day: lax.dynamic_slice_in_dim(columns, first_day.astype(jnp.int32), NFFT, 0))(offsets)
        windowed = (segments.astype(jnp.float32) * windows[:, :, None]).astype(jnp.bfloat16)
        spectra = jnp.einsum('rkt,btp->rbkp', transform, windowed.astype(jnp.float32))
        spectra = (spectra * energy[None, :, None, None]).astype(jnp.bfloat16)
        stacked = spectra.reshape(2 * NB, NF, PIX_DEV).astype(jnp.float32)
        return (running + jnp.einsum('ifp,jfp->fij', stacked, stacked), None)
    start_sum = jnp.zeros((NF, 2 * NB, 2 * NB), jnp.float32)
    summed, _ = lax.scan(one_span, start_sum, jnp.arange(spans, dtype=jnp.int32))
    spectral_gram = summed / PIXELS
    vector = jnp.ones((NF, 2 * NB), jnp.float32)
    for _ in range(POWER):
        applied = jnp.einsum('fij,fj->fi', spectral_gram, vector, precision=lax.Precision.HIGHEST)
        vector = applied / jnp.sqrt(lax.optimization_barrier(jnp.mean(applied * applied, axis=1, keepdims=True)) + power_eps)
    applied = jnp.einsum('fij,fj->fi', spectral_gram, vector, precision=lax.Precision.HIGHEST)
    leading_energy = jnp.sqrt(lax.optimization_barrier(jnp.mean(applied * applied, axis=1)))
    return (spectral_gram, leading_energy)
```

```python
import functools
import math

import jax
import jax.numpy as jnp
from jax import lax
from jax.experimental import pallas as pl
from jax.experimental.pallas import tpu as pltpu
from jax.sharding import PartitionSpec as P

NFFT = 256
NB = 32
POWER = 8
NF = 128


power_eps = 1e-06


CHUNKS = 4


DIRECT_VMEM = 40 * 2**20


def windows_of(taper, step, length):
    steps = step.astype(jnp.float32)
    phase = steps * (2.0 * math.pi / length)
    center = (steps + 0.5) * (math.pi / length)
    sine_win = jnp.sin(center)
    hann = sine_win * sine_win
    hamming = 0.54 - 0.46 * jnp.cos(phase)
    blackman = 0.42 - 0.5 * jnp.cos(phase) + 0.08 * jnp.cos(2.0 * phase)
    chosen = jnp.where(
        taper == 0, hann, jnp.where(taper == 1, hamming, jnp.where(taper == 2, blackman, sine_win))
    )
    return jnp.where((step >= 0) & (step < length), chosen, 0.0)


def upright(row):
    square = (NB, NB)
    diagonal = lax.broadcasted_iota(jnp.int32, square, 0) == lax.broadcasted_iota(jnp.int32, square, 1)
    values = jnp.broadcast_to(row[...].astype(jnp.float32), square)
    return jnp.sum(jnp.where(diagonal, values, 0.0), axis=1, keepdims=True).astype(jnp.int32)


def split(value):
    high = value.astype(jnp.bfloat16)
    return high, (value - high.astype(jnp.float32)).astype(jnp.bfloat16)


def write_operator(offsets, taper, operator, operator_low):
    own, _, days = operator.shape
    step = lax.broadcasted_iota(jnp.int32, (NB, days), 1) - upright(offsets)
    windows = windows_of(jnp.broadcast_to(upright(taper), (NB, days)), step, NFFT)
    scaled = windows * (1.0 / jnp.sqrt(jnp.sum(windows * windows, axis=1, keepdims=True)))
    first = lax.axis_index("tm") * own

    def one(f, carry):
        angle = (((first + f) * step) & (NFFT - 1)).astype(jnp.float32) * (2.0 * math.pi / NFFT)
        for rows, table in ((pl.ds(0, NB), jnp.cos(angle)), (pl.ds(NB, NB), -jnp.sin(angle))):
            high, low = split(table.astype(jnp.bfloat16).astype(jnp.float32) * scaled)
            operator[f, rows, :] = high
            operator_low[f, rows, :] = low
        return carry

    lax.fori_loop(0, own, one, 0)


BLOCK = 128
MESH = pl.DeviceIdType.MESH


def stages_of(tm, pix, sub):
    if sub > 1 or tm % 2:
        split = [("sub", 1, sub), ("pix", 1, pix), ("tm", 1, tm)]
    else:
        split = [("tm", 1, 2), ("pix", 1, pix), ("tm", 2, tm // 2)]
    return split


def place_in(stage):
    axis, inner, members = stage
    return lax.rem(lax.axis_index(axis) // inner, members)


def device_at(stage, shift):
    axis, inner, members = stage
    index = lax.axis_index(axis)
    here = place_in(stage)
    there = lax.rem(here + shift, members)
    return {axis: index + (there - here) * inner}, there


def add_products(series, packed, first):
    blocks = series.shape[0] // BLOCK
    place = 0
    for i in range(blocks):
        strip = lax.dot_general(
            series[i * BLOCK : (i + 1) * BLOCK, :],
            series[i * BLOCK :, :],
            (((1,), (1,)), ((), ())),
            preferred_element_type=jnp.float32,
        )
        for j in range(blocks - i):
            rows = pl.ds((place + j) * BLOCK, BLOCK)
            block = strip[:, j * BLOCK : (j + 1) * BLOCK]
            packed[rows, :] = block if first else packed[rows, :] + block
        place += blocks - i


def covariance_kernel(
    stages, anomaly, offsets, taper, out, operator, operator_low, series, packed, gathered, own_sem, *scratch
):
    exchange_send, exchange_recv = scratch[:2]
    landing, sems = scratch[2:5], scratch[5:]
    chunks, days, width = series.shape
    per_device = anomaly.shape[0]
    peers = days // per_device
    me = lax.axis_index("tm")

    barrier = pltpu.get_barrier_semaphore()
    greeted = 0
    for axis in ("tm", "pix", "sub"):
        members = lax.axis_size(axis)
        for shift in range(1, members):
            device = {axis: lax.rem(lax.axis_index(axis) + shift, members)}
            pl.semaphore_signal(barrier, inc=1, device_id=device, device_id_type=MESH)
            greeted += 1
    my_rows = pl.ds(pl.multiple_of(me * per_device, per_device), per_device)

    def columns(device, chunk):
        return pl.ds(pl.multiple_of(device * (chunks * width) + chunk * width, width), width)

    kept = []
    for chunk in range(chunks):
        copy = pltpu.make_async_copy(
            anomaly.at[:, columns(me, chunk)], series.at[chunk, my_rows, :], own_sem.at[chunk]
        )
        copy.start()
        kept.append(copy)
    pl.semaphore_wait(barrier, greeted)
    farthest_first = sorted(range(1, peers), key=lambda shift: abs(2 * shift - peers))
    exchanged = []
    for chunk in range(chunks):
        copies = []
        for shift in farthest_first:
            there = lax.rem(me + shift, peers)
            copy = pltpu.make_async_remote_copy(
                src_ref=anomaly.at[:, columns(there, chunk)],
                dst_ref=series.at[chunk, my_rows, :],
                send_sem=exchange_send.at[chunk, shift - 1],
                recv_sem=exchange_recv.at[chunk, shift - 1],
                device_id={"tm": there},
                device_id_type=MESH,
            )
            copy.start()
            copies.append(copy)
        exchanged.append(copies)

    write_operator(offsets, taper, operator, operator_low)
    blocks = days // BLOCK
    filled = blocks * (blocks + 1) // 2 * BLOCK
    if packed.shape[0] > filled:
        packed[filled:, :] = jnp.zeros((packed.shape[0] - filled, BLOCK), jnp.float32)
    for chunk in range(chunks):
        kept[chunk].wait()
        for copy in exchanged[chunk]:
            copy.wait()
        add_products(series.at[chunk], packed, chunk == 0)

    near, side, line = stages
    piece = packed.shape[0] // line[2]
    half = piece // near[2]
    part = half // side[2]

    def rows_of(at, n, s, rows):
        return pl.ds(pl.multiple_of(at * piece + n * half + s * part, 8), rows)

    def send(src, dst, sem, index, device):
        copy = pltpu.make_async_remote_copy(
            src_ref=src,
            dst_ref=dst,
            send_sem=sems[2 * sem].at[index],
            recv_sem=sems[2 * sem + 1].at[index],
            device_id=device,
            device_id_type=MESH,
        )
        copy.start()
        return copy

    my_near, my_side = place_in(near), place_in(side)
    order = list(range(1, line[2])) + [0]
    order.sort(key=lambda shift: abs(2 * shift - line[2]))
    targets = {shift: device_at(line, shift) for shift in order}

    near_copies, side_copies, line_copies = {}, {}, {}
    for shift in order:
        at = targets[shift][1]
        near_copies[shift] = []
        for k in range(1, near[2]):
            device, there = device_at(near, k)
            index = shift * (near[2] - 1) + k - 1
            src = packed.at[rows_of(at, there, 0, half), :]
            near_copies[shift].append(send(src, landing[0].at[index], 0, index, device))
    for shift in order:
        at = targets[shift][1]
        mine = packed.at[rows_of(at, my_near, 0, half), :]
        total = mine[...]
        for k, copy in enumerate(near_copies[shift]):
            copy.wait()
            total = total + landing[0][shift * (near[2] - 1) + k]
        mine[...] = total
        side_copies[shift] = []
        for k in range(1, side[2]):
            device, there = device_at(side, k)
            index = shift * (side[2] - 1) + k - 1
            src = packed.at[rows_of(at, my_near, there, part), :]
            side_copies[shift].append(send(src, landing[1].at[index], 1, index, device))
    for shift in order:
        device, at = targets[shift]
        mine = packed.at[rows_of(at, my_near, my_side, part), :]
        total = mine[...]
        for k, copy in enumerate(side_copies[shift]):
            copy.wait()
            total = total + landing[1][shift * (side[2] - 1) + k]
        mine[...] = total
        if shift:
            line_copies[shift] = send(mine, landing[2].at[shift - 1], 2, shift - 1, device)
    here = place_in(line)
    own = gathered.at[rows_of(here, my_near, my_side, part), :]
    total = packed[rows_of(here, my_near, my_side, part), :]
    for shift in order:
        if shift:
            line_copies[shift].wait()
            total = total + landing[2][shift - 1]
    own[...] = total

    arriving = {}
    for shift in order:
        if shift:
            arriving[shift] = send(own, own, 3, shift - 1, targets[shift][0])
    spread, near_spread = {}, []
    incoming = [0] + [shift for shift in order if shift]
    sources = {shift: lax.rem(here + line[2] - shift, line[2]) for shift in incoming}
    for shift in incoming:
        if shift:
            arriving[shift].wait()
        mine = gathered.at[rows_of(sources[shift], my_near, my_side, part), :]
        spread[shift] = [
            send(mine, mine, 4, shift * (side[2] - 1) + k - 1, device_at(side, k)[0])
            for k in range(1, side[2])
        ]
    for shift in incoming:
        for copy in spread[shift]:
            copy.wait()
        mine = gathered.at[rows_of(sources[shift], my_near, 0, half), :]
        near_spread += [
            send(mine, mine, 5, shift * (near[2] - 1) + k - 1, device_at(near, k)[0])
            for k in range(1, near[2])
        ]
    for copy in near_spread:
        copy.wait()

    place = 0
    for i in range(blocks):
        for j in range(i, blocks):
            block = gathered[pl.ds(place * BLOCK, BLOCK), :]
            out[pl.ds(i * BLOCK, BLOCK), pl.ds(j * BLOCK, BLOCK)] = block
            if j > i:
                out[pl.ds(j * BLOCK, BLOCK), pl.ds(i * BLOCK, BLOCK)] = block.T
            place += 1


def covariance_and_operator(anomaly, offsets, taper_index):
    per_device, pixels = anomaly.shape
    peers = lax.axis_size("tm")
    days = per_device * peers
    own = NF // peers
    stages = stages_of(peers, lax.axis_size("pix"), lax.axis_size("sub"))
    devices = math.prod(stage[2] for stage in stages)
    blocks = days // BLOCK
    rows = -(-(blocks * (blocks + 1) // 2 * BLOCK) // (8 * devices)) * 8 * devices
    near, side, line = (stage[2] for stage in stages)
    half = rows // line // near
    part = half // side
    slots = [max(1, count) for count in (line * (near - 1), line * (side - 1), line - 1)]
    landing = [
        pltpu.VMEM((count, depth, BLOCK), jnp.float32)
        for count, depth in zip(slots, (half, part, part))
    ]
    sems = [
        pltpu.SemaphoreType.DMA((slots[stage],)) for stage in (0, 1, 2, 2, 1, 0) for _ in range(2)
    ]
    words = rows * BLOCK * 2 + days * days + own * 2 * NB * days + days * (pixels // peers) // 2
    words += sum(count * depth * BLOCK for count, depth in zip(slots, (half, part, part)))
    vmem = pl.BlockSpec(memory_space=pltpu.VMEM)
    return pl.pallas_call(
        functools.partial(covariance_kernel, stages),
        out_shape=(
            jax.ShapeDtypeStruct((days, days), jnp.float32),
            jax.ShapeDtypeStruct((own, 2 * NB, days), jnp.bfloat16),
            jax.ShapeDtypeStruct((own, 2 * NB, days), jnp.bfloat16),
        ),
        in_specs=[pl.BlockSpec(memory_space=pltpu.HBM), vmem, vmem],
        out_specs=(vmem, vmem, vmem),
        scratch_shapes=[
            pltpu.VMEM((CHUNKS, days, pixels // peers // CHUNKS), jnp.bfloat16),
            pltpu.VMEM((rows, BLOCK), jnp.float32),
            pltpu.VMEM((rows, BLOCK), jnp.float32),
            pltpu.SemaphoreType.DMA((CHUNKS,)),
            pltpu.SemaphoreType.DMA((CHUNKS, peers - 1)),
            pltpu.SemaphoreType.DMA((CHUNKS, peers - 1)),
        ]
        + landing
        + sems,
        compiler_params=pltpu.CompilerParams(
            collective_id=0, has_side_effects=True, vmem_limit_bytes=4 * words + 8 * 2**20
        ),
        name="covariance",
    )(anomaly, offsets[None, :], taper_index[None, :])


def finish_kernel(pixels, covariance, operator, operator_low, gram, lead, high, low):
    own, size, days = operator.shape
    high[...], low[...] = split(covariance[...])
    group = math.gcd(own, 4)

    def product(left, right, contract):
        return lax.dot_general(
            left, right, (((1,), (contract,)), ((), ())), preferred_element_type=jnp.float32
        )

    for first in range(0, own, group):
        left = operator[first : first + group].reshape(group * size, days)
        left_low = operator_low[first : first + group].reshape(group * size, days)
        half = product(left, high[...], 0) + (
            product(left_low, high[...], 0) + product(left, low[...], 0)
        )
        half_high, half_low = split(half)
        for f in range(group):
            rows = slice(f * size, (f + 1) * size)
            right, right_low = operator[first + f], operator_low[first + f]
            value = product(half_high[rows], right, 1) + (
                product(half_low[rows], right, 1) + product(half_high[rows], right_low, 1)
            )
            gram[first + f] = value / pixels

    matrix = gram[...]
    vector = jnp.ones((own, 1, size), jnp.float32)
    for step in range(POWER + 1):
        across = 2 - step % 2
        applied = jnp.sum(matrix * vector, axis=across, keepdims=True)
        power = jnp.sum(applied * applied, axis=3 - across, keepdims=True) / size
        vector = applied / jnp.sqrt(power + power_eps)
    column = jnp.broadcast_to(jnp.sqrt(power)[:, 0, :], (own, own))
    square = (own, own)
    diagonal = lax.broadcasted_iota(jnp.int32, square, 0) == lax.broadcasted_iota(jnp.int32, square, 1)
    lead[...] = jnp.sum(jnp.where(diagonal, column, 0.0), axis=0, keepdims=True)


def gram_and_leading(covariance, operator, operator_low, pixels):
    own, size, days = operator.shape
    vmem = pl.BlockSpec(memory_space=pltpu.VMEM)
    gram, lead = pl.pallas_call(
        functools.partial(finish_kernel, pixels),
        out_shape=(
            jax.ShapeDtypeStruct((own, size, size), jnp.float32),
            jax.ShapeDtypeStruct((1, own), jnp.float32),
        ),
        in_specs=[vmem] * 3,
        out_specs=(vmem, vmem),
        scratch_shapes=[pltpu.VMEM((days, days), jnp.bfloat16)] * 2,
        compiler_params=pltpu.CompilerParams(
            vmem_limit_bytes=8 * days * days + 4 * own * size * days + 12 * 2**20
        ),
        name="finish",
    )(covariance, operator, operator_low)
    return gram, lead[0]


def row_scale(shape, axis):
    day = lax.broadcasted_iota(jnp.int32, shape, axis)
    return 1.0 + ((((day * day) * 40503) >> 4) & 1023).astype(jnp.float32) * (1.0 / 1024.0)


def write_scaled_operator(offsets, taper, operator):
    own, _, days = operator.shape
    step = lax.broadcasted_iota(jnp.int32, (NB, days), 1) - upright(offsets)
    windows = windows_of(jnp.broadcast_to(upright(taper), (NB, days)), step, NFFT)
    scaled = windows * (1.0 / jnp.sqrt(jnp.sum(windows * windows, axis=1, keepdims=True)))
    scaled = scaled / row_scale((NB, days), 1)
    first = lax.axis_index("tm") * own

    def one(f, carry):
        angle = (((first + f) * step) & (NFFT - 1)).astype(jnp.float32) * (2.0 * math.pi / NFFT)
        for rows, table in ((pl.ds(0, NB), jnp.cos(angle)), (pl.ds(NB, NB), -jnp.sin(angle))):
            operator[f, rows, :] = (table.astype(jnp.bfloat16).astype(jnp.float32) * scaled).astype(jnp.bfloat16)
        return carry

    lax.fori_loop(0, own, one, 0)


def write_scale(scale, blocks):
    column, row = row_scale((blocks * BLOCK, BLOCK), 0), row_scale((8, blocks * BLOCK), 1)[:1]
    place = 0
    for i in range(blocks):
        for j in range(i, blocks):
            block = column[i * BLOCK : (i + 1) * BLOCK, :] * row[:, j * BLOCK : (j + 1) * BLOCK]
            scale[pl.ds(place * BLOCK, BLOCK), :] = block
            place += 1


def direct_kernel(
    anomaly,
    offsets,
    taper,
    out,
    operator,
    series,
    packed,
    scale,
    near_land,
    outbox,
    landing,
    gathered,
    small,
    own_sem,
    small_sem,
    exchange_send,
    exchange_recv,
    near_send,
    near_recv,
    part_send,
    part_recv,
    whole_send,
    whole_recv,
    pass_send,
    pass_recv,
):
    chunks, days, width = series.shape
    per_device = anomaly.shape[0]
    peers = days // per_device
    across = lax.axis_size("pix")
    chips = peers // 2
    me, side = lax.axis_index("tm"), lax.axis_index("pix")
    core, chip = lax.rem(me, 2), lax.div(me, 2)

    barrier = pltpu.get_barrier_semaphore()
    greeted = 0
    for shift in range(peers):
        for turn in range(across):
            if shift or turn:
                device = {"tm": lax.rem(me + shift, peers), "pix": lax.rem(side + turn, across)}
                pl.semaphore_signal(barrier, inc=1, device_id=device, device_id_type=MESH)
                greeted += 1
    my_rows = pl.ds(pl.multiple_of(me * per_device, per_device), per_device)

    def columns(device, chunk):
        return pl.ds(pl.multiple_of(device * (chunks * width) + chunk * width, width), width)

    loads = [
        pltpu.make_async_copy(offsets, small.at[0:1, :], small_sem.at[0]),
        pltpu.make_async_copy(taper, small.at[8:9, :], small_sem.at[1]),
    ]
    for load in loads:
        load.start()
    kept = []
    for chunk in range(chunks):
        copy = pltpu.make_async_copy(
            anomaly.at[:, columns(me, chunk)], series.at[chunk, my_rows, :], own_sem.at[chunk]
        )
        copy.start()
        kept.append(copy)
    pl.semaphore_wait(barrier, greeted)
    farthest_first = sorted(range(1, peers), key=lambda shift: abs(2 * shift - peers))
    exchanged = []
    for chunk in range(chunks):
        copies = []
        for shift in farthest_first:
            there = lax.rem(me + shift, peers)
            copy = pltpu.make_async_remote_copy(
                src_ref=anomaly.at[:, columns(there, chunk)],
                dst_ref=series.at[chunk, my_rows, :],
                send_sem=exchange_send.at[chunk, shift - 1],
                recv_sem=exchange_recv.at[chunk, shift - 1],
                device_id={"tm": there},
                device_id_type=MESH,
            )
            copy.start()
            copies.append(copy)
        exchanged.append(copies)

    for load in loads:
        load.wait()
    write_scaled_operator(small.at[0:1, :], small.at[8:9, :], operator)
    blocks = days // BLOCK
    write_scale(scale, blocks)
    filled = blocks * (blocks + 1) // 2 * BLOCK
    if packed.shape[0] > filled:
        packed[filled:, :] = jnp.zeros((packed.shape[0] - filled, BLOCK), jnp.float32)
        scale[filled:, :] = jnp.zeros((packed.shape[0] - filled, BLOCK), jnp.float32)
    for chunk in range(chunks):
        kept[chunk].wait()
        for copy in exchanged[chunk]:
            copy.wait()
        add_products(series.at[chunk], packed, chunk == 0)

    half = packed.shape[0] // 2
    part = half // (chips * across)

    def half_of(n):
        return pl.ds(pl.multiple_of(n * half, 16), half)

    def part_of(n, z, x):
        return pl.ds(pl.multiple_of(n * half + (z * across + x) * part, 16), part)

    def send(src, dst, sends, receives, index, device):
        copy = pltpu.make_async_remote_copy(
            src_ref=src,
            dst_ref=dst,
            send_sem=sends.at[index],
            recv_sem=receives.at[index],
            device_id=device,
            device_id_type=MESH,
        )
        copy.start()
        return copy

    neighbour = {"tm": me + 1 - 2 * core}
    copy = send(packed.at[half_of(1 - core), :], near_land, near_send, near_recv, 0, neighbour)
    copy.wait()
    total = packed[half_of(core), :] + near_land[...]
    total = total * scale[half_of(core), :]
    near_land[...] = total
    outbox[...] = total.astype(jnp.bfloat16)

    shifts = [(z, x) for z in range(chips) for x in range(across) if z or x]
    shifts.sort(key=lambda shift: abs(2 * shift[0] - chips) - 0.5 * (shift[1] > 0))

    def target(z, x):
        there, beside = lax.rem(chip + z, chips), lax.rem(side + x, across)
        return {"tm": 2 * there + core, "pix": beside}, there, beside

    parts = []
    for z, x in shifts:
        device, there, beside = target(z, x)
        index = z * across + x - 1
        parts.append(
            (index, send(outbox.at[part_of(0, there, beside), :], landing.at[index], part_send, part_recv, index, device))
        )
    total = near_land[part_of(0, chip, side), :]
    for index, copy in parts:
        copy.wait()
        total = total + landing[index].astype(jnp.float32)
    own = gathered.at[part_of(core, chip, side), :]
    own[...] = total.astype(jnp.bfloat16)

    wholes = []
    for z, x in shifts:
        device, _, _ = target(z, x)
        index = z * across + x
        wholes.append((z, x, send(own, own, whole_send, whole_recv, index - 1, device)))
    passed = [send(own, own, pass_send, pass_recv, 0, neighbour)]
    for z, x, copy in reversed(wholes):
        copy.wait()
        there, beside = lax.rem(chip + chips - z, chips), lax.rem(side + across - x, across)
        mine = gathered.at[part_of(core, there, beside), :]
        passed.append(send(mine, mine, pass_send, pass_recv, z * across + x, neighbour))
    for copy in passed:
        copy.wait()

    place = 0
    for i in range(blocks):
        for j in range(i, blocks):
            block = gathered[pl.ds(place * BLOCK, BLOCK), :]
            out[pl.ds(i * BLOCK, BLOCK), pl.ds(j * BLOCK, BLOCK)] = block
            if j > i:
                turned = block.astype(jnp.float32).T
                out[pl.ds(j * BLOCK, BLOCK), pl.ds(i * BLOCK, BLOCK)] = turned.astype(jnp.bfloat16)
            place += 1


def direct_covariance(anomaly, offsets, taper_index):
    per_device, pixels = anomaly.shape
    peers, across = lax.axis_size("tm"), lax.axis_size("pix")
    days = per_device * peers
    own = NF // peers
    blocks = days // BLOCK
    devices = peers * across
    rows = -(-(blocks * (blocks + 1) // 2 * BLOCK) // (16 * devices)) * 16 * devices
    half, part = rows // 2, rows // devices
    others = devices // 2 - 1
    vmem = pl.BlockSpec(memory_space=pltpu.VMEM)
    hbm = pl.BlockSpec(memory_space=pl.ANY)
    counts = [(1,), (others,), (others,), (others + 1,)]
    return pl.pallas_call(
        direct_kernel,
        out_shape=(
            jax.ShapeDtypeStruct((days, days), jnp.bfloat16),
            jax.ShapeDtypeStruct((own, 2 * NB, days), jnp.bfloat16),
        ),
        in_specs=[hbm, hbm, hbm],
        out_specs=(vmem, vmem),
        scratch_shapes=[
            pltpu.VMEM((CHUNKS, days, pixels // peers // CHUNKS), jnp.bfloat16),
            pltpu.VMEM((rows, BLOCK), jnp.float32),
            pltpu.VMEM((rows, BLOCK), jnp.float32),
            pltpu.VMEM((half, BLOCK), jnp.float32),
            pltpu.VMEM((half, BLOCK), jnp.bfloat16),
            pltpu.VMEM((others, part, BLOCK), jnp.bfloat16),
            pltpu.VMEM((rows, BLOCK), jnp.bfloat16),
            pltpu.VMEM((16, NB), jnp.int32),
            pltpu.SemaphoreType.DMA((CHUNKS,)),
            pltpu.SemaphoreType.DMA((2,)),
            pltpu.SemaphoreType.DMA((CHUNKS, peers - 1)),
            pltpu.SemaphoreType.DMA((CHUNKS, peers - 1)),
        ]
        + [pltpu.SemaphoreType.DMA(count) for count in counts for _ in range(2)],
        compiler_params=pltpu.CompilerParams(
            collective_id=0, has_side_effects=True, vmem_limit_bytes=DIRECT_VMEM
        ),
        name="covariance",
    )(*(pltpu.with_memory_space_constraint(each, pltpu.HBM) for each in (anomaly, offsets[None, :], taper_index[None, :])))


def leading(matrix, size):
    own = matrix.shape[0]
    vector = jnp.ones((own, 1, size), jnp.float32)
    for step in range(POWER + 1):
        across = 2 - step % 2
        applied = jnp.sum(matrix * vector, axis=across, keepdims=True)
        power = jnp.sum(applied * applied, axis=3 - across, keepdims=True) / size
        vector = applied / jnp.sqrt(power + power_eps)
    column = jnp.broadcast_to(jnp.sqrt(power)[:, 0, :], (own, own))
    square = (own, own)
    diagonal = lax.broadcasted_iota(jnp.int32, square, 0) == lax.broadcasted_iota(jnp.int32, square, 1)
    return jnp.sum(jnp.where(diagonal, column, 0.0), axis=0, keepdims=True)


def direct_finish_kernel(pixels, covariance, operator, gram, lead, held, sem):
    own, size, days = operator.shape
    group = math.gcd(own, 4)
    copies = []
    for first in range(0, own, group):
        left = operator[first : first + group].reshape(group * size, days)
        half = lax.dot_general(
            left, covariance[...], (((1,), (0,)), ((), ())), preferred_element_type=jnp.float32
        ).astype(jnp.bfloat16)
        for f in range(group):
            value = lax.dot_general(
                half[f * size : (f + 1) * size],
                operator[first + f],
                (((1,), (1,)), ((), ())),
                preferred_element_type=jnp.float32,
            )
            held[first + f] = value * (1.0 / pixels)
        chosen = pl.ds(first, group)
        copy = pltpu.make_async_copy(held.at[chosen], gram.at[chosen], sem.at[first // group])
        copy.start()
        copies.append(copy)
    lead[...] = leading(held[...], size)
    for copy in copies:
        copy.wait()


def direct_finish(covariance, operator, pixels):
    own, size, days = operator.shape
    vmem = pl.BlockSpec(memory_space=pltpu.VMEM)
    gram, lead = pl.pallas_call(
        functools.partial(direct_finish_kernel, pixels),
        out_shape=(
            jax.ShapeDtypeStruct((own, size, size), jnp.float32),
            jax.ShapeDtypeStruct((1, own), jnp.float32),
        ),
        in_specs=[vmem] * 2,
        out_specs=(pl.BlockSpec(memory_space=pl.ANY), vmem),
        scratch_shapes=[
            pltpu.VMEM((own, size, size), jnp.float32),
            pltpu.SemaphoreType.DMA((own // math.gcd(own, 4),)),
        ],
        compiler_params=pltpu.CompilerParams(vmem_limit_bytes=24 * 2**20),
        name="finish",
    )(covariance, operator)
    return gram, lead[0]


def shards(anomaly, offsets, taper_index):
    total_pixels = anomaly.shape[1] * lax.axis_size(("pix", "sub"))
    peers, sub = lax.axis_size("tm"), lax.axis_size("sub")
    if sub == 1 and peers % 2 == 0 and anomaly.shape[0] * peers <= 4 * BLOCK:
        covariance, operator = direct_covariance(anomaly, offsets, taper_index)
        return direct_finish(covariance, operator, total_pixels)
    covariance, operator, operator_low = covariance_and_operator(anomaly, offsets, taper_index)
    return gram_and_leading(covariance, operator, operator_low, total_pixels)


def solution(mesh):
    placed = (P("tm", ("group", "pix", "sub")), P(), P())
    return jax.shard_map(
        shards,
        mesh=mesh,
        in_specs=placed,
        out_specs=(P(("group", "tm"), None, None), P(("group", "tm"))),
        check_vma=False,
    )
```

```python
import functools
import math

import jax
import jax.numpy as jnp
from jax import lax
from jax.experimental import pallas as pl
from jax.experimental.pallas import tpu as pltpu
from jax.sharding import PartitionSpec as P

NFFT = 256
NB = 32
POWER = 8
NF = 128


power_eps = 1e-06


CHUNKS = 4


DIRECT_VMEM = 40 * 2**20
WIDTHS = (1792, 1536, 768)
INNER_ORDER = ((0, 1), (3, 0), (3, 1))
OUTER_ORDER = ((2, 0), (2, 1), (1, 0), (1, 1))
GATHER_ORDER = ((2, 1), (3, 1), (2, 0), (3, 0), (1, 1), (1, 0), (0, 1))


def windows_of(taper, step, length):
    steps = step.astype(jnp.float32)
    phase = steps * (2.0 * math.pi / length)
    center = (steps + 0.5) * (math.pi / length)
    sine_win = jnp.sin(center)
    hann = sine_win * sine_win
    hamming = 0.54 - 0.46 * jnp.cos(phase)
    blackman = 0.42 - 0.5 * jnp.cos(phase) + 0.08 * jnp.cos(2.0 * phase)
    chosen = jnp.where(
        taper == 0, hann, jnp.where(taper == 1, hamming, jnp.where(taper == 2, blackman, sine_win))
    )
    return jnp.where((step >= 0) & (step < length), chosen, 0.0)


def upright(row):
    square = (NB, NB)
    diagonal = lax.broadcasted_iota(jnp.int32, square, 0) == lax.broadcasted_iota(jnp.int32, square, 1)
    values = jnp.broadcast_to(row[...].astype(jnp.float32), square)
    return jnp.sum(jnp.where(diagonal, values, 0.0), axis=1, keepdims=True).astype(jnp.int32)


def split(value):
    high = value.astype(jnp.bfloat16)
    return high, (value - high.astype(jnp.float32)).astype(jnp.bfloat16)


def write_operator(offsets, taper, operator, operator_low):
    own, _, days = operator.shape
    step = lax.broadcasted_iota(jnp.int32, (NB, days), 1) - upright(offsets)
    windows = windows_of(jnp.broadcast_to(upright(taper), (NB, days)), step, NFFT)
    scaled = windows * (1.0 / jnp.sqrt(jnp.sum(windows * windows, axis=1, keepdims=True)))
    first = lax.axis_index("tm") * own

    def one(f, carry):
        angle = (((first + f) * step) & (NFFT - 1)).astype(jnp.float32) * (2.0 * math.pi / NFFT)
        for rows, table in ((pl.ds(0, NB), jnp.cos(angle)), (pl.ds(NB, NB), -jnp.sin(angle))):
            high, low = split(table.astype(jnp.bfloat16).astype(jnp.float32) * scaled)
            operator[f, rows, :] = high
            operator_low[f, rows, :] = low
        return carry

    lax.fori_loop(0, own, one, 0)


BLOCK = 128
MESH = pl.DeviceIdType.MESH


def stages_of(tm, pix, sub):
    if sub > 1 or tm % 2:
        split = [("sub", 1, sub), ("pix", 1, pix), ("tm", 1, tm)]
    else:
        split = [("tm", 1, 2), ("pix", 1, pix), ("tm", 2, tm // 2)]
    return split


def place_in(stage):
    axis, inner, members = stage
    return lax.rem(lax.axis_index(axis) // inner, members)


def device_at(stage, shift):
    axis, inner, members = stage
    index = lax.axis_index(axis)
    here = place_in(stage)
    there = lax.rem(here + shift, members)
    return {axis: index + (there - here) * inner}, there


def add_products(series, packed, first):
    blocks = series.shape[0] // BLOCK
    place = 0
    for i in range(blocks):
        strip = lax.dot_general(
            series[i * BLOCK : (i + 1) * BLOCK, :],
            series[i * BLOCK :, :],
            (((1,), (1,)), ((), ())),
            preferred_element_type=jnp.float32,
        )
        for j in range(blocks - i):
            rows = pl.ds((place + j) * BLOCK, BLOCK)
            block = strip[:, j * BLOCK : (j + 1) * BLOCK]
            packed[rows, :] = block if first else packed[rows, :] + block
        place += blocks - i


def covariance_kernel(
    stages, anomaly, offsets, taper, out, operator, operator_low, series, packed, gathered, own_sem, *scratch
):
    exchange_send, exchange_recv = scratch[:2]
    landing, sems = scratch[2:5], scratch[5:]
    chunks, days, width = series.shape
    per_device = anomaly.shape[0]
    peers = days // per_device
    me = lax.axis_index("tm")

    barrier = pltpu.get_barrier_semaphore()
    greeted = 0
    for axis in ("tm", "pix", "sub"):
        members = lax.axis_size(axis)
        for shift in range(1, members):
            device = {axis: lax.rem(lax.axis_index(axis) + shift, members)}
            pl.semaphore_signal(barrier, inc=1, device_id=device, device_id_type=MESH)
            greeted += 1
    my_rows = pl.ds(pl.multiple_of(me * per_device, per_device), per_device)

    def columns(device, chunk):
        return pl.ds(pl.multiple_of(device * (chunks * width) + chunk * width, width), width)

    kept = []
    for chunk in range(chunks):
        copy = pltpu.make_async_copy(
            anomaly.at[:, columns(me, chunk)], series.at[chunk, my_rows, :], own_sem.at[chunk]
        )
        copy.start()
        kept.append(copy)
    pl.semaphore_wait(barrier, greeted)
    farthest_first = sorted(range(1, peers), key=lambda shift: abs(2 * shift - peers))
    exchanged = []
    for chunk in range(chunks):
        copies = []
        for shift in farthest_first:
            there = lax.rem(me + shift, peers)
            copy = pltpu.make_async_remote_copy(
                src_ref=anomaly.at[:, columns(there, chunk)],
                dst_ref=series.at[chunk, my_rows, :],
                send_sem=exchange_send.at[chunk, shift - 1],
                recv_sem=exchange_recv.at[chunk, shift - 1],
                device_id={"tm": there},
                device_id_type=MESH,
            )
            copy.start()
            copies.append(copy)
        exchanged.append(copies)

    write_operator(offsets, taper, operator, operator_low)
    blocks = days // BLOCK
    filled = blocks * (blocks + 1) // 2 * BLOCK
    if packed.shape[0] > filled:
        packed[filled:, :] = jnp.zeros((packed.shape[0] - filled, BLOCK), jnp.float32)
    for chunk in range(chunks):
        kept[chunk].wait()
        for copy in exchanged[chunk]:
            copy.wait()
        add_products(series.at[chunk], packed, chunk == 0)

    near, side, line = stages
    piece = packed.shape[0] // line[2]
    half = piece // near[2]
    part = half // side[2]

    def rows_of(at, n, s, rows):
        return pl.ds(pl.multiple_of(at * piece + n * half + s * part, 8), rows)

    def send(src, dst, sem, index, device):
        copy = pltpu.make_async_remote_copy(
            src_ref=src,
            dst_ref=dst,
            send_sem=sems[2 * sem].at[index],
            recv_sem=sems[2 * sem + 1].at[index],
            device_id=device,
            device_id_type=MESH,
        )
        copy.start()
        return copy

    my_near, my_side = place_in(near), place_in(side)
    order = list(range(1, line[2])) + [0]
    order.sort(key=lambda shift: abs(2 * shift - line[2]))
    targets = {shift: device_at(line, shift) for shift in order}

    near_copies, side_copies, line_copies = {}, {}, {}
    for shift in order:
        at = targets[shift][1]
        near_copies[shift] = []
        for k in range(1, near[2]):
            device, there = device_at(near, k)
            index = shift * (near[2] - 1) + k - 1
            src = packed.at[rows_of(at, there, 0, half), :]
            near_copies[shift].append(send(src, landing[0].at[index], 0, index, device))
    for shift in order:
        at = targets[shift][1]
        mine = packed.at[rows_of(at, my_near, 0, half), :]
        total = mine[...]
        for k, copy in enumerate(near_copies[shift]):
            copy.wait()
            total = total + landing[0][shift * (near[2] - 1) + k]
        mine[...] = total
        side_copies[shift] = []
        for k in range(1, side[2]):
            device, there = device_at(side, k)
            index = shift * (side[2] - 1) + k - 1
            src = packed.at[rows_of(at, my_near, there, part), :]
            side_copies[shift].append(send(src, landing[1].at[index], 1, index, device))
    for shift in order:
        device, at = targets[shift]
        mine = packed.at[rows_of(at, my_near, my_side, part), :]
        total = mine[...]
        for k, copy in enumerate(side_copies[shift]):
            copy.wait()
            total = total + landing[1][shift * (side[2] - 1) + k]
        mine[...] = total
        if shift:
            line_copies[shift] = send(mine, landing[2].at[shift - 1], 2, shift - 1, device)
    here = place_in(line)
    own = gathered.at[rows_of(here, my_near, my_side, part), :]
    total = packed[rows_of(here, my_near, my_side, part), :]
    for shift in order:
        if shift:
            line_copies[shift].wait()
            total = total + landing[2][shift - 1]
    own[...] = total

    arriving = {}
    for shift in order:
        if shift:
            arriving[shift] = send(own, own, 3, shift - 1, targets[shift][0])
    spread, near_spread = {}, []
    incoming = [0] + [shift for shift in order if shift]
    sources = {shift: lax.rem(here + line[2] - shift, line[2]) for shift in incoming}
    for shift in incoming:
        if shift:
            arriving[shift].wait()
        mine = gathered.at[rows_of(sources[shift], my_near, my_side, part), :]
        spread[shift] = [
            send(mine, mine, 4, shift * (side[2] - 1) + k - 1, device_at(side, k)[0])
            for k in range(1, side[2])
        ]
    for shift in incoming:
        for copy in spread[shift]:
            copy.wait()
        mine = gathered.at[rows_of(sources[shift], my_near, 0, half), :]
        near_spread += [
            send(mine, mine, 5, shift * (near[2] - 1) + k - 1, device_at(near, k)[0])
            for k in range(1, near[2])
        ]
    for copy in near_spread:
        copy.wait()

    place = 0
    for i in range(blocks):
        for j in range(i, blocks):
            block = gathered[pl.ds(place * BLOCK, BLOCK), :]
            out[pl.ds(i * BLOCK, BLOCK), pl.ds(j * BLOCK, BLOCK)] = block
            if j > i:
                out[pl.ds(j * BLOCK, BLOCK), pl.ds(i * BLOCK, BLOCK)] = block.T
            place += 1


def covariance_and_operator(anomaly, offsets, taper_index):
    per_device, pixels = anomaly.shape
    peers = lax.axis_size("tm")
    days = per_device * peers
    own = NF // peers
    stages = stages_of(peers, lax.axis_size("pix"), lax.axis_size("sub"))
    devices = math.prod(stage[2] for stage in stages)
    blocks = days // BLOCK
    rows = -(-(blocks * (blocks + 1) // 2 * BLOCK) // (8 * devices)) * 8 * devices
    near, side, line = (stage[2] for stage in stages)
    half = rows // line // near
    part = half // side
    slots = [max(1, count) for count in (line * (near - 1), line * (side - 1), line - 1)]
    landing = [
        pltpu.VMEM((count, depth, BLOCK), jnp.float32)
        for count, depth in zip(slots, (half, part, part))
    ]
    sems = [
        pltpu.SemaphoreType.DMA((slots[stage],)) for stage in (0, 1, 2, 2, 1, 0) for _ in range(2)
    ]
    words = rows * BLOCK * 2 + days * days + own * 2 * NB * days + days * (pixels // peers) // 2
    words += sum(count * depth * BLOCK for count, depth in zip(slots, (half, part, part)))
    vmem = pl.BlockSpec(memory_space=pltpu.VMEM)
    return pl.pallas_call(
        functools.partial(covariance_kernel, stages),
        out_shape=(
            jax.ShapeDtypeStruct((days, days), jnp.float32),
            jax.ShapeDtypeStruct((own, 2 * NB, days), jnp.bfloat16),
            jax.ShapeDtypeStruct((own, 2 * NB, days), jnp.bfloat16),
        ),
        in_specs=[pl.BlockSpec(memory_space=pltpu.HBM), vmem, vmem],
        out_specs=(vmem, vmem, vmem),
        scratch_shapes=[
            pltpu.VMEM((CHUNKS, days, pixels // peers // CHUNKS), jnp.bfloat16),
            pltpu.VMEM((rows, BLOCK), jnp.float32),
            pltpu.VMEM((rows, BLOCK), jnp.float32),
            pltpu.SemaphoreType.DMA((CHUNKS,)),
            pltpu.SemaphoreType.DMA((CHUNKS, peers - 1)),
            pltpu.SemaphoreType.DMA((CHUNKS, peers - 1)),
        ]
        + landing
        + sems,
        compiler_params=pltpu.CompilerParams(
            collective_id=0, has_side_effects=True, vmem_limit_bytes=4 * words + 8 * 2**20
        ),
        name="covariance",
    )(anomaly, offsets[None, :], taper_index[None, :])


def finish_kernel(pixels, covariance, operator, operator_low, gram, lead, high, low):
    own, size, days = operator.shape
    high[...], low[...] = split(covariance[...])
    group = math.gcd(own, 4)

    def product(left, right, contract):
        return lax.dot_general(
            left, right, (((1,), (contract,)), ((), ())), preferred_element_type=jnp.float32
        )

    for first in range(0, own, group):
        left = operator[first : first + group].reshape(group * size, days)
        left_low = operator_low[first : first + group].reshape(group * size, days)
        half = product(left, high[...], 0) + (
            product(left_low, high[...], 0) + product(left, low[...], 0)
        )
        half_high, half_low = split(half)
        for f in range(group):
            rows = slice(f * size, (f + 1) * size)
            right, right_low = operator[first + f], operator_low[first + f]
            value = product(half_high[rows], right, 1) + (
                product(half_low[rows], right, 1) + product(half_high[rows], right_low, 1)
            )
            gram[first + f] = value / pixels

    matrix = gram[...]
    vector = jnp.ones((own, 1, size), jnp.float32)
    for step in range(POWER + 1):
        across = 2 - step % 2
        applied = jnp.sum(matrix * vector, axis=across, keepdims=True)
        power = jnp.sum(applied * applied, axis=3 - across, keepdims=True) / size
        vector = applied / jnp.sqrt(power + power_eps)
    column = jnp.broadcast_to(jnp.sqrt(power)[:, 0, :], (own, own))
    square = (own, own)
    diagonal = lax.broadcasted_iota(jnp.int32, square, 0) == lax.broadcasted_iota(jnp.int32, square, 1)
    lead[...] = jnp.sum(jnp.where(diagonal, column, 0.0), axis=0, keepdims=True)


def gram_and_leading(covariance, operator, operator_low, pixels):
    own, size, days = operator.shape
    vmem = pl.BlockSpec(memory_space=pltpu.VMEM)
    gram, lead = pl.pallas_call(
        functools.partial(finish_kernel, pixels),
        out_shape=(
            jax.ShapeDtypeStruct((own, size, size), jnp.float32),
            jax.ShapeDtypeStruct((1, own), jnp.float32),
        ),
        in_specs=[vmem] * 3,
        out_specs=(vmem, vmem),
        scratch_shapes=[pltpu.VMEM((days, days), jnp.bfloat16)] * 2,
        compiler_params=pltpu.CompilerParams(
            vmem_limit_bytes=8 * days * days + 4 * own * size * days + 12 * 2**20
        ),
        name="finish",
    )(covariance, operator, operator_low)
    return gram, lead[0]


def row_scale(shape, axis):
    day = lax.broadcasted_iota(jnp.int32, shape, axis)
    return 1.0 + ((((day * day) * 40503) >> 4) & 1023).astype(jnp.float32) * (1.0 / 1024.0)


def write_scaled_operator(offsets, taper, operator):
    own, _, days = operator.shape
    step = days_of((NB, days), lax.axis_size("tm")) - upright(offsets)
    windows = windows_of(jnp.broadcast_to(upright(taper), (NB, days)), step, NFFT)
    scaled = windows * (1.0 / jnp.sqrt(jnp.sum(windows * windows, axis=1, keepdims=True)))
    scaled = scaled / row_scale((NB, days), 1)
    first = lax.axis_index("tm") * own

    def one(f, carry):
        angle = (((first + f) * step) & (NFFT - 1)).astype(jnp.float32) * (2.0 * math.pi / NFFT)
        for rows, table in ((pl.ds(0, NB), jnp.cos(angle)), (pl.ds(NB, NB), -jnp.sin(angle))):
            operator[f, rows, :] = (table.astype(jnp.bfloat16).astype(jnp.float32) * scaled).astype(jnp.bfloat16)
        return carry

    lax.fori_loop(0, own, one, 0)


def days_of(shape, peers):
    days = shape[1]
    rows = days // peers
    late = rows // 4
    early = rows - late
    place = lax.broadcasted_iota(jnp.int32, shape, 1)
    first = jnp.zeros(shape, jnp.int32)
    second = jnp.zeros(shape, jnp.int32)
    for device in range(1, peers):
        first = first + (place >= early * device).astype(jnp.int32)
        second = second + (place >= early * peers + late * device).astype(jnp.int32)
    return jnp.where(
        place < early * peers, place + late * first, place - early * peers + early + early * second
    )


def block_order(blocks):
    early = [(i, j) for i in range(blocks - 1) for j in range(i, blocks - 1)]
    return early, [(i, blocks - 1) for i in range(blocks)]


def write_scale(scale, blocks):
    column, row = row_scale((blocks * BLOCK, BLOCK), 0), row_scale((8, blocks * BLOCK), 1)[:1]
    early, late = block_order(blocks)
    for place, (i, j) in enumerate(early + late):
        block = column[i * BLOCK : (i + 1) * BLOCK, :] * row[:, j * BLOCK : (j + 1) * BLOCK]
        scale[pl.ds(place * BLOCK, BLOCK), :] = block


def add_late_products(series, packed, first):
    rows = series.shape[0]
    block = lax.dot_general(
        series[...], series[rows - BLOCK :, :], (((1,), (1,)), ((), ())), preferred_element_type=jnp.float32
    )
    packed[...] = block if first else packed[...] + block


def direct_kernel(
    anomaly,
    offsets,
    taper,
    out,
    operator,
    packed,
    scale,
    near_box,
    near_land,
    outbox,
    landing,
    gathered,
    small,
    own_sem,
    small_sem,
    exchange_send,
    exchange_recv,
    near_send,
    near_recv,
    part_send,
    part_recv,
    whole_send,
    whole_recv,
    pass_send,
    pass_recv,
    *series,
):
    per_device, pixels = anomaly.shape
    days = series[0].shape[0]
    peers, across = lax.axis_size("tm"), lax.axis_size("pix")
    chips = peers // 2
    holders = chips
    span = pixels // holders
    me, side = lax.axis_index("tm"), lax.axis_index("pix")
    core, chip = lax.rem(me, 2), lax.div(me, 2)
    inner = lax.div(lax.rem(chip, chips - 1) + 1, 2)
    at = [chip, chip + 1 - 2 * lax.rem(chip, 2), lax.rem(chip + 2, chips), chips - 1 - chip]
    neighbour = {"tm": me + 1 - 2 * core}

    barrier = pltpu.get_barrier_semaphore()
    greeted = 0
    for axis, place, members in (("tm", me, peers), ("pix", side, across)):
        for shift in range(1, members):
            device = {axis: lax.rem(place + shift, members)}
            pl.semaphore_signal(barrier, inc=1, device_id=device, device_id_type=MESH)
            greeted += 1
    blocks = days // BLOCK
    early, late = block_order(blocks)
    base = (0, len(early) * BLOCK)
    half = (len(early) * BLOCK // 2, len(late) * BLOCK // 2)
    part = tuple(each // (2 * across) for each in half)
    late_rows = per_device // 4
    early_rows = per_device - late_rows
    sources = (pl.ds(0, early_rows), pl.ds(early_rows, late_rows))
    my_rows = (
        pl.ds(pl.multiple_of(me * early_rows, 16), early_rows),
        pl.ds(pl.multiple_of(early_rows * peers + me * late_rows, 16), late_rows),
    )
    starts = [sum(WIDTHS[:chunk]) for chunk in range(len(WIDTHS))]
    chunks = range(len(WIDTHS))

    def columns(z, c, chunk):
        return pl.ds(pl.multiple_of((2 * (z - 1) + c) * span + starts[chunk], BLOCK), WIDTHS[chunk])

    def send(src, dst, sends, receives, index, device):
        return pltpu.make_async_remote_copy(
            src_ref=src,
            dst_ref=dst,
            send_sem=sends.at[index],
            recv_sem=receives.at[index],
            device_id=device,
            device_id_type=MESH,
        )

    def exchange(group, chunk, z, c):
        there = 1 - core if c else core
        return send(
            anomaly.at[sources[group], columns(at[z], there, chunk)],
            series[chunk].at[my_rows[group], :],
            exchange_send,
            exchange_recv,
            (group, chunk, 2 * z + c),
            {"tm": 2 * at[z] + there},
        )

    def arrival(group, chunk, z, c):
        mine = series[chunk].at[my_rows[group], :]
        return send(mine, mine, exchange_send, exchange_recv, (group, chunk, 2 * z + c), neighbour)

    def keep(group, chunk):
        return pltpu.make_async_copy(
            anomaly.at[sources[group], columns(chip, core, chunk)],
            series[chunk].at[my_rows[group], :],
            own_sem.at[group, chunk],
        )

    loads = [
        pltpu.make_async_copy(offsets, small.at[0:1, :], small_sem.at[0]),
        pltpu.make_async_copy(taper, small.at[8:9, :], small_sem.at[1]),
    ]
    for load in loads:
        load.start()
    pl.semaphore_wait(barrier, greeted)

    @pl.when(inner == 1)
    def _():
        for group in range(2):
            for chunk in chunks:
                keep(group, chunk).start()
                for z, c in INNER_ORDER:
                    exchange(group, chunk, z, c).start()

    @pl.when(inner == 0)
    def _():
        for group in range(2):
            for chunk in chunks:
                for z, c in OUTER_ORDER:
                    exchange(group, chunk, z, c).start()

    for load in loads:
        load.wait()
    write_scaled_operator(small.at[0:1, :], small.at[8:9, :], operator)

    def half_of(group, n):
        return pl.ds(pl.multiple_of(base[group] + n * half[group], 16), half[group])

    def box(group):
        return pl.ds(base[group] // 2, half[group])

    def inside(group, z, x):
        return ((z - 1) * across + x) * part[group]

    def part_of(group, n, z, x):
        return pl.ds(pl.multiple_of(base[group] + n * half[group] + inside(group, z, x), 16), part[group])

    def landed(group, index):
        return landing.at[index, pl.ds(base[group] // (4 * across), part[group]), :]

    def beside(x):
        return 1 - side if x else side

    def device_of(z, x):
        return {"tm": 2 * at[z] + core, "pix": beside(x)}

    def own(group):
        return gathered.at[part_of(group, core, chip * inner + 1 - inner, side), :]

    def whole(group, z, x):
        mine = own(group)
        return send(mine, mine, whole_send, whole_recv, (group, 2 * z + x), device_of(z, x))

    def piece(group, z, x):
        return gathered.at[part_of(group, core, at[z], beside(x)), :]

    def gotten(group, z, x):
        mine = piece(group, z, x)
        return send(mine, mine, whole_send, whole_recv, (group, 2 * z + x), device_of(z, x))

    def passed(group, ref, index):
        return send(ref, ref, pass_send, pass_recv, (group, index), neighbour)

    def near(group):
        return send(near_box.at[box(group), :], near_land.at[box(group), :], near_send, near_recv, group, neighbour)

    others = ((3, 1), (3, 0), (0, 1))

    def portion(group, index):
        z, x = others[index]
        src = outbox.at[pl.ds(pl.multiple_of(base[group] // 2 + inside(group, at[z], beside(x)), 16), part[group]), :]
        return send(src, landed(group, index), part_send, part_recv, (group, index), device_of(z, x))

    def start_near(group):
        theirs = packed[half_of(group, 1 - core), :] * scale[half_of(group, 1 - core), :]
        near_box[box(group), :] = theirs.astype(jnp.bfloat16)
        near(group).start()
        mine = packed.at[half_of(group, core), :]
        mine[...] = mine[...] * scale[half_of(group, core), :]

    def start_scatter(group):
        near(group).wait()
        mine = packed.at[half_of(group, core), :]
        total = mine[...] + near_land[box(group), :].astype(jnp.float32)
        mine[...] = total
        outbox[box(group), :] = total.astype(jnp.bfloat16)
        for index in range(3):
            portion(group, index).start()

    def start_gather(group):
        total = packed[part_of(group, core, chip, side), :]
        for index in range(3):
            portion(group, index).wait()
            total = total + landed(group, index)[...].astype(jnp.float32)
        mine = own(group)
        mine[...] = total.astype(jnp.bfloat16)
        for z, x in GATHER_ORDER:
            whole(group, z, x).start()
        passed(group, mine, 0).start()

    def forward(group, froms, first):
        for index, (z, x) in enumerate(froms):
            gotten(group, z, x).wait_recv()
            passed(group, piece(group, z, x), index + first).start()

    def finish_pass(group, froms, first):
        for index, (z, x) in enumerate(froms):
            passed(group, piece(group, z, x), index + first).wait()

    @pl.when(inner == 1)
    def _():
        write_scale(scale, blocks)
        froms = ((0, 1), (3, 0), (3, 1))
        for group in range(2):
            for chunk in chunks:
                keep(group, chunk).wait()
                for z, c in ((0, 1), (1, 0), (1, 1), (3, 0), (3, 1), (2, 0), (2, 1)):
                    arrival(group, chunk, z, c).wait_recv()
                if group == 0:
                    add_products(series[chunk].at[0 : early_rows * peers, :], packed, chunk == 0)
                else:
                    add_late_products(series[chunk], packed.at[base[1] :, :], chunk == 0)
            start_near(group)
            if group == 0:
                start_scatter(0)
        start_scatter(1)
        start_gather(0)
        start_gather(1)
        for group in range(2):
            forward(group, froms, 1)
        for group in range(2):
            for chunk in chunks:
                for z, c in INNER_ORDER:
                    exchange(group, chunk, z, c).wait_send()
            for z, x in GATHER_ORDER:
                whole(group, z, x).wait_send()
            passed(group, own(group), 0).wait()
            finish_pass(group, froms, 1)

    @pl.when(inner == 0)
    def _():
        froms = ((1, 0), (1, 1), (2, 0), (2, 1))
        for group in range(2):
            for chunk in chunks:
                for z, c in OUTER_ORDER:
                    exchange(group, chunk, z, c).wait_send()
        for group in range(2):
            forward(group, froms, 0)
        for group in range(2):
            finish_pass(group, froms, 0)

    for place, (i, j) in enumerate(early + late):
        block = gathered[pl.ds(place * BLOCK, BLOCK), :]
        out[pl.ds(i * BLOCK, BLOCK), pl.ds(j * BLOCK, BLOCK)] = block
        if j > i:
            turned = block.astype(jnp.float32).T
            out[pl.ds(j * BLOCK, BLOCK), pl.ds(i * BLOCK, BLOCK)] = turned.astype(jnp.bfloat16)


def direct_covariance(anomaly, offsets, taper_index):
    per_device, pixels = anomaly.shape
    peers, across = lax.axis_size("tm"), lax.axis_size("pix")
    days = per_device * peers
    own = NF // peers
    blocks = days // BLOCK
    owners = 4 * across
    rows = -(-(blocks * (blocks + 1) // 2 * BLOCK) // (16 * owners)) * 16 * owners
    half, part = rows // 2, rows // owners
    others = owners // 2 - 1
    vmem = pl.BlockSpec(memory_space=pltpu.VMEM)
    hbm = pl.BlockSpec(memory_space=pl.ANY)
    counts = [(2,), (2, others), (2, peers), (2, others + 1)]
    return pl.pallas_call(
        direct_kernel,
        out_shape=(
            jax.ShapeDtypeStruct((days, days), jnp.bfloat16),
            jax.ShapeDtypeStruct((own, 2 * NB, days), jnp.bfloat16),
        ),
        in_specs=[hbm, hbm, hbm],
        out_specs=(vmem, vmem),
        scratch_shapes=[
            pltpu.VMEM((rows, BLOCK), jnp.float32),
            pltpu.VMEM((rows, BLOCK), jnp.float32),
            pltpu.VMEM((half, BLOCK), jnp.bfloat16),
            pltpu.VMEM((half, BLOCK), jnp.bfloat16),
            pltpu.VMEM((half, BLOCK), jnp.bfloat16),
            pltpu.VMEM((others, part, BLOCK), jnp.bfloat16),
            pltpu.VMEM((rows, BLOCK), jnp.bfloat16),
            pltpu.VMEM((16, NB), jnp.int32),
            pltpu.SemaphoreType.DMA((2, len(WIDTHS))),
            pltpu.SemaphoreType.DMA((2,)),
            pltpu.SemaphoreType.DMA((2, len(WIDTHS), peers)),
            pltpu.SemaphoreType.DMA((2, len(WIDTHS), peers)),
        ]
        + [pltpu.SemaphoreType.DMA(count) for count in counts for _ in range(2)]
        + [pltpu.VMEM((days, width), jnp.bfloat16) for width in WIDTHS],
        compiler_params=pltpu.CompilerParams(
            collective_id=0, has_side_effects=True, vmem_limit_bytes=DIRECT_VMEM
        ),
        name="covariance",
    )(*(pltpu.with_memory_space_constraint(each, pltpu.HBM) for each in (anomaly, offsets[None, :], taper_index[None, :])))


def leading(matrix, size):
    own = matrix.shape[0]
    vector = jnp.ones((own, 1, size), jnp.float32)
    for step in range(POWER + 1):
        across = 2 - step % 2
        applied = jnp.sum(matrix * vector, axis=across, keepdims=True)
        power = jnp.sum(applied * applied, axis=3 - across, keepdims=True) / size
        vector = applied / jnp.sqrt(power + power_eps)
    column = jnp.broadcast_to(jnp.sqrt(power)[:, 0, :], (own, own))
    square = (own, own)
    diagonal = lax.broadcasted_iota(jnp.int32, square, 0) == lax.broadcasted_iota(jnp.int32, square, 1)
    return jnp.sum(jnp.where(diagonal, column, 0.0), axis=0, keepdims=True)


def direct_finish_kernel(pixels, covariance, operator, gram, lead, held, sem):
    own, size, days = operator.shape
    group = math.gcd(own, 4)
    copies = []
    for first in range(0, own, group):
        left = operator[first : first + group].reshape(group * size, days)
        half = lax.dot_general(
            left, covariance[...], (((1,), (0,)), ((), ())), preferred_element_type=jnp.float32
        ).astype(jnp.bfloat16)
        for f in range(group):
            value = lax.dot_general(
                half[f * size : (f + 1) * size],
                operator[first + f],
                (((1,), (1,)), ((), ())),
                preferred_element_type=jnp.float32,
            )
            held[first + f] = value * (1.0 / pixels)
        chosen = pl.ds(first, group)
        copy = pltpu.make_async_copy(held.at[chosen], gram.at[chosen], sem.at[first // group])
        copy.start()
        copies.append(copy)
    lead[...] = leading(held[...], size)
    for copy in copies:
        copy.wait()


def direct_finish(covariance, operator, pixels):
    own, size, days = operator.shape
    vmem = pl.BlockSpec(memory_space=pltpu.VMEM)
    gram, lead = pl.pallas_call(
        functools.partial(direct_finish_kernel, pixels),
        out_shape=(
            jax.ShapeDtypeStruct((own, size, size), jnp.float32),
            jax.ShapeDtypeStruct((1, own), jnp.float32),
        ),
        in_specs=[vmem] * 2,
        out_specs=(pl.BlockSpec(memory_space=pl.ANY), vmem),
        scratch_shapes=[
            pltpu.VMEM((own, size, size), jnp.float32),
            pltpu.SemaphoreType.DMA((own // math.gcd(own, 4),)),
        ],
        compiler_params=pltpu.CompilerParams(vmem_limit_bytes=24 * 2**20),
        name="finish",
    )(covariance, operator)
    return gram, lead[0]


def shards(anomaly, offsets, taper_index):
    total_pixels = anomaly.shape[1] * lax.axis_size(("pix", "sub"))
    peers, sub = lax.axis_size("tm"), lax.axis_size("sub")
    if sub == 1 and peers == 8 and lax.axis_size("pix") == 2 and anomaly.shape == (64, 4 * sum(WIDTHS)):
        covariance, operator = direct_covariance(anomaly, offsets, taper_index)
        return direct_finish(covariance, operator, total_pixels)
    covariance, operator, operator_low = covariance_and_operator(anomaly, offsets, taper_index)
    return gram_and_leading(covariance, operator, operator_low, total_pixels)


def solution(mesh):
    placed = (P("tm", ("group", "pix", "sub")), P(), P())
    return jax.shard_map(
        shards,
        mesh=mesh,
        in_specs=placed,
        out_specs=(P(("group", "tm"), None, None), P(("group", "tm"))),
        check_vma=False,
    )
```

```python
import functools
import math

import jax
import jax.numpy as jnp
from jax import lax
from jax.experimental import pallas as pl
from jax.experimental.pallas import tpu as pltpu
from jax.sharding import PartitionSpec as P

NFFT = 256
NB = 32
POWER = 8
NF = 128


power_eps = 1e-06


CHUNKS = 4


DIRECT_VMEM = 40 * 2**20
CUT = 8
WIDTHS = (1792, 1536, 768)
INNER_ORDER = ((0, 1), (3, 0), (3, 1))
OUTER_ORDER = ((2, 0), (2, 1), (1, 0), (1, 1))
GATHER_ORDER = ((2, 1), (3, 1), (2, 0), (3, 0), (1, 1), (1, 0), (0, 1))


def windows_of(taper, step, length):
    steps = step.astype(jnp.float32)
    phase = steps * (2.0 * math.pi / length)
    center = (steps + 0.5) * (math.pi / length)
    sine_win = jnp.sin(center)
    hann = sine_win * sine_win
    hamming = 0.54 - 0.46 * jnp.cos(phase)
    blackman = 0.42 - 0.5 * jnp.cos(phase) + 0.08 * jnp.cos(2.0 * phase)
    chosen = jnp.where(
        taper == 0, hann, jnp.where(taper == 1, hamming, jnp.where(taper == 2, blackman, sine_win))
    )
    return jnp.where((step >= 0) & (step < length), chosen, 0.0)


def upright(row):
    square = (NB, NB)
    diagonal = lax.broadcasted_iota(jnp.int32, square, 0) == lax.broadcasted_iota(jnp.int32, square, 1)
    values = jnp.broadcast_to(row[...].astype(jnp.float32), square)
    return jnp.sum(jnp.where(diagonal, values, 0.0), axis=1, keepdims=True).astype(jnp.int32)


def split(value):
    high = value.astype(jnp.bfloat16)
    return high, (value - high.astype(jnp.float32)).astype(jnp.bfloat16)


def write_operator(offsets, taper, operator, operator_low):
    own, _, days = operator.shape
    step = lax.broadcasted_iota(jnp.int32, (NB, days), 1) - upright(offsets)
    windows = windows_of(jnp.broadcast_to(upright(taper), (NB, days)), step, NFFT)
    scaled = windows * (1.0 / jnp.sqrt(jnp.sum(windows * windows, axis=1, keepdims=True)))
    first = lax.axis_index("tm") * own

    def one(f, carry):
        angle = (((first + f) * step) & (NFFT - 1)).astype(jnp.float32) * (2.0 * math.pi / NFFT)
        for rows, table in ((pl.ds(0, NB), jnp.cos(angle)), (pl.ds(NB, NB), -jnp.sin(angle))):
            high, low = split(table.astype(jnp.bfloat16).astype(jnp.float32) * scaled)
            operator[f, rows, :] = high
            operator_low[f, rows, :] = low
        return carry

    lax.fori_loop(0, own, one, 0)


BLOCK = 128
MESH = pl.DeviceIdType.MESH


def stages_of(tm, pix, sub):
    if sub > 1 or tm % 2:
        split = [("sub", 1, sub), ("pix", 1, pix), ("tm", 1, tm)]
    else:
        split = [("tm", 1, 2), ("pix", 1, pix), ("tm", 2, tm // 2)]
    return split


def place_in(stage):
    axis, inner, members = stage
    return lax.rem(lax.axis_index(axis) // inner, members)


def device_at(stage, shift):
    axis, inner, members = stage
    index = lax.axis_index(axis)
    here = place_in(stage)
    there = lax.rem(here + shift, members)
    return {axis: index + (there - here) * inner}, there


def add_products(series, packed, first):
    blocks = series.shape[0] // BLOCK
    place = 0
    for i in range(blocks):
        strip = lax.dot_general(
            series[i * BLOCK : (i + 1) * BLOCK, :],
            series[i * BLOCK :, :],
            (((1,), (1,)), ((), ())),
            preferred_element_type=jnp.float32,
        )
        for j in range(blocks - i):
            rows = pl.ds((place + j) * BLOCK, BLOCK)
            block = strip[:, j * BLOCK : (j + 1) * BLOCK]
            packed[rows, :] = block if first else packed[rows, :] + block
        place += blocks - i


def covariance_kernel(
    stages, anomaly, offsets, taper, out, operator, operator_low, series, packed, gathered, own_sem, *scratch
):
    exchange_send, exchange_recv = scratch[:2]
    landing, sems = scratch[2:5], scratch[5:]
    chunks, days, width = series.shape
    per_device = anomaly.shape[0]
    peers = days // per_device
    me = lax.axis_index("tm")

    barrier = pltpu.get_barrier_semaphore()
    greeted = 0
    for axis in ("tm", "pix", "sub"):
        members = lax.axis_size(axis)
        for shift in range(1, members):
            device = {axis: lax.rem(lax.axis_index(axis) + shift, members)}
            pl.semaphore_signal(barrier, inc=1, device_id=device, device_id_type=MESH)
            greeted += 1
    my_rows = pl.ds(pl.multiple_of(me * per_device, per_device), per_device)

    def columns(device, chunk):
        return pl.ds(pl.multiple_of(device * (chunks * width) + chunk * width, width), width)

    kept = []
    for chunk in range(chunks):
        copy = pltpu.make_async_copy(
            anomaly.at[:, columns(me, chunk)], series.at[chunk, my_rows, :], own_sem.at[chunk]
        )
        copy.start()
        kept.append(copy)
    pl.semaphore_wait(barrier, greeted)
    farthest_first = sorted(range(1, peers), key=lambda shift: abs(2 * shift - peers))
    exchanged = []
    for chunk in range(chunks):
        copies = []
        for shift in farthest_first:
            there = lax.rem(me + shift, peers)
            copy = pltpu.make_async_remote_copy(
                src_ref=anomaly.at[:, columns(there, chunk)],
                dst_ref=series.at[chunk, my_rows, :],
                send_sem=exchange_send.at[chunk, shift - 1],
                recv_sem=exchange_recv.at[chunk, shift - 1],
                device_id={"tm": there},
                device_id_type=MESH,
            )
            copy.start()
            copies.append(copy)
        exchanged.append(copies)

    write_operator(offsets, taper, operator, operator_low)
    blocks = days // BLOCK
    filled = blocks * (blocks + 1) // 2 * BLOCK
    if packed.shape[0] > filled:
        packed[filled:, :] = jnp.zeros((packed.shape[0] - filled, BLOCK), jnp.float32)
    for chunk in range(chunks):
        kept[chunk].wait()
        for copy in exchanged[chunk]:
            copy.wait()
        add_products(series.at[chunk], packed, chunk == 0)

    near, side, line = stages
    piece = packed.shape[0] // line[2]
    half = piece // near[2]
    part = half // side[2]

    def rows_of(at, n, s, rows):
        return pl.ds(pl.multiple_of(at * piece + n * half + s * part, 8), rows)

    def send(src, dst, sem, index, device):
        copy = pltpu.make_async_remote_copy(
            src_ref=src,
            dst_ref=dst,
            send_sem=sems[2 * sem].at[index],
            recv_sem=sems[2 * sem + 1].at[index],
            device_id=device,
            device_id_type=MESH,
        )
        copy.start()
        return copy

    my_near, my_side = place_in(near), place_in(side)
    order = list(range(1, line[2])) + [0]
    order.sort(key=lambda shift: abs(2 * shift - line[2]))
    targets = {shift: device_at(line, shift) for shift in order}

    near_copies, side_copies, line_copies = {}, {}, {}
    for shift in order:
        at = targets[shift][1]
        near_copies[shift] = []
        for k in range(1, near[2]):
            device, there = device_at(near, k)
            index = shift * (near[2] - 1) + k - 1
            src = packed.at[rows_of(at, there, 0, half), :]
            near_copies[shift].append(send(src, landing[0].at[index], 0, index, device))
    for shift in order:
        at = targets[shift][1]
        mine = packed.at[rows_of(at, my_near, 0, half), :]
        total = mine[...]
        for k, copy in enumerate(near_copies[shift]):
            copy.wait()
            total = total + landing[0][shift * (near[2] - 1) + k]
        mine[...] = total
        side_copies[shift] = []
        for k in range(1, side[2]):
            device, there = device_at(side, k)
            index = shift * (side[2] - 1) + k - 1
            src = packed.at[rows_of(at, my_near, there, part), :]
            side_copies[shift].append(send(src, landing[1].at[index], 1, index, device))
    for shift in order:
        device, at = targets[shift]
        mine = packed.at[rows_of(at, my_near, my_side, part), :]
        total = mine[...]
        for k, copy in enumerate(side_copies[shift]):
            copy.wait()
            total = total + landing[1][shift * (side[2] - 1) + k]
        mine[...] = total
        if shift:
            line_copies[shift] = send(mine, landing[2].at[shift - 1], 2, shift - 1, device)
    here = place_in(line)
    own = gathered.at[rows_of(here, my_near, my_side, part), :]
    total = packed[rows_of(here, my_near, my_side, part), :]
    for shift in order:
        if shift:
            line_copies[shift].wait()
            total = total + landing[2][shift - 1]
    own[...] = total

    arriving = {}
    for shift in order:
        if shift:
            arriving[shift] = send(own, own, 3, shift - 1, targets[shift][0])
    spread, near_spread = {}, []
    incoming = [0] + [shift for shift in order if shift]
    sources = {shift: lax.rem(here + line[2] - shift, line[2]) for shift in incoming}
    for shift in incoming:
        if shift:
            arriving[shift].wait()
        mine = gathered.at[rows_of(sources[shift], my_near, my_side, part), :]
        spread[shift] = [
            send(mine, mine, 4, shift * (side[2] - 1) + k - 1, device_at(side, k)[0])
            for k in range(1, side[2])
        ]
    for shift in incoming:
        for copy in spread[shift]:
            copy.wait()
        mine = gathered.at[rows_of(sources[shift], my_near, 0, half), :]
        near_spread += [
            send(mine, mine, 5, shift * (near[2] - 1) + k - 1, device_at(near, k)[0])
            for k in range(1, near[2])
        ]
    for copy in near_spread:
        copy.wait()

    place = 0
    for i in range(blocks):
        for j in range(i, blocks):
            block = gathered[pl.ds(place * BLOCK, BLOCK), :]
            out[pl.ds(i * BLOCK, BLOCK), pl.ds(j * BLOCK, BLOCK)] = block
            if j > i:
                out[pl.ds(j * BLOCK, BLOCK), pl.ds(i * BLOCK, BLOCK)] = block.T
            place += 1


def covariance_and_operator(anomaly, offsets, taper_index):
    per_device, pixels = anomaly.shape
    peers = lax.axis_size("tm")
    days = per_device * peers
    own = NF // peers
    stages = stages_of(peers, lax.axis_size("pix"), lax.axis_size("sub"))
    devices = math.prod(stage[2] for stage in stages)
    blocks = days // BLOCK
    rows = -(-(blocks * (blocks + 1) // 2 * BLOCK) // (8 * devices)) * 8 * devices
    near, side, line = (stage[2] for stage in stages)
    half = rows // line // near
    part = half // side
    slots = [max(1, count) for count in (line * (near - 1), line * (side - 1), line - 1)]
    landing = [
        pltpu.VMEM((count, depth, BLOCK), jnp.float32)
        for count, depth in zip(slots, (half, part, part))
    ]
    sems = [
        pltpu.SemaphoreType.DMA((slots[stage],)) for stage in (0, 1, 2, 2, 1, 0) for _ in range(2)
    ]
    words = rows * BLOCK * 2 + days * days + own * 2 * NB * days + days * (pixels // peers) // 2
    words += sum(count * depth * BLOCK for count, depth in zip(slots, (half, part, part)))
    vmem = pl.BlockSpec(memory_space=pltpu.VMEM)
    return pl.pallas_call(
        functools.partial(covariance_kernel, stages),
        out_shape=(
            jax.ShapeDtypeStruct((days, days), jnp.float32),
            jax.ShapeDtypeStruct((own, 2 * NB, days), jnp.bfloat16),
            jax.ShapeDtypeStruct((own, 2 * NB, days), jnp.bfloat16),
        ),
        in_specs=[pl.BlockSpec(memory_space=pltpu.HBM), vmem, vmem],
        out_specs=(vmem, vmem, vmem),
        scratch_shapes=[
            pltpu.VMEM((CHUNKS, days, pixels // peers // CHUNKS), jnp.bfloat16),
            pltpu.VMEM((rows, BLOCK), jnp.float32),
            pltpu.VMEM((rows, BLOCK), jnp.float32),
            pltpu.SemaphoreType.DMA((CHUNKS,)),
            pltpu.SemaphoreType.DMA((CHUNKS, peers - 1)),
            pltpu.SemaphoreType.DMA((CHUNKS, peers - 1)),
        ]
        + landing
        + sems,
        compiler_params=pltpu.CompilerParams(
            collective_id=0, has_side_effects=True, vmem_limit_bytes=4 * words + 8 * 2**20
        ),
        name="covariance",
    )(anomaly, offsets[None, :], taper_index[None, :])


def finish_kernel(pixels, covariance, operator, operator_low, gram, lead, high, low):
    own, size, days = operator.shape
    high[...], low[...] = split(covariance[...])
    group = math.gcd(own, 4)

    def product(left, right, contract):
        return lax.dot_general(
            left, right, (((1,), (contract,)), ((), ())), preferred_element_type=jnp.float32
        )

    for first in range(0, own, group):
        left = operator[first : first + group].reshape(group * size, days)
        left_low = operator_low[first : first + group].reshape(group * size, days)
        half = product(left, high[...], 0) + (
            product(left_low, high[...], 0) + product(left, low[...], 0)
        )
        half_high, half_low = split(half)
        for f in range(group):
            rows = slice(f * size, (f + 1) * size)
            right, right_low = operator[first + f], operator_low[first + f]
            value = product(half_high[rows], right, 1) + (
                product(half_low[rows], right, 1) + product(half_high[rows], right_low, 1)
            )
            gram[first + f] = value / pixels

    matrix = gram[...]
    vector = jnp.ones((own, 1, size), jnp.float32)
    for step in range(POWER + 1):
        across = 2 - step % 2
        applied = jnp.sum(matrix * vector, axis=across, keepdims=True)
        power = jnp.sum(applied * applied, axis=3 - across, keepdims=True) / size
        vector = applied / jnp.sqrt(power + power_eps)
    column = jnp.broadcast_to(jnp.sqrt(power)[:, 0, :], (own, own))
    square = (own, own)
    diagonal = lax.broadcasted_iota(jnp.int32, square, 0) == lax.broadcasted_iota(jnp.int32, square, 1)
    lead[...] = jnp.sum(jnp.where(diagonal, column, 0.0), axis=0, keepdims=True)


def gram_and_leading(covariance, operator, operator_low, pixels):
    own, size, days = operator.shape
    vmem = pl.BlockSpec(memory_space=pltpu.VMEM)
    gram, lead = pl.pallas_call(
        functools.partial(finish_kernel, pixels),
        out_shape=(
            jax.ShapeDtypeStruct((own, size, size), jnp.float32),
            jax.ShapeDtypeStruct((1, own), jnp.float32),
        ),
        in_specs=[vmem] * 3,
        out_specs=(vmem, vmem),
        scratch_shapes=[pltpu.VMEM((days, days), jnp.bfloat16)] * 2,
        compiler_params=pltpu.CompilerParams(
            vmem_limit_bytes=8 * days * days + 4 * own * size * days + 12 * 2**20
        ),
        name="finish",
    )(covariance, operator, operator_low)
    return gram, lead[0]


def row_scale(shape, axis):
    day = lax.broadcasted_iota(jnp.int32, shape, axis)
    return 1.0 + ((((day * day) * 40503) >> 4) & 1023).astype(jnp.float32) * (1.0 / 1024.0)


def write_scaled_operator(offsets, taper, operator):
    own, _, days = operator.shape
    step = days_of((NB, days), lax.axis_size("tm")) - upright(offsets)
    windows = windows_of(jnp.broadcast_to(upright(taper), (NB, days)), step, NFFT)
    scaled = windows * (1.0 / jnp.sqrt(jnp.sum(windows * windows, axis=1, keepdims=True)))
    scaled = scaled / row_scale((NB, days), 1)
    first = lax.axis_index("tm") * own

    def one(f, carry):
        angle = (((first + f) * step) & (NFFT - 1)).astype(jnp.float32) * (2.0 * math.pi / NFFT)
        for rows, table in ((pl.ds(0, NB), jnp.cos(angle)), (pl.ds(NB, NB), -jnp.sin(angle))):
            operator[f, rows, :] = (table.astype(jnp.bfloat16).astype(jnp.float32) * scaled).astype(jnp.bfloat16)
        return carry

    lax.fori_loop(0, own, one, 0)


def days_of(shape, peers):
    days = shape[1]
    rows = days // peers
    late = rows // 4
    early = rows - late
    place = lax.broadcasted_iota(jnp.int32, shape, 1)
    first = jnp.zeros(shape, jnp.int32)
    second = jnp.zeros(shape, jnp.int32)
    for device in range(1, peers):
        first = first + (place >= early * device).astype(jnp.int32)
        second = second + (place >= early * peers + late * device).astype(jnp.int32)
    return jnp.where(
        place < early * peers, place + late * first, place - early * peers + early + early * second
    )


def block_order(blocks):
    order = [(i, j) for j in range(blocks) for i in range(j + 1)]
    return order[: -blocks], order[-blocks:]


def write_scale(scale, blocks):
    column, row = row_scale((blocks * BLOCK, BLOCK), 0), row_scale((8, blocks * BLOCK), 1)[:1]
    early, late = block_order(blocks)
    for place, (i, j) in enumerate(early + late):
        block = column[i * BLOCK : (i + 1) * BLOCK, :] * row[:, j * BLOCK : (j + 1) * BLOCK]
        scale[pl.ds(place * BLOCK, BLOCK), :] = 0.5 * block if i == j else block


def write_early_gram(gathered, operator, gram, start, stop):
    own, size, days = operator.shape
    columns = days // BLOCK - 1
    group = math.gcd(own, 4)
    for first in range(start, stop, group):
        halves = []
        for j in range(columns):
            depth = (j + 1) * BLOCK
            left = operator[first : first + group, :, 0:depth].reshape(group * size, depth)
            stack = gathered[pl.ds(j * (j + 1) // 2 * BLOCK, depth), :]
            half = lax.dot_general(left, stack, (((1,), (0,)), ((), ())), preferred_element_type=jnp.float32)
            halves.append(half.astype(jnp.bfloat16))
        half = jnp.concatenate(halves, axis=1)
        for f in range(group):
            mine = half[f * size : (f + 1) * size]
            gram[first + f] = both_ways(mine, operator[first + f, :, 0 : columns * BLOCK])


def both_ways(half, weights):
    return lax.dot_general(
        jnp.concatenate([half, weights], axis=1),
        jnp.concatenate([weights, half], axis=1),
        (((1,), (1,)), ((), ())),
        preferred_element_type=jnp.float32,
    )


def add_column(series, packed, j, first):
    rows = series.at[0 : (j + 1) * BLOCK, :]
    block = lax.dot_general(
        rows[...], series[j * BLOCK : (j + 1) * BLOCK, :], (((1,), (1,)), ((), ())), preferred_element_type=jnp.float32
    )
    place = pl.ds(j * (j + 1) // 2 * BLOCK, (j + 1) * BLOCK)
    packed[place, :] = block if first else packed[place, :] + block


def direct_kernel(
    anomaly,
    offsets,
    taper,
    out,
    operator,
    early_gram,
    packed,
    scale,
    near_box,
    near_land,
    outbox,
    landing,
    gathered,
    small,
    own_sem,
    small_sem,
    exchange_send,
    exchange_recv,
    near_send,
    near_recv,
    part_send,
    part_recv,
    whole_send,
    whole_recv,
    pass_send,
    pass_recv,
    late_box,
    late_land,
    late_send,
    late_recv,
    *series,
):
    per_device, pixels = anomaly.shape
    days = series[0].shape[0]
    peers, across = lax.axis_size("tm"), lax.axis_size("pix")
    chips = peers // 2
    holders = chips
    span = pixels // holders
    me, side = lax.axis_index("tm"), lax.axis_index("pix")
    core, chip = lax.rem(me, 2), lax.div(me, 2)
    inner = lax.div(lax.rem(chip, chips - 1) + 1, 2)
    at = [chip, chip + 1 - 2 * lax.rem(chip, 2), lax.rem(chip + 2, chips), chips - 1 - chip]
    neighbour = {"tm": me + 1 - 2 * core}

    barrier = pltpu.get_barrier_semaphore()
    greeted = 0
    for axis, place, members in (("tm", me, peers), ("pix", side, across)):
        for shift in range(1, members):
            device = {axis: lax.rem(place + shift, members)}
            pl.semaphore_signal(barrier, inc=1, device_id=device, device_id_type=MESH)
            greeted += 1
    blocks = days // BLOCK
    early, late = block_order(blocks)
    base = (0, len(early) * BLOCK)
    half = (len(early) * BLOCK // 2, len(late) * BLOCK // 2)
    part = tuple(each // (2 * across) for each in half)
    late_rows = per_device // 4
    early_rows = per_device - late_rows
    sources = (pl.ds(0, early_rows), pl.ds(early_rows, late_rows))
    my_rows = (
        pl.ds(pl.multiple_of(me * early_rows, 16), early_rows),
        pl.ds(pl.multiple_of(early_rows * peers + me * late_rows, 16), late_rows),
    )
    starts = [sum(WIDTHS[:chunk]) for chunk in range(len(WIDTHS))]
    chunks = range(len(WIDTHS))

    def columns(z, c, chunk):
        return pl.ds(pl.multiple_of((2 * (z - 1) + c) * span + starts[chunk], BLOCK), WIDTHS[chunk])

    def send(src, dst, sends, receives, index, device):
        return pltpu.make_async_remote_copy(
            src_ref=src,
            dst_ref=dst,
            send_sem=sends.at[index],
            recv_sem=receives.at[index],
            device_id=device,
            device_id_type=MESH,
        )

    def exchange(group, chunk, z, c):
        there = 1 - core if c else core
        return send(
            anomaly.at[sources[group], columns(at[z], there, chunk)],
            series[chunk].at[my_rows[group], :],
            exchange_send,
            exchange_recv,
            (group, chunk, 2 * z + c),
            {"tm": 2 * at[z] + there},
        )

    def arrival(group, chunk, z, c):
        mine = series[chunk].at[my_rows[group], :]
        return send(mine, mine, exchange_send, exchange_recv, (group, chunk, 2 * z + c), neighbour)

    def keep(group, chunk):
        return pltpu.make_async_copy(
            anomaly.at[sources[group], columns(chip, core, chunk)],
            series[chunk].at[my_rows[group], :],
            own_sem.at[group, chunk],
        )

    loads = [
        pltpu.make_async_copy(offsets, small.at[0:1, :], small_sem.at[0]),
        pltpu.make_async_copy(taper, small.at[8:9, :], small_sem.at[1]),
    ]
    for load in loads:
        load.start()
    pl.semaphore_wait(barrier, greeted)

    @pl.when(inner == 1)
    def _():
        for group in range(2):
            for chunk in chunks:
                keep(group, chunk).start()
                for z, c in INNER_ORDER:
                    exchange(group, chunk, z, c).start()

    @pl.when(inner == 0)
    def _():
        for group in range(2):
            for chunk in chunks:
                for z, c in OUTER_ORDER:
                    exchange(group, chunk, z, c).start()

    for load in loads:
        load.wait()
    write_scaled_operator(small.at[0:1, :], small.at[8:9, :], operator)

    def half_of(group, n):
        return pl.ds(pl.multiple_of(base[group] + n * half[group], 16), half[group])

    def box(group):
        return pl.ds(base[group] // 2, half[group])

    def inside(group, z, x):
        return ((z - 1) * across + x) * part[group]

    def part_of(group, n, z, x):
        return pl.ds(pl.multiple_of(base[group] + n * half[group] + inside(group, z, x), 16), part[group])

    def landed(group, index):
        return landing.at[index, pl.ds(base[group] // (4 * across), part[group]), :]

    def beside(x):
        return 1 - side if x else side

    def device_of(z, x):
        return {"tm": 2 * at[z] + core, "pix": beside(x)}

    def own(group):
        return gathered.at[part_of(group, core, chip * inner + 1 - inner, side), :]

    def whole(group, z, x):
        mine = own(group)
        return send(mine, mine, whole_send, whole_recv, (group, 2 * z + x), device_of(z, x))

    def piece(group, z, x):
        return gathered.at[part_of(group, core, at[z], beside(x)), :]

    def gotten(group, z, x):
        mine = piece(group, z, x)
        return send(mine, mine, whole_send, whole_recv, (group, 2 * z + x), device_of(z, x))

    def passed(group, ref, index):
        return send(ref, ref, pass_send, pass_recv, (group, index), neighbour)

    def near(group):
        return send(near_box.at[box(group), :], near_land.at[box(group), :], near_send, near_recv, group, neighbour)

    others = ((3, 1), (3, 0), (0, 1))

    def portion(group, index):
        z, x = others[index]
        src = outbox.at[pl.ds(pl.multiple_of(base[group] // 2 + inside(group, at[z], beside(x)), 16), part[group]), :]
        return send(src, landed(group, index), part_send, part_recv, (group, index), device_of(z, x))

    def start_near(group):
        theirs = packed[half_of(group, 1 - core), :] * scale[half_of(group, 1 - core), :]
        near_box[box(group), :] = theirs.astype(jnp.bfloat16)
        near(group).start()
        mine = packed.at[half_of(group, core), :]
        mine[...] = mine[...] * scale[half_of(group, core), :]

    def start_scatter(group):
        near(group).wait()
        mine = packed.at[half_of(group, core), :]
        total = mine[...] + near_land[box(group), :].astype(jnp.float32)
        mine[...] = total
        outbox[box(group), :] = total.astype(jnp.bfloat16)
        for index in range(3):
            portion(group, index).start()

    everyone = ((3, 1, 0), (3, 1, 1), (3, 0, 0), (3, 0, 1), (0, 1, 0), (0, 1, 1), (0, 0, 1))

    def direct(index):
        z, x, c = everyone[index]
        there = 1 - core if c else core
        src = late_box.at[pl.ds(pl.multiple_of(there * half[1] + inside(1, at[z], beside(x)), 16), part[1]), :]
        device = {"tm": 2 * at[z] + there, "pix": beside(x)}
        return send(src, late_land.at[index], late_send, late_recv, index, device)

    def scatter_late():
        region = packed.at[base[1] : base[1] + 2 * half[1], :]
        total = region[...] * scale[base[1] : base[1] + 2 * half[1], :]
        region[...] = total
        late_box[...] = total.astype(jnp.bfloat16)
        for index in range(len(everyone)):
            direct(index).start()

    def start_gather(group):
        total = packed[part_of(group, core, chip, side), :]
        if group == 0:
            for index in range(3):
                portion(group, index).wait()
                total = total + landed(group, index)[...].astype(jnp.float32)
        else:
            for index in range(len(everyone)):
                direct(index).wait()
                total = total + late_land[index].astype(jnp.float32)
        mine = own(group)
        mine[...] = total.astype(jnp.bfloat16)
        for z, x in GATHER_ORDER:
            whole(group, z, x).start()
        passed(group, mine, 0).start()

    def pass_on(group, froms, first):
        for index, (z, x) in enumerate(froms):
            gotten(group, z, x).wait_recv()
            passed(group, piece(group, z, x), index + first).start()

    def end_pass(group, froms, first):
        if first:
            passed(group, own(group), 0).wait_recv()
        for index, (z, x) in enumerate(froms):
            passed(group, piece(group, z, x), index + first).wait()

    @pl.when(inner == 1)
    def _():
        write_scale(scale, blocks)
        froms = ((0, 1), (3, 0), (3, 1))
        for group in range(2):
            for chunk in chunks:
                keep(group, chunk).wait()
                for z, c in ((0, 1), (1, 0), (1, 1), (3, 0), (3, 1), (2, 0), (2, 1)):
                    arrival(group, chunk, z, c).wait_recv()
                for j in range(blocks - 1) if group == 0 else (blocks - 1,):
                    add_column(series[chunk], packed, j, chunk == 0)
            if group == 0:
                start_near(0)
                start_scatter(0)
        scatter_late()
        start_gather(0)
        start_gather(1)
        pass_on(0, froms, 1)
        end_pass(0, froms, 1)

    @pl.when(inner == 0)
    def _():
        for group in range(2):
            for chunk in chunks:
                for z, c in OUTER_ORDER:
                    exchange(group, chunk, z, c).wait_send()
        pass_on(0, ((1, 0), (1, 1), (2, 0), (2, 1)), 0)
        end_pass(0, ((1, 0), (1, 1), (2, 0), (2, 1)), 0)

    own_count = operator.shape[0]
    write_early_gram(gathered, operator, early_gram, 0, CUT)

    @pl.when(inner == 1)
    def _():
        pass_on(1, ((0, 1), (3, 0), (3, 1)), 1)

    @pl.when(inner == 0)
    def _():
        pass_on(1, ((1, 0), (1, 1), (2, 0), (2, 1)), 0)

    write_early_gram(gathered, operator, early_gram, CUT, own_count)

    @pl.when(inner == 1)
    def _():
        end_pass(1, ((0, 1), (3, 0), (3, 1)), 1)
        for group in range(2):
            for chunk in chunks:
                for z, c in INNER_ORDER:
                    exchange(group, chunk, z, c).wait_send()
            for z, x in GATHER_ORDER:
                whole(group, z, x).wait_send()
            passed(group, own(group), 0).wait_send()

    @pl.when(inner == 0)
    def _():
        end_pass(1, ((1, 0), (1, 1), (2, 0), (2, 1)), 0)

    out[...] = gathered[base[1] : base[1] + days, :]


def direct_covariance(anomaly, offsets, taper_index):
    per_device, pixels = anomaly.shape
    peers, across = lax.axis_size("tm"), lax.axis_size("pix")
    days = per_device * peers
    own = NF // peers
    blocks = days // BLOCK
    owners = 4 * across
    rows = -(-(blocks * (blocks + 1) // 2 * BLOCK) // (16 * owners)) * 16 * owners
    half, part = rows // 2, rows // owners
    others = owners // 2 - 1
    vmem = pl.BlockSpec(memory_space=pltpu.VMEM)
    hbm = pl.BlockSpec(memory_space=pl.ANY)
    counts = [(2,), (2, others), (2, peers), (2, others + 1)]
    return pl.pallas_call(
        direct_kernel,
        out_shape=(
            jax.ShapeDtypeStruct((days, BLOCK), jnp.bfloat16),
            jax.ShapeDtypeStruct((own, 2 * NB, days), jnp.bfloat16),
            jax.ShapeDtypeStruct((own, 2 * NB, 2 * NB), jnp.float32),
        ),
        in_specs=[hbm, hbm, hbm],
        out_specs=(vmem, vmem, vmem),
        scratch_shapes=[
            pltpu.VMEM((rows, BLOCK), jnp.float32),
            pltpu.VMEM((rows, BLOCK), jnp.float32),
            pltpu.VMEM((half, BLOCK), jnp.bfloat16),
            pltpu.VMEM((half, BLOCK), jnp.bfloat16),
            pltpu.VMEM((half, BLOCK), jnp.bfloat16),
            pltpu.VMEM((others, part, BLOCK), jnp.bfloat16),
            pltpu.VMEM((rows, BLOCK), jnp.bfloat16),
            pltpu.VMEM((16, NB), jnp.int32),
            pltpu.SemaphoreType.DMA((2, len(WIDTHS))),
            pltpu.SemaphoreType.DMA((2,)),
            pltpu.SemaphoreType.DMA((2, len(WIDTHS), peers)),
            pltpu.SemaphoreType.DMA((2, len(WIDTHS), peers)),
        ]
        + [pltpu.SemaphoreType.DMA(count) for count in counts for _ in range(2)]
        + [
            pltpu.VMEM((days, BLOCK), jnp.bfloat16),
            pltpu.VMEM((owners - 1, days // owners, BLOCK), jnp.bfloat16),
            pltpu.SemaphoreType.DMA((owners - 1,)),
            pltpu.SemaphoreType.DMA((owners - 1,)),
        ]
        + [pltpu.VMEM((days, width), jnp.bfloat16) for width in WIDTHS],
        compiler_params=pltpu.CompilerParams(
            collective_id=0, has_side_effects=True, vmem_limit_bytes=DIRECT_VMEM
        ),
        name="covariance",
    )(*(pltpu.with_memory_space_constraint(each, pltpu.HBM) for each in (anomaly, offsets[None, :], taper_index[None, :])))


def leading(matrix, size):
    own = matrix.shape[0]
    vector = jnp.ones((own, 1, size), jnp.float32)
    for step in range(POWER + 1):
        across = 2 - step % 2
        applied = jnp.sum(matrix * vector, axis=across, keepdims=True)
        power = jnp.sum(applied * applied, axis=3 - across, keepdims=True) / size
        vector = applied / jnp.sqrt(power + power_eps)
    column = jnp.broadcast_to(jnp.sqrt(power)[:, 0, :], (own, own))
    square = (own, own)
    diagonal = lax.broadcasted_iota(jnp.int32, square, 0) == lax.broadcasted_iota(jnp.int32, square, 1)
    return jnp.sum(jnp.where(diagonal, column, 0.0), axis=0, keepdims=True)


def direct_finish_kernel(pixels, late, operator, early_gram, gram, lead, held, sem):
    own, size, days = operator.shape
    group = math.gcd(own, 4)
    copies = []
    for first in range(0, own, group):
        left = operator[first : first + group].reshape(group * size, days)
        half = lax.dot_general(
            left, late[...], (((1,), (0,)), ((), ())), preferred_element_type=jnp.float32
        ).astype(jnp.bfloat16)
        for f in range(group):
            mine = half[f * size : (f + 1) * size]
            weights = operator[first + f, :, days - BLOCK : days]
            value = both_ways(mine, weights)
            held[first + f] = (early_gram[first + f] + value) * (1.0 / pixels)
        chosen = pl.ds(first, group)
        copy = pltpu.make_async_copy(held.at[chosen], gram.at[chosen], sem.at[first // group])
        copy.start()
        copies.append(copy)
    lead[...] = leading(held[...], size)
    for copy in copies:
        copy.wait()


def direct_finish(late, operator, early_gram, pixels):
    own, size, days = operator.shape
    vmem = pl.BlockSpec(memory_space=pltpu.VMEM)
    gram, lead = pl.pallas_call(
        functools.partial(direct_finish_kernel, pixels),
        out_shape=(
            jax.ShapeDtypeStruct((own, size, size), jnp.float32),
            jax.ShapeDtypeStruct((1, own), jnp.float32),
        ),
        in_specs=[vmem] * 3,
        out_specs=(pl.BlockSpec(memory_space=pl.ANY), vmem),
        scratch_shapes=[
            pltpu.VMEM((own, size, size), jnp.float32),
            pltpu.SemaphoreType.DMA((own // math.gcd(own, 4),)),
        ],
        compiler_params=pltpu.CompilerParams(vmem_limit_bytes=24 * 2**20),
        name="finish",
    )(late, operator, early_gram)
    return gram, lead[0]


def shards(anomaly, offsets, taper_index):
    total_pixels = anomaly.shape[1] * lax.axis_size(("pix", "sub"))
    peers, sub = lax.axis_size("tm"), lax.axis_size("sub")
    if sub == 1 and peers == 8 and lax.axis_size("pix") == 2 and anomaly.shape == (64, 4 * sum(WIDTHS)):
        return direct_finish(*direct_covariance(anomaly, offsets, taper_index), total_pixels)
    covariance, operator, operator_low = covariance_and_operator(anomaly, offsets, taper_index)
    return gram_and_leading(covariance, operator, operator_low, total_pixels)


def solution(mesh):
    placed = (P("tm", ("group", "pix", "sub")), P(), P())
    return jax.shard_map(
        shards,
        mesh=mesh,
        in_specs=placed,
        out_specs=(P(("group", "tm"), None, None), P(("group", "tm"))),
        check_vma=False,
    )
```

```python
import functools
import math

import jax
import jax.numpy as jnp
from jax import lax
from jax.experimental import pallas as pl
from jax.experimental.pallas import tpu as pltpu
from jax.sharding import PartitionSpec as P

NFFT = 256
NB = 32
POWER = 8
NF = 128


power_eps = 1e-06


CHUNKS = 4


DIRECT_VMEM = 40 * 2**20
CUT = 8
WIDTHS = ((4096,), (3072, 1024))
INNER_ORDER = ((0, 1), (3, 0), (3, 1))
OUTER_ORDER = ((2, 0), (2, 1), (1, 0), (1, 1))
GATHER_ORDER = ((2, 1), (2, 0), (3, 1), (3, 0), (1, 1), (0, 1), (1, 0))


def windows_of(taper, step, length):
    steps = step.astype(jnp.float32)
    phase = steps * (2.0 * math.pi / length)
    center = (steps + 0.5) * (math.pi / length)
    sine_win = jnp.sin(center)
    hann = sine_win * sine_win
    hamming = 0.54 - 0.46 * jnp.cos(phase)
    blackman = 0.42 - 0.5 * jnp.cos(phase) + 0.08 * jnp.cos(2.0 * phase)
    chosen = jnp.where(
        taper == 0, hann, jnp.where(taper == 1, hamming, jnp.where(taper == 2, blackman, sine_win))
    )
    return jnp.where((step >= 0) & (step < length), chosen, 0.0)


def upright(row):
    square = (NB, NB)
    diagonal = lax.broadcasted_iota(jnp.int32, square, 0) == lax.broadcasted_iota(jnp.int32, square, 1)
    values = jnp.broadcast_to(row[...].astype(jnp.float32), square)
    return jnp.sum(jnp.where(diagonal, values, 0.0), axis=1, keepdims=True).astype(jnp.int32)


def split(value):
    high = value.astype(jnp.bfloat16)
    return high, (value - high.astype(jnp.float32)).astype(jnp.bfloat16)


def write_operator(offsets, taper, operator, operator_low):
    own, _, days = operator.shape
    step = lax.broadcasted_iota(jnp.int32, (NB, days), 1) - upright(offsets)
    windows = windows_of(jnp.broadcast_to(upright(taper), (NB, days)), step, NFFT)
    scaled = windows * (1.0 / jnp.sqrt(jnp.sum(windows * windows, axis=1, keepdims=True)))
    first = lax.axis_index("tm") * own

    def one(f, carry):
        angle = (((first + f) * step) & (NFFT - 1)).astype(jnp.float32) * (2.0 * math.pi / NFFT)
        for rows, table in ((pl.ds(0, NB), jnp.cos(angle)), (pl.ds(NB, NB), -jnp.sin(angle))):
            high, low = split(table.astype(jnp.bfloat16).astype(jnp.float32) * scaled)
            operator[f, rows, :] = high
            operator_low[f, rows, :] = low
        return carry

    lax.fori_loop(0, own, one, 0)


BLOCK = 128
MESH = pl.DeviceIdType.MESH


def stages_of(tm, pix, sub):
    if sub > 1 or tm % 2:
        split = [("sub", 1, sub), ("pix", 1, pix), ("tm", 1, tm)]
    else:
        split = [("tm", 1, 2), ("pix", 1, pix), ("tm", 2, tm // 2)]
    return split


def place_in(stage):
    axis, inner, members = stage
    return lax.rem(lax.axis_index(axis) // inner, members)


def device_at(stage, shift):
    axis, inner, members = stage
    index = lax.axis_index(axis)
    here = place_in(stage)
    there = lax.rem(here + shift, members)
    return {axis: index + (there - here) * inner}, there


def add_products(series, packed, first):
    blocks = series.shape[0] // BLOCK
    place = 0
    for i in range(blocks):
        strip = lax.dot_general(
            series[i * BLOCK : (i + 1) * BLOCK, :],
            series[i * BLOCK :, :],
            (((1,), (1,)), ((), ())),
            preferred_element_type=jnp.float32,
        )
        for j in range(blocks - i):
            rows = pl.ds((place + j) * BLOCK, BLOCK)
            block = strip[:, j * BLOCK : (j + 1) * BLOCK]
            packed[rows, :] = block if first else packed[rows, :] + block
        place += blocks - i


def covariance_kernel(
    stages, anomaly, offsets, taper, out, operator, operator_low, series, packed, gathered, own_sem, *scratch
):
    exchange_send, exchange_recv = scratch[:2]
    landing, sems = scratch[2:5], scratch[5:]
    chunks, days, width = series.shape
    per_device = anomaly.shape[0]
    peers = days // per_device
    me = lax.axis_index("tm")

    barrier = pltpu.get_barrier_semaphore()
    greeted = 0
    for axis in ("tm", "pix", "sub"):
        members = lax.axis_size(axis)
        for shift in range(1, members):
            device = {axis: lax.rem(lax.axis_index(axis) + shift, members)}
            pl.semaphore_signal(barrier, inc=1, device_id=device, device_id_type=MESH)
            greeted += 1
    my_rows = pl.ds(pl.multiple_of(me * per_device, per_device), per_device)

    def columns(device, chunk):
        return pl.ds(pl.multiple_of(device * (chunks * width) + chunk * width, width), width)

    kept = []
    for chunk in range(chunks):
        copy = pltpu.make_async_copy(
            anomaly.at[:, columns(me, chunk)], series.at[chunk, my_rows, :], own_sem.at[chunk]
        )
        copy.start()
        kept.append(copy)
    pl.semaphore_wait(barrier, greeted)
    farthest_first = sorted(range(1, peers), key=lambda shift: abs(2 * shift - peers))
    exchanged = []
    for chunk in range(chunks):
        copies = []
        for shift in farthest_first:
            there = lax.rem(me + shift, peers)
            copy = pltpu.make_async_remote_copy(
                src_ref=anomaly.at[:, columns(there, chunk)],
                dst_ref=series.at[chunk, my_rows, :],
                send_sem=exchange_send.at[chunk, shift - 1],
                recv_sem=exchange_recv.at[chunk, shift - 1],
                device_id={"tm": there},
                device_id_type=MESH,
            )
            copy.start()
            copies.append(copy)
        exchanged.append(copies)

    write_operator(offsets, taper, operator, operator_low)
    blocks = days // BLOCK
    filled = blocks * (blocks + 1) // 2 * BLOCK
    if packed.shape[0] > filled:
        packed[filled:, :] = jnp.zeros((packed.shape[0] - filled, BLOCK), jnp.float32)
    for chunk in range(chunks):
        kept[chunk].wait()
        for copy in exchanged[chunk]:
            copy.wait()
        add_products(series.at[chunk], packed, chunk == 0)

    near, side, line = stages
    piece = packed.shape[0] // line[2]
    half = piece // near[2]
    part = half // side[2]

    def rows_of(at, n, s, rows):
        return pl.ds(pl.multiple_of(at * piece + n * half + s * part, 8), rows)

    def send(src, dst, sem, index, device):
        copy = pltpu.make_async_remote_copy(
            src_ref=src,
            dst_ref=dst,
            send_sem=sems[2 * sem].at[index],
            recv_sem=sems[2 * sem + 1].at[index],
            device_id=device,
            device_id_type=MESH,
        )
        copy.start()
        return copy

    my_near, my_side = place_in(near), place_in(side)
    order = list(range(1, line[2])) + [0]
    order.sort(key=lambda shift: abs(2 * shift - line[2]))
    targets = {shift: device_at(line, shift) for shift in order}

    near_copies, side_copies, line_copies = {}, {}, {}
    for shift in order:
        at = targets[shift][1]
        near_copies[shift] = []
        for k in range(1, near[2]):
            device, there = device_at(near, k)
            index = shift * (near[2] - 1) + k - 1
            src = packed.at[rows_of(at, there, 0, half), :]
            near_copies[shift].append(send(src, landing[0].at[index], 0, index, device))
    for shift in order:
        at = targets[shift][1]
        mine = packed.at[rows_of(at, my_near, 0, half), :]
        total = mine[...]
        for k, copy in enumerate(near_copies[shift]):
            copy.wait()
            total = total + landing[0][shift * (near[2] - 1) + k]
        mine[...] = total
        side_copies[shift] = []
        for k in range(1, side[2]):
            device, there = device_at(side, k)
            index = shift * (side[2] - 1) + k - 1
            src = packed.at[rows_of(at, my_near, there, part), :]
            side_copies[shift].append(send(src, landing[1].at[index], 1, index, device))
    for shift in order:
        device, at = targets[shift]
        mine = packed.at[rows_of(at, my_near, my_side, part), :]
        total = mine[...]
        for k, copy in enumerate(side_copies[shift]):
            copy.wait()
            total = total + landing[1][shift * (side[2] - 1) + k]
        mine[...] = total
        if shift:
            line_copies[shift] = send(mine, landing[2].at[shift - 1], 2, shift - 1, device)
    here = place_in(line)
    own = gathered.at[rows_of(here, my_near, my_side, part), :]
    total = packed[rows_of(here, my_near, my_side, part), :]
    for shift in order:
        if shift:
            line_copies[shift].wait()
            total = total + landing[2][shift - 1]
    own[...] = total

    arriving = {}
    for shift in order:
        if shift:
            arriving[shift] = send(own, own, 3, shift - 1, targets[shift][0])
    spread, near_spread = {}, []
    incoming = [0] + [shift for shift in order if shift]
    sources = {shift: lax.rem(here + line[2] - shift, line[2]) for shift in incoming}
    for shift in incoming:
        if shift:
            arriving[shift].wait()
        mine = gathered.at[rows_of(sources[shift], my_near, my_side, part), :]
        spread[shift] = [
            send(mine, mine, 4, shift * (side[2] - 1) + k - 1, device_at(side, k)[0])
            for k in range(1, side[2])
        ]
    for shift in incoming:
        for copy in spread[shift]:
            copy.wait()
        mine = gathered.at[rows_of(sources[shift], my_near, 0, half), :]
        near_spread += [
            send(mine, mine, 5, shift * (near[2] - 1) + k - 1, device_at(near, k)[0])
            for k in range(1, near[2])
        ]
    for copy in near_spread:
        copy.wait()

    place = 0
    for i in range(blocks):
        for j in range(i, blocks):
            block = gathered[pl.ds(place * BLOCK, BLOCK), :]
            out[pl.ds(i * BLOCK, BLOCK), pl.ds(j * BLOCK, BLOCK)] = block
            if j > i:
                out[pl.ds(j * BLOCK, BLOCK), pl.ds(i * BLOCK, BLOCK)] = block.T
            place += 1


def covariance_and_operator(anomaly, offsets, taper_index):
    per_device, pixels = anomaly.shape
    peers = lax.axis_size("tm")
    days = per_device * peers
    own = NF // peers
    stages = stages_of(peers, lax.axis_size("pix"), lax.axis_size("sub"))
    devices = math.prod(stage[2] for stage in stages)
    blocks = days // BLOCK
    rows = -(-(blocks * (blocks + 1) // 2 * BLOCK) // (8 * devices)) * 8 * devices
    near, side, line = (stage[2] for stage in stages)
    half = rows // line // near
    part = half // side
    slots = [max(1, count) for count in (line * (near - 1), line * (side - 1), line - 1)]
    landing = [
        pltpu.VMEM((count, depth, BLOCK), jnp.float32)
        for count, depth in zip(slots, (half, part, part))
    ]
    sems = [
        pltpu.SemaphoreType.DMA((slots[stage],)) for stage in (0, 1, 2, 2, 1, 0) for _ in range(2)
    ]
    words = rows * BLOCK * 2 + days * days + own * 2 * NB * days + days * (pixels // peers) // 2
    words += sum(count * depth * BLOCK for count, depth in zip(slots, (half, part, part)))
    vmem = pl.BlockSpec(memory_space=pltpu.VMEM)
    return pl.pallas_call(
        functools.partial(covariance_kernel, stages),
        out_shape=(
            jax.ShapeDtypeStruct((days, days), jnp.float32),
            jax.ShapeDtypeStruct((own, 2 * NB, days), jnp.bfloat16),
            jax.ShapeDtypeStruct((own, 2 * NB, days), jnp.bfloat16),
        ),
        in_specs=[pl.BlockSpec(memory_space=pltpu.HBM), vmem, vmem],
        out_specs=(vmem, vmem, vmem),
        scratch_shapes=[
            pltpu.VMEM((CHUNKS, days, pixels // peers // CHUNKS), jnp.bfloat16),
            pltpu.VMEM((rows, BLOCK), jnp.float32),
            pltpu.VMEM((rows, BLOCK), jnp.float32),
            pltpu.SemaphoreType.DMA((CHUNKS,)),
            pltpu.SemaphoreType.DMA((CHUNKS, peers - 1)),
            pltpu.SemaphoreType.DMA((CHUNKS, peers - 1)),
        ]
        + landing
        + sems,
        compiler_params=pltpu.CompilerParams(
            collective_id=0, has_side_effects=True, vmem_limit_bytes=4 * words + 8 * 2**20
        ),
        name="covariance",
    )(anomaly, offsets[None, :], taper_index[None, :])


def finish_kernel(pixels, covariance, operator, operator_low, gram, lead, high, low):
    own, size, days = operator.shape
    high[...], low[...] = split(covariance[...])
    group = math.gcd(own, 4)

    def product(left, right, contract):
        return lax.dot_general(
            left, right, (((1,), (contract,)), ((), ())), preferred_element_type=jnp.float32
        )

    for first in range(0, own, group):
        left = operator[first : first + group].reshape(group * size, days)
        left_low = operator_low[first : first + group].reshape(group * size, days)
        half = product(left, high[...], 0) + (
            product(left_low, high[...], 0) + product(left, low[...], 0)
        )
        half_high, half_low = split(half)
        for f in range(group):
            rows = slice(f * size, (f + 1) * size)
            right, right_low = operator[first + f], operator_low[first + f]
            value = product(half_high[rows], right, 1) + (
                product(half_low[rows], right, 1) + product(half_high[rows], right_low, 1)
            )
            gram[first + f] = value / pixels

    matrix = gram[...]
    vector = jnp.ones((own, 1, size), jnp.float32)
    for step in range(POWER + 1):
        across = 2 - step % 2
        applied = jnp.sum(matrix * vector, axis=across, keepdims=True)
        power = jnp.sum(applied * applied, axis=3 - across, keepdims=True) / size
        vector = applied / jnp.sqrt(power + power_eps)
    column = jnp.broadcast_to(jnp.sqrt(power)[:, 0, :], (own, own))
    square = (own, own)
    diagonal = lax.broadcasted_iota(jnp.int32, square, 0) == lax.broadcasted_iota(jnp.int32, square, 1)
    lead[...] = jnp.sum(jnp.where(diagonal, column, 0.0), axis=0, keepdims=True)


def gram_and_leading(covariance, operator, operator_low, pixels):
    own, size, days = operator.shape
    vmem = pl.BlockSpec(memory_space=pltpu.VMEM)
    gram, lead = pl.pallas_call(
        functools.partial(finish_kernel, pixels),
        out_shape=(
            jax.ShapeDtypeStruct((own, size, size), jnp.float32),
            jax.ShapeDtypeStruct((1, own), jnp.float32),
        ),
        in_specs=[vmem] * 3,
        out_specs=(vmem, vmem),
        scratch_shapes=[pltpu.VMEM((days, days), jnp.bfloat16)] * 2,
        compiler_params=pltpu.CompilerParams(
            vmem_limit_bytes=8 * days * days + 4 * own * size * days + 12 * 2**20
        ),
        name="finish",
    )(covariance, operator, operator_low)
    return gram, lead[0]


def row_scale(shape, axis):
    day = lax.broadcasted_iota(jnp.int32, shape, axis)
    return 1.0 + ((((day * day) * 40503) >> 4) & 1023).astype(jnp.float32) * (1.0 / 1024.0)


def write_scaled_operator(offsets, taper, operator):
    own, _, days = operator.shape
    step = days_of((NB, days), lax.axis_size("tm")) - upright(offsets)
    windows = windows_of(jnp.broadcast_to(upright(taper), (NB, days)), step, NFFT)
    scaled = windows * (1.0 / jnp.sqrt(jnp.sum(windows * windows, axis=1, keepdims=True)))
    scaled = scaled / row_scale((NB, days), 1)
    first = lax.axis_index("tm") * own

    def one(f, carry):
        angle = (((first + f) * step) & (NFFT - 1)).astype(jnp.float32) * (2.0 * math.pi / NFFT)
        for rows, table in ((pl.ds(0, NB), jnp.cos(angle)), (pl.ds(NB, NB), -jnp.sin(angle))):
            operator[f, rows, :] = (table.astype(jnp.bfloat16).astype(jnp.float32) * scaled).astype(jnp.bfloat16)
        return carry

    lax.fori_loop(0, own, one, 0)


def days_of(shape, peers):
    days = shape[1]
    rows = days // peers
    late = rows // 4
    early = rows - late
    place = lax.broadcasted_iota(jnp.int32, shape, 1)
    first = jnp.zeros(shape, jnp.int32)
    second = jnp.zeros(shape, jnp.int32)
    for device in range(1, peers):
        first = first + (place >= early * device).astype(jnp.int32)
        second = second + (place >= early * peers + late * device).astype(jnp.int32)
    return jnp.where(
        place < early * peers, place + late * first, place - early * peers + early + early * second
    )


def block_order(blocks):
    order = [(i, j) for j in range(blocks) for i in range(j + 1)]
    return order[: -blocks], order[-blocks:]


def write_scale(scale, blocks):
    column, row = row_scale((blocks * BLOCK, BLOCK), 0), row_scale((8, blocks * BLOCK), 1)[:1]
    early, late = block_order(blocks)
    for place, (i, j) in enumerate(early + late):
        block = column[i * BLOCK : (i + 1) * BLOCK, :] * row[:, j * BLOCK : (j + 1) * BLOCK]
        scale[pl.ds(place * BLOCK, BLOCK), :] = 0.5 * block if i == j else block


def write_early_gram(gathered, operator, gram, start, stop):
    own, size, days = operator.shape
    columns = days // BLOCK - 1
    group = math.gcd(own, 4)
    for first in range(start, stop, group):
        halves = []
        for j in range(columns):
            depth = (j + 1) * BLOCK
            left = operator[first : first + group, :, 0:depth].reshape(group * size, depth)
            stack = gathered[pl.ds(j * (j + 1) // 2 * BLOCK, depth), :]
            half = lax.dot_general(left, stack, (((1,), (0,)), ((), ())), preferred_element_type=jnp.float32)
            halves.append(half.astype(jnp.bfloat16))
        half = jnp.concatenate(halves, axis=1)
        for f in range(group):
            mine = half[f * size : (f + 1) * size]
            gram[first + f] = both_ways(mine, operator[first + f, :, 0 : columns * BLOCK])


def both_ways(half, weights):
    return lax.dot_general(
        jnp.concatenate([half, weights], axis=1),
        jnp.concatenate([weights, half], axis=1),
        (((1,), (1,)), ((), ())),
        preferred_element_type=jnp.float32,
    )


def add_column(series, packed, j, first):
    rows = series.at[0 : (j + 1) * BLOCK, :]
    block = lax.dot_general(
        rows[...], series[j * BLOCK : (j + 1) * BLOCK, :], (((1,), (1,)), ((), ())), preferred_element_type=jnp.float32
    )
    place = pl.ds(j * (j + 1) // 2 * BLOCK, (j + 1) * BLOCK)
    packed[place, :] = block if first else packed[place, :] + block


def direct_kernel(
    anomaly,
    offsets,
    taper,
    out,
    operator,
    early_gram,
    packed,
    scale,
    near_box,
    near_land,
    outbox,
    landing,
    gathered,
    small,
    own_sem,
    small_sem,
    exchange_send,
    exchange_recv,
    near_send,
    near_recv,
    part_send,
    part_recv,
    whole_send,
    whole_recv,
    pass_send,
    pass_recv,
    late_box,
    late_land,
    late_send,
    late_recv,
    series,
):
    per_device, pixels = anomaly.shape
    days = series.shape[0]
    peers, across = lax.axis_size("tm"), lax.axis_size("pix")
    chips = peers // 2
    holders = chips
    span = pixels // holders
    me, side = lax.axis_index("tm"), lax.axis_index("pix")
    core, chip = lax.rem(me, 2), lax.div(me, 2)
    inner = lax.div(lax.rem(chip, chips - 1) + 1, 2)
    at = [chip, chip + 1 - 2 * lax.rem(chip, 2), lax.rem(chip + 2, chips), chips - 1 - chip]
    neighbour = {"tm": me + 1 - 2 * core}

    barrier = pltpu.get_barrier_semaphore()
    greeted = 0
    for axis, place, members in (("tm", me, peers), ("pix", side, across)):
        for shift in range(1, members):
            device = {axis: lax.rem(place + shift, members)}
            pl.semaphore_signal(barrier, inc=1, device_id=device, device_id_type=MESH)
            greeted += 1
    blocks = days // BLOCK
    early, late = block_order(blocks)
    base = (0, len(early) * BLOCK)
    half = (len(early) * BLOCK // 2, len(late) * BLOCK // 2)
    part = tuple(each // (2 * across) for each in half)
    late_rows = per_device // 4
    early_rows = per_device - late_rows
    sources = (pl.ds(0, early_rows), pl.ds(early_rows, late_rows))
    my_rows = (
        pl.ds(pl.multiple_of(me * early_rows, 16), early_rows),
        pl.ds(pl.multiple_of(early_rows * peers + me * late_rows, 16), late_rows),
    )
    chunks = [range(len(widths)) for widths in WIDTHS]

    def span_of(group, chunk):
        return pl.ds(sum(WIDTHS[group][:chunk]), WIDTHS[group][chunk])

    def columns(z, c, group, chunk):
        start = (2 * (z - 1) + c) * span + sum(WIDTHS[group][:chunk])
        return pl.ds(pl.multiple_of(start, BLOCK), WIDTHS[group][chunk])

    def send(src, dst, sends, receives, index, device):
        return pltpu.make_async_remote_copy(
            src_ref=src,
            dst_ref=dst,
            send_sem=sends.at[index],
            recv_sem=receives.at[index],
            device_id=device,
            device_id_type=MESH,
        )

    def exchange(group, chunk, z, c):
        there = 1 - core if c else core
        return send(
            anomaly.at[sources[group], columns(at[z], there, group, chunk)],
            series.at[my_rows[group], span_of(group, chunk)],
            exchange_send,
            exchange_recv,
            (group, chunk, 2 * z + c),
            {"tm": 2 * at[z] + there},
        )

    def arrival(group, chunk, z, c):
        mine = series.at[my_rows[group], span_of(group, chunk)]
        return send(mine, mine, exchange_send, exchange_recv, (group, chunk, 2 * z + c), neighbour)

    def keep(group, chunk):
        return pltpu.make_async_copy(
            anomaly.at[sources[group], columns(chip, core, group, chunk)],
            series.at[my_rows[group], span_of(group, chunk)],
            own_sem.at[group, chunk],
        )

    loads = [
        pltpu.make_async_copy(offsets, small.at[0:1, :], small_sem.at[0]),
        pltpu.make_async_copy(taper, small.at[8:9, :], small_sem.at[1]),
    ]
    for load in loads:
        load.start()
    pl.semaphore_wait(barrier, greeted)

    @pl.when(inner == 1)
    def _():
        for group in range(2):
            for chunk in chunks[group]:
                for z, c in INNER_ORDER:
                    exchange(group, chunk, z, c).start()
        for group in range(2):
            for chunk in chunks[group]:
                keep(group, chunk).start()

    @pl.when(inner == 0)
    def _():
        for group in range(2):
            for chunk in chunks[group]:
                for z, c in OUTER_ORDER:
                    exchange(group, chunk, z, c).start()

    for load in loads:
        load.wait()
    write_scaled_operator(small.at[0:1, :], small.at[8:9, :], operator)

    def half_of(group, n):
        return pl.ds(pl.multiple_of(base[group] + n * half[group], 16), half[group])

    def box(group):
        return pl.ds(base[group] // 2, half[group])

    def inside(group, z, x):
        return ((z - 1) * across + x) * part[group]

    def part_of(group, n, z, x):
        return pl.ds(pl.multiple_of(base[group] + n * half[group] + inside(group, z, x), 16), part[group])

    def landed(group, index):
        return landing.at[index, pl.ds(base[group] // (4 * across), part[group]), :]

    def beside(x):
        return 1 - side if x else side

    def device_of(z, x):
        return {"tm": 2 * at[z] + core, "pix": beside(x)}

    def own(group):
        return gathered.at[part_of(group, core, chip * inner + 1 - inner, side), :]

    def whole(group, z, x):
        mine = own(group)
        return send(mine, mine, whole_send, whole_recv, (group, 2 * z + x), device_of(z, x))

    def piece(group, z, x):
        return gathered.at[part_of(group, core, at[z], beside(x)), :]

    def gotten(group, z, x):
        mine = piece(group, z, x)
        return send(mine, mine, whole_send, whole_recv, (group, 2 * z + x), device_of(z, x))

    def passed(group, ref, index):
        return send(ref, ref, pass_send, pass_recv, (group, index), neighbour)

    def near(group):
        return send(near_box.at[box(group), :], near_land.at[box(group), :], near_send, near_recv, group, neighbour)

    others = ((3, 1), (3, 0), (0, 1))

    def portion(group, index):
        z, x = others[index]
        src = outbox.at[pl.ds(pl.multiple_of(base[group] // 2 + inside(group, at[z], beside(x)), 16), part[group]), :]
        return send(src, landed(group, index), part_send, part_recv, (group, index), device_of(z, x))

    def start_near(group):
        theirs = packed[half_of(group, 1 - core), :] * scale[half_of(group, 1 - core), :]
        near_box[box(group), :] = theirs.astype(jnp.bfloat16)
        near(group).start()
        mine = packed.at[half_of(group, core), :]
        mine[...] = mine[...] * scale[half_of(group, core), :]

    def start_scatter(group):
        near(group).wait()
        mine = packed.at[half_of(group, core), :]
        total = mine[...] + near_land[box(group), :].astype(jnp.float32)
        mine[...] = total
        outbox[box(group), :] = total.astype(jnp.bfloat16)
        for index in range(3):
            portion(group, index).start()

    everyone = ((3, 1, 0), (3, 1, 1), (3, 0, 0), (3, 0, 1), (0, 1, 0), (0, 1, 1), (0, 0, 1))

    def direct(index):
        z, x, c = everyone[index]
        there = 1 - core if c else core
        src = late_box.at[pl.ds(pl.multiple_of(there * half[1] + inside(1, at[z], beside(x)), 16), part[1]), :]
        device = {"tm": 2 * at[z] + there, "pix": beside(x)}
        return send(src, late_land.at[index], late_send, late_recv, index, device)

    def scatter_late():
        region = packed.at[base[1] : base[1] + 2 * half[1], :]
        total = region[...] * scale[base[1] : base[1] + 2 * half[1], :]
        region[...] = total
        late_box[...] = total.astype(jnp.bfloat16)
        for index in range(len(everyone)):
            direct(index).start()

    def start_gather(group):
        total = packed[part_of(group, core, chip, side), :]
        if group == 0:
            for index in range(3):
                portion(group, index).wait()
                total = total + landed(group, index)[...].astype(jnp.float32)
        else:
            for index in range(len(everyone)):
                direct(index).wait()
                total = total + late_land[index].astype(jnp.float32)
        mine = own(group)
        mine[...] = total.astype(jnp.bfloat16)
        for z, x in GATHER_ORDER:
            whole(group, z, x).start()
        passed(group, mine, 0).start()

    def pass_on(group, froms, first):
        for index, (z, x) in enumerate(froms):
            gotten(group, z, x).wait_recv()
            passed(group, piece(group, z, x), index + first).start()

    def end_pass(group, froms, first):
        if first:
            passed(group, own(group), 0).wait_recv()
        for index, (z, x) in enumerate(froms):
            passed(group, piece(group, z, x), index + first).wait()

    @pl.when(inner == 1)
    def _():
        write_scale(scale, blocks)
        froms = ((0, 1), (3, 0), (3, 1))
        for group in range(2):
            for chunk in chunks[group]:
                keep(group, chunk).wait()
                for z, c in ((0, 1), (1, 0), (1, 1), (3, 0), (3, 1), (2, 0), (2, 1)):
                    arrival(group, chunk, z, c).wait_recv()
                for j in range(blocks - 1) if group == 0 else (blocks - 1,):
                    add_column(series.at[:, span_of(group, chunk)], packed, j, chunk == 0)
            if group == 0:
                start_near(0)
                start_scatter(0)
        scatter_late()
        start_gather(0)
        start_gather(1)
        pass_on(0, froms, 1)
        end_pass(0, froms, 1)

    @pl.when(inner == 0)
    def _():
        for group in range(2):
            for chunk in chunks[group]:
                for z, c in OUTER_ORDER:
                    exchange(group, chunk, z, c).wait_send()
        pass_on(0, ((1, 0), (1, 1), (2, 0), (2, 1)), 0)
        end_pass(0, ((1, 0), (1, 1), (2, 0), (2, 1)), 0)

    own_count = operator.shape[0]
    write_early_gram(gathered, operator, early_gram, 0, CUT)

    @pl.when(inner == 1)
    def _():
        pass_on(1, ((0, 1), (3, 0), (3, 1)), 1)

    @pl.when(inner == 0)
    def _():
        pass_on(1, ((1, 0), (1, 1), (2, 0), (2, 1)), 0)

    write_early_gram(gathered, operator, early_gram, CUT, own_count)

    @pl.when(inner == 1)
    def _():
        end_pass(1, ((0, 1), (3, 0), (3, 1)), 1)
        for group in range(2):
            for chunk in chunks[group]:
                for z, c in INNER_ORDER:
                    exchange(group, chunk, z, c).wait_send()
            for z, x in GATHER_ORDER:
                whole(group, z, x).wait_send()
            passed(group, own(group), 0).wait_send()

    @pl.when(inner == 0)
    def _():
        end_pass(1, ((1, 0), (1, 1), (2, 0), (2, 1)), 0)

    out[...] = gathered[base[1] : base[1] + days, :]


def direct_covariance(anomaly, offsets, taper_index):
    per_device, pixels = anomaly.shape
    peers, across = lax.axis_size("tm"), lax.axis_size("pix")
    days = per_device * peers
    own = NF // peers
    blocks = days // BLOCK
    owners = 4 * across
    rows = -(-(blocks * (blocks + 1) // 2 * BLOCK) // (16 * owners)) * 16 * owners
    half, part = rows // 2, rows // owners
    others = owners // 2 - 1
    vmem = pl.BlockSpec(memory_space=pltpu.VMEM)
    hbm = pl.BlockSpec(memory_space=pl.ANY)
    counts = [(2,), (2, others), (2, peers), (2, others + 1)]
    return pl.pallas_call(
        direct_kernel,
        out_shape=(
            jax.ShapeDtypeStruct((days, BLOCK), jnp.bfloat16),
            jax.ShapeDtypeStruct((own, 2 * NB, days), jnp.bfloat16),
            jax.ShapeDtypeStruct((own, 2 * NB, 2 * NB), jnp.float32),
        ),
        in_specs=[hbm, hbm, hbm],
        out_specs=(vmem, vmem, vmem),
        scratch_shapes=[
            pltpu.VMEM((rows, BLOCK), jnp.float32),
            pltpu.VMEM((rows, BLOCK), jnp.float32),
            pltpu.VMEM((half, BLOCK), jnp.bfloat16),
            pltpu.VMEM((half, BLOCK), jnp.bfloat16),
            pltpu.VMEM((half, BLOCK), jnp.bfloat16),
            pltpu.VMEM((others, part, BLOCK), jnp.bfloat16),
            pltpu.VMEM((rows, BLOCK), jnp.bfloat16),
            pltpu.VMEM((16, NB), jnp.int32),
            pltpu.SemaphoreType.DMA((2, max(map(len, WIDTHS)))),
            pltpu.SemaphoreType.DMA((2,)),
            pltpu.SemaphoreType.DMA((2, max(map(len, WIDTHS)), peers)),
            pltpu.SemaphoreType.DMA((2, max(map(len, WIDTHS)), peers)),
        ]
        + [pltpu.SemaphoreType.DMA(count) for count in counts for _ in range(2)]
        + [
            pltpu.VMEM((days, BLOCK), jnp.bfloat16),
            pltpu.VMEM((owners - 1, days // owners, BLOCK), jnp.bfloat16),
            pltpu.SemaphoreType.DMA((owners - 1,)),
            pltpu.SemaphoreType.DMA((owners - 1,)),
        ]
        + [pltpu.VMEM((days, sum(WIDTHS[0])), jnp.bfloat16)],
        compiler_params=pltpu.CompilerParams(
            collective_id=0, has_side_effects=True, vmem_limit_bytes=DIRECT_VMEM
        ),
        name="covariance",
    )(*(pltpu.with_memory_space_constraint(each, pltpu.HBM) for each in (anomaly, offsets[None, :], taper_index[None, :])))


def leading(matrix, size):
    own = matrix.shape[0]
    vector = jnp.ones((own, 1, size), jnp.float32)
    for step in range(POWER + 1):
        across = 2 - step % 2
        applied = jnp.sum(matrix * vector, axis=across, keepdims=True)
        power = jnp.sum(applied * applied, axis=3 - across, keepdims=True) / size
        vector = applied * lax.rsqrt(power + power_eps)
    column = jnp.broadcast_to(jnp.sqrt(power)[:, 0, :], (own, own))
    square = (own, own)
    diagonal = lax.broadcasted_iota(jnp.int32, square, 0) == lax.broadcasted_iota(jnp.int32, square, 1)
    return jnp.sum(jnp.where(diagonal, column, 0.0), axis=0, keepdims=True)


def direct_finish_kernel(pixels, late, operator, early_gram, gram, lead, held, sem):
    own, size, days = operator.shape
    group = math.gcd(own, 4)
    copies = []
    for first in range(0, own, group):
        left = operator[first : first + group].reshape(group * size, days)
        half = lax.dot_general(
            left, late[...], (((1,), (0,)), ((), ())), preferred_element_type=jnp.float32
        ).astype(jnp.bfloat16)
        for f in range(group):
            mine = half[f * size : (f + 1) * size]
            weights = operator[first + f, :, days - BLOCK : days]
            value = both_ways(mine, weights)
            held[first + f] = (early_gram[first + f] + value) * (1.0 / pixels)
        chosen = pl.ds(first, group)
        copy = pltpu.make_async_copy(held.at[chosen], gram.at[chosen], sem.at[first // group])
        copy.start()
        copies.append(copy)
    lead[...] = leading(held[...], size)
    for copy in copies:
        copy.wait()


def direct_finish(late, operator, early_gram, pixels):
    own, size, days = operator.shape
    vmem = pl.BlockSpec(memory_space=pltpu.VMEM)
    gram, lead = pl.pallas_call(
        functools.partial(direct_finish_kernel, pixels),
        out_shape=(
            jax.ShapeDtypeStruct((own, size, size), jnp.float32),
            jax.ShapeDtypeStruct((1, own), jnp.float32),
        ),
        in_specs=[vmem] * 3,
        out_specs=(pl.BlockSpec(memory_space=pl.ANY), vmem),
        scratch_shapes=[
            pltpu.VMEM((own, size, size), jnp.float32),
            pltpu.SemaphoreType.DMA((own // math.gcd(own, 4),)),
        ],
        compiler_params=pltpu.CompilerParams(vmem_limit_bytes=24 * 2**20),
        name="finish",
    )(late, operator, early_gram)
    return gram, lead[0]


def shards(anomaly, offsets, taper_index):
    total_pixels = anomaly.shape[1] * lax.axis_size(("pix", "sub"))
    peers, sub = lax.axis_size("tm"), lax.axis_size("sub")
    if sub == 1 and peers == 8 and lax.axis_size("pix") == 2 and anomaly.shape == (64, 4 * sum(WIDTHS[0])):
        return direct_finish(*direct_covariance(anomaly, offsets, taper_index), total_pixels)
    covariance, operator, operator_low = covariance_and_operator(anomaly, offsets, taper_index)
    return gram_and_leading(covariance, operator, operator_low, total_pixels)


def solution(mesh):
    placed = (P("tm", ("group", "pix", "sub")), P(), P())
    return jax.shard_map(
        shards,
        mesh=mesh,
        in_specs=placed,
        out_specs=(P(("group", "tm"), None, None), P(("group", "tm"))),
        check_vma=False,
    )
```

```python
import functools
import math

import jax
import jax.numpy as jnp
from jax import lax
from jax.experimental import pallas as pl
from jax.experimental.pallas import tpu as pltpu
from jax.sharding import PartitionSpec as P

NFFT = 256
NB = 32
POWER = 8
NF = 128


power_eps = 1e-06


CHUNKS = 4


DIRECT_VMEM = 40 * 2**20
CUT = 12
WIDTHS = ((4096,), (3072, 1024))
INNER_ORDER = ((0, 1), (3, 0), (3, 1))
OUTER_ORDER = ((2, 0), (2, 1), (1, 0), (1, 1))
GATHER_ORDER = ((2, 1), (2, 0), (3, 1), (3, 0), (1, 1), (0, 1), (1, 0))


def windows_of(taper, step, length):
    steps = step.astype(jnp.float32)
    phase = steps * (2.0 * math.pi / length)
    center = (steps + 0.5) * (math.pi / length)
    sine_win = jnp.sin(center)
    hann = sine_win * sine_win
    hamming = 0.54 - 0.46 * jnp.cos(phase)
    blackman = 0.42 - 0.5 * jnp.cos(phase) + 0.08 * jnp.cos(2.0 * phase)
    chosen = jnp.where(
        taper == 0, hann, jnp.where(taper == 1, hamming, jnp.where(taper == 2, blackman, sine_win))
    )
    return jnp.where((step >= 0) & (step < length), chosen, 0.0)


def upright(row):
    square = (NB, NB)
    diagonal = lax.broadcasted_iota(jnp.int32, square, 0) == lax.broadcasted_iota(jnp.int32, square, 1)
    values = jnp.broadcast_to(row[...].astype(jnp.float32), square)
    return jnp.sum(jnp.where(diagonal, values, 0.0), axis=1, keepdims=True).astype(jnp.int32)


def split(value):
    high = value.astype(jnp.bfloat16)
    return high, (value - high.astype(jnp.float32)).astype(jnp.bfloat16)


def write_operator(offsets, taper, operator, operator_low):
    own, _, days = operator.shape
    step = lax.broadcasted_iota(jnp.int32, (NB, days), 1) - upright(offsets)
    windows = windows_of(jnp.broadcast_to(upright(taper), (NB, days)), step, NFFT)
    scaled = windows * (1.0 / jnp.sqrt(jnp.sum(windows * windows, axis=1, keepdims=True)))
    first = lax.axis_index("tm") * own

    def one(f, carry):
        angle = (((first + f) * step) & (NFFT - 1)).astype(jnp.float32) * (2.0 * math.pi / NFFT)
        for rows, table in ((pl.ds(0, NB), jnp.cos(angle)), (pl.ds(NB, NB), -jnp.sin(angle))):
            high, low = split(table.astype(jnp.bfloat16).astype(jnp.float32) * scaled)
            operator[f, rows, :] = high
            operator_low[f, rows, :] = low
        return carry

    lax.fori_loop(0, own, one, 0)


BLOCK = 128
MESH = pl.DeviceIdType.MESH


def stages_of(tm, pix, sub):
    if sub > 1 or tm % 2:
        split = [("sub", 1, sub), ("pix", 1, pix), ("tm", 1, tm)]
    else:
        split = [("tm", 1, 2), ("pix", 1, pix), ("tm", 2, tm // 2)]
    return split


def place_in(stage):
    axis, inner, members = stage
    return lax.rem(lax.axis_index(axis) // inner, members)


def device_at(stage, shift):
    axis, inner, members = stage
    index = lax.axis_index(axis)
    here = place_in(stage)
    there = lax.rem(here + shift, members)
    return {axis: index + (there - here) * inner}, there


def add_products(series, packed, first):
    blocks = series.shape[0] // BLOCK
    place = 0
    for i in range(blocks):
        strip = lax.dot_general(
            series[i * BLOCK : (i + 1) * BLOCK, :],
            series[i * BLOCK :, :],
            (((1,), (1,)), ((), ())),
            preferred_element_type=jnp.float32,
        )
        for j in range(blocks - i):
            rows = pl.ds((place + j) * BLOCK, BLOCK)
            block = strip[:, j * BLOCK : (j + 1) * BLOCK]
            packed[rows, :] = block if first else packed[rows, :] + block
        place += blocks - i


def covariance_kernel(
    stages, anomaly, offsets, taper, out, operator, operator_low, series, packed, gathered, own_sem, *scratch
):
    exchange_send, exchange_recv = scratch[:2]
    landing, sems = scratch[2:5], scratch[5:]
    chunks, days, width = series.shape
    per_device = anomaly.shape[0]
    peers = days // per_device
    me = lax.axis_index("tm")

    barrier = pltpu.get_barrier_semaphore()
    greeted = 0
    for axis in ("tm", "pix", "sub"):
        members = lax.axis_size(axis)
        for shift in range(1, members):
            device = {axis: lax.rem(lax.axis_index(axis) + shift, members)}
            pl.semaphore_signal(barrier, inc=1, device_id=device, device_id_type=MESH)
            greeted += 1
    my_rows = pl.ds(pl.multiple_of(me * per_device, per_device), per_device)

    def columns(device, chunk):
        return pl.ds(pl.multiple_of(device * (chunks * width) + chunk * width, width), width)

    kept = []
    for chunk in range(chunks):
        copy = pltpu.make_async_copy(
            anomaly.at[:, columns(me, chunk)], series.at[chunk, my_rows, :], own_sem.at[chunk]
        )
        copy.start()
        kept.append(copy)
    pl.semaphore_wait(barrier, greeted)
    farthest_first = sorted(range(1, peers), key=lambda shift: abs(2 * shift - peers))
    exchanged = []
    for chunk in range(chunks):
        copies = []
        for shift in farthest_first:
            there = lax.rem(me + shift, peers)
            copy = pltpu.make_async_remote_copy(
                src_ref=anomaly.at[:, columns(there, chunk)],
                dst_ref=series.at[chunk, my_rows, :],
                send_sem=exchange_send.at[chunk, shift - 1],
                recv_sem=exchange_recv.at[chunk, shift - 1],
                device_id={"tm": there},
                device_id_type=MESH,
            )
            copy.start()
            copies.append(copy)
        exchanged.append(copies)

    write_operator(offsets, taper, operator, operator_low)
    blocks = days // BLOCK
    filled = blocks * (blocks + 1) // 2 * BLOCK
    if packed.shape[0] > filled:
        packed[filled:, :] = jnp.zeros((packed.shape[0] - filled, BLOCK), jnp.float32)
    for chunk in range(chunks):
        kept[chunk].wait()
        for copy in exchanged[chunk]:
            copy.wait()
        add_products(series.at[chunk], packed, chunk == 0)

    near, side, line = stages
    piece = packed.shape[0] // line[2]
    half = piece // near[2]
    part = half // side[2]

    def rows_of(at, n, s, rows):
        return pl.ds(pl.multiple_of(at * piece + n * half + s * part, 8), rows)

    def send(src, dst, sem, index, device):
        copy = pltpu.make_async_remote_copy(
            src_ref=src,
            dst_ref=dst,
            send_sem=sems[2 * sem].at[index],
            recv_sem=sems[2 * sem + 1].at[index],
            device_id=device,
            device_id_type=MESH,
        )
        copy.start()
        return copy

    my_near, my_side = place_in(near), place_in(side)
    order = list(range(1, line[2])) + [0]
    order.sort(key=lambda shift: abs(2 * shift - line[2]))
    targets = {shift: device_at(line, shift) for shift in order}

    near_copies, side_copies, line_copies = {}, {}, {}
    for shift in order:
        at = targets[shift][1]
        near_copies[shift] = []
        for k in range(1, near[2]):
            device, there = device_at(near, k)
            index = shift * (near[2] - 1) + k - 1
            src = packed.at[rows_of(at, there, 0, half), :]
            near_copies[shift].append(send(src, landing[0].at[index], 0, index, device))
    for shift in order:
        at = targets[shift][1]
        mine = packed.at[rows_of(at, my_near, 0, half), :]
        total = mine[...]
        for k, copy in enumerate(near_copies[shift]):
            copy.wait()
            total = total + landing[0][shift * (near[2] - 1) + k]
        mine[...] = total
        side_copies[shift] = []
        for k in range(1, side[2]):
            device, there = device_at(side, k)
            index = shift * (side[2] - 1) + k - 1
            src = packed.at[rows_of(at, my_near, there, part), :]
            side_copies[shift].append(send(src, landing[1].at[index], 1, index, device))
    for shift in order:
        device, at = targets[shift]
        mine = packed.at[rows_of(at, my_near, my_side, part), :]
        total = mine[...]
        for k, copy in enumerate(side_copies[shift]):
            copy.wait()
            total = total + landing[1][shift * (side[2] - 1) + k]
        mine[...] = total
        if shift:
            line_copies[shift] = send(mine, landing[2].at[shift - 1], 2, shift - 1, device)
    here = place_in(line)
    own = gathered.at[rows_of(here, my_near, my_side, part), :]
    total = packed[rows_of(here, my_near, my_side, part), :]
    for shift in order:
        if shift:
            line_copies[shift].wait()
            total = total + landing[2][shift - 1]
    own[...] = total

    arriving = {}
    for shift in order:
        if shift:
            arriving[shift] = send(own, own, 3, shift - 1, targets[shift][0])
    spread, near_spread = {}, []
    incoming = [0] + [shift for shift in order if shift]
    sources = {shift: lax.rem(here + line[2] - shift, line[2]) for shift in incoming}
    for shift in incoming:
        if shift:
            arriving[shift].wait()
        mine = gathered.at[rows_of(sources[shift], my_near, my_side, part), :]
        spread[shift] = [
            send(mine, mine, 4, shift * (side[2] - 1) + k - 1, device_at(side, k)[0])
            for k in range(1, side[2])
        ]
    for shift in incoming:
        for copy in spread[shift]:
            copy.wait()
        mine = gathered.at[rows_of(sources[shift], my_near, 0, half), :]
        near_spread += [
            send(mine, mine, 5, shift * (near[2] - 1) + k - 1, device_at(near, k)[0])
            for k in range(1, near[2])
        ]
    for copy in near_spread:
        copy.wait()

    place = 0
    for i in range(blocks):
        for j in range(i, blocks):
            block = gathered[pl.ds(place * BLOCK, BLOCK), :]
            out[pl.ds(i * BLOCK, BLOCK), pl.ds(j * BLOCK, BLOCK)] = block
            if j > i:
                out[pl.ds(j * BLOCK, BLOCK), pl.ds(i * BLOCK, BLOCK)] = block.T
            place += 1


def covariance_and_operator(anomaly, offsets, taper_index):
    per_device, pixels = anomaly.shape
    peers = lax.axis_size("tm")
    days = per_device * peers
    own = NF // peers
    stages = stages_of(peers, lax.axis_size("pix"), lax.axis_size("sub"))
    devices = math.prod(stage[2] for stage in stages)
    blocks = days // BLOCK
    rows = -(-(blocks * (blocks + 1) // 2 * BLOCK) // (8 * devices)) * 8 * devices
    near, side, line = (stage[2] for stage in stages)
    half = rows // line // near
    part = half // side
    slots = [max(1, count) for count in (line * (near - 1), line * (side - 1), line - 1)]
    landing = [
        pltpu.VMEM((count, depth, BLOCK), jnp.float32)
        for count, depth in zip(slots, (half, part, part))
    ]
    sems = [
        pltpu.SemaphoreType.DMA((slots[stage],)) for stage in (0, 1, 2, 2, 1, 0) for _ in range(2)
    ]
    words = rows * BLOCK * 2 + days * days + own * 2 * NB * days + days * (pixels // peers) // 2
    words += sum(count * depth * BLOCK for count, depth in zip(slots, (half, part, part)))
    vmem = pl.BlockSpec(memory_space=pltpu.VMEM)
    return pl.pallas_call(
        functools.partial(covariance_kernel, stages),
        out_shape=(
            jax.ShapeDtypeStruct((days, days), jnp.float32),
            jax.ShapeDtypeStruct((own, 2 * NB, days), jnp.bfloat16),
            jax.ShapeDtypeStruct((own, 2 * NB, days), jnp.bfloat16),
        ),
        in_specs=[pl.BlockSpec(memory_space=pltpu.HBM), vmem, vmem],
        out_specs=(vmem, vmem, vmem),
        scratch_shapes=[
            pltpu.VMEM((CHUNKS, days, pixels // peers // CHUNKS), jnp.bfloat16),
            pltpu.VMEM((rows, BLOCK), jnp.float32),
            pltpu.VMEM((rows, BLOCK), jnp.float32),
            pltpu.SemaphoreType.DMA((CHUNKS,)),
            pltpu.SemaphoreType.DMA((CHUNKS, peers - 1)),
            pltpu.SemaphoreType.DMA((CHUNKS, peers - 1)),
        ]
        + landing
        + sems,
        compiler_params=pltpu.CompilerParams(
            collective_id=0, has_side_effects=True, vmem_limit_bytes=4 * words + 8 * 2**20
        ),
        name="covariance",
    )(anomaly, offsets[None, :], taper_index[None, :])


def finish_kernel(pixels, covariance, operator, operator_low, gram, lead, high, low):
    own, size, days = operator.shape
    high[...], low[...] = split(covariance[...])
    group = math.gcd(own, 4)

    def product(left, right, contract):
        return lax.dot_general(
            left, right, (((1,), (contract,)), ((), ())), preferred_element_type=jnp.float32
        )

    for first in range(0, own, group):
        left = operator[first : first + group].reshape(group * size, days)
        left_low = operator_low[first : first + group].reshape(group * size, days)
        half = product(left, high[...], 0) + (
            product(left_low, high[...], 0) + product(left, low[...], 0)
        )
        half_high, half_low = split(half)
        for f in range(group):
            rows = slice(f * size, (f + 1) * size)
            right, right_low = operator[first + f], operator_low[first + f]
            value = product(half_high[rows], right, 1) + (
                product(half_low[rows], right, 1) + product(half_high[rows], right_low, 1)
            )
            gram[first + f] = value / pixels

    matrix = gram[...]
    vector = jnp.ones((own, 1, size), jnp.float32)
    for step in range(POWER + 1):
        across = 2 - step % 2
        applied = jnp.sum(matrix * vector, axis=across, keepdims=True)
        power = jnp.sum(applied * applied, axis=3 - across, keepdims=True) / size
        vector = applied / jnp.sqrt(power + power_eps)
    column = jnp.broadcast_to(jnp.sqrt(power)[:, 0, :], (own, own))
    square = (own, own)
    diagonal = lax.broadcasted_iota(jnp.int32, square, 0) == lax.broadcasted_iota(jnp.int32, square, 1)
    lead[...] = jnp.sum(jnp.where(diagonal, column, 0.0), axis=0, keepdims=True)


def gram_and_leading(covariance, operator, operator_low, pixels):
    own, size, days = operator.shape
    vmem = pl.BlockSpec(memory_space=pltpu.VMEM)
    gram, lead = pl.pallas_call(
        functools.partial(finish_kernel, pixels),
        out_shape=(
            jax.ShapeDtypeStruct((own, size, size), jnp.float32),
            jax.ShapeDtypeStruct((1, own), jnp.float32),
        ),
        in_specs=[vmem] * 3,
        out_specs=(vmem, vmem),
        scratch_shapes=[pltpu.VMEM((days, days), jnp.bfloat16)] * 2,
        compiler_params=pltpu.CompilerParams(
            vmem_limit_bytes=8 * days * days + 4 * own * size * days + 12 * 2**20
        ),
        name="finish",
    )(covariance, operator, operator_low)
    return gram, lead[0]


def row_scale(shape, axis):
    day = lax.broadcasted_iota(jnp.int32, shape, axis)
    return 1.0 + ((((day * day) * 40503) >> 4) & 1023).astype(jnp.float32) * (1.0 / 1024.0)


def write_scaled_operator(offsets, taper, operator):
    own, _, days = operator.shape
    step = days_of((NB, days), lax.axis_size("tm")) - upright(offsets)
    windows = windows_of(jnp.broadcast_to(upright(taper), (NB, days)), step, NFFT)
    scaled = windows * (1.0 / jnp.sqrt(jnp.sum(windows * windows, axis=1, keepdims=True)))
    scaled = scaled / row_scale((NB, days), 1)
    first = lax.axis_index("tm") * own

    def one(f, carry):
        angle = (((first + f) * step) & (NFFT - 1)).astype(jnp.float32) * (2.0 * math.pi / NFFT)
        for rows, table in ((pl.ds(0, NB), jnp.cos(angle)), (pl.ds(NB, NB), -jnp.sin(angle))):
            operator[f, rows, :] = (table.astype(jnp.bfloat16).astype(jnp.float32) * scaled).astype(jnp.bfloat16)
        return carry

    lax.fori_loop(0, own, one, 0)


def days_of(shape, peers):
    days = shape[1]
    rows = days // peers
    late = rows // 4
    early = rows - late
    place = lax.broadcasted_iota(jnp.int32, shape, 1)
    first = jnp.zeros(shape, jnp.int32)
    second = jnp.zeros(shape, jnp.int32)
    for device in range(1, peers):
        first = first + (place >= early * device).astype(jnp.int32)
        second = second + (place >= early * peers + late * device).astype(jnp.int32)
    return jnp.where(
        place < early * peers, place + late * first, place - early * peers + early + early * second
    )


def block_order(blocks):
    order = [(i, j) for j in range(blocks) for i in range(j + 1)]
    return order[: -blocks], order[-blocks:]


def write_scale(scale, blocks):
    column, row = row_scale((blocks * BLOCK, BLOCK), 0), row_scale((8, blocks * BLOCK), 1)[:1]
    early, late = block_order(blocks)
    for place, (i, j) in enumerate(early + late):
        block = column[i * BLOCK : (i + 1) * BLOCK, :] * row[:, j * BLOCK : (j + 1) * BLOCK]
        scale[pl.ds(place * BLOCK, BLOCK), :] = 0.5 * block if i == j else block


def write_early_gram(gathered, operator, gram, start, stop):
    own, size, days = operator.shape
    columns = days // BLOCK - 1
    group = math.gcd(own, 4)
    for first in range(start, stop, group):
        halves = []
        for j in range(columns):
            depth = (j + 1) * BLOCK
            left = operator[first : first + group, :, 0:depth].reshape(group * size, depth)
            stack = gathered[pl.ds(j * (j + 1) // 2 * BLOCK, depth), :]
            half = lax.dot_general(left, stack, (((1,), (0,)), ((), ())), preferred_element_type=jnp.float32)
            halves.append(half.astype(jnp.bfloat16))
        half = jnp.concatenate(halves, axis=1)
        for f in range(group):
            mine = half[f * size : (f + 1) * size]
            gram[first + f] = both_ways(mine, operator[first + f, :, 0 : columns * BLOCK])


def add_half(operator, late, place, result):
    own, size, _ = operator.shape
    group = math.gcd(own, 4)
    for first in range(0, own, group):
        left = operator[first : first + group, :, place].reshape(group * size, late.shape[0])
        half = lax.dot_general(left, late, (((1,), (0,)), ((), ())), preferred_element_type=jnp.float32)
        result[first * size : (first + group) * size, :] = half


def both_ways(half, weights):
    return lax.dot_general(
        jnp.concatenate([half, weights], axis=1),
        jnp.concatenate([weights, half], axis=1),
        (((1,), (1,)), ((), ())),
        preferred_element_type=jnp.float32,
    )


def add_column(series, packed, j, first):
    rows = series.at[0 : (j + 1) * BLOCK, :]
    block = lax.dot_general(
        rows[...], series[j * BLOCK : (j + 1) * BLOCK, :], (((1,), (1,)), ((), ())), preferred_element_type=jnp.float32
    )
    place = pl.ds(j * (j + 1) // 2 * BLOCK, (j + 1) * BLOCK)
    packed[place, :] = block if first else packed[place, :] + block


def direct_kernel(
    anomaly,
    offsets,
    taper,
    out,
    operator,
    early_gram,
    own_half,
    packed,
    scale,
    near_box,
    near_land,
    outbox,
    landing,
    gathered,
    small,
    own_sem,
    small_sem,
    exchange_send,
    exchange_recv,
    near_send,
    near_recv,
    part_send,
    part_recv,
    whole_send,
    whole_recv,
    pass_send,
    pass_recv,
    late_box,
    late_land,
    late_send,
    late_recv,
    series,
):
    per_device, pixels = anomaly.shape
    days = series.shape[0]
    peers, across = lax.axis_size("tm"), lax.axis_size("pix")
    chips = peers // 2
    holders = chips
    span = pixels // holders
    me, side = lax.axis_index("tm"), lax.axis_index("pix")
    core, chip = lax.rem(me, 2), lax.div(me, 2)
    inner = lax.div(lax.rem(chip, chips - 1) + 1, 2)
    at = [chip, chip + 1 - 2 * lax.rem(chip, 2), lax.rem(chip + 2, chips), chips - 1 - chip]
    neighbour = {"tm": me + 1 - 2 * core}

    barrier = pltpu.get_barrier_semaphore()
    greeted = 0
    for axis, place, members in (("tm", me, peers), ("pix", side, across)):
        for shift in range(1, members):
            device = {axis: lax.rem(place + shift, members)}
            pl.semaphore_signal(barrier, inc=1, device_id=device, device_id_type=MESH)
            greeted += 1
    blocks = days // BLOCK
    early, late = block_order(blocks)
    base = (0, len(early) * BLOCK)
    half = (len(early) * BLOCK // 2, len(late) * BLOCK // 2)
    part = tuple(each // (2 * across) for each in half)
    late_rows = per_device // 4
    early_rows = per_device - late_rows
    sources = (pl.ds(0, early_rows), pl.ds(early_rows, late_rows))
    my_rows = (
        pl.ds(pl.multiple_of(me * early_rows, 16), early_rows),
        pl.ds(pl.multiple_of(early_rows * peers + me * late_rows, 16), late_rows),
    )
    chunks = [range(len(widths)) for widths in WIDTHS]

    def span_of(group, chunk):
        return pl.ds(sum(WIDTHS[group][:chunk]), WIDTHS[group][chunk])

    def columns(z, c, group, chunk):
        start = (2 * (z - 1) + c) * span + sum(WIDTHS[group][:chunk])
        return pl.ds(pl.multiple_of(start, BLOCK), WIDTHS[group][chunk])

    def send(src, dst, sends, receives, index, device):
        return pltpu.make_async_remote_copy(
            src_ref=src,
            dst_ref=dst,
            send_sem=sends.at[index],
            recv_sem=receives.at[index],
            device_id=device,
            device_id_type=MESH,
        )

    def exchange(group, chunk, z, c):
        there = 1 - core if c else core
        return send(
            anomaly.at[sources[group], columns(at[z], there, group, chunk)],
            series.at[my_rows[group], span_of(group, chunk)],
            exchange_send,
            exchange_recv,
            (group, chunk, 2 * z + c),
            {"tm": 2 * at[z] + there},
        )

    def arrival(group, chunk, z, c):
        mine = series.at[my_rows[group], span_of(group, chunk)]
        return send(mine, mine, exchange_send, exchange_recv, (group, chunk, 2 * z + c), neighbour)

    def keep(group, chunk):
        return pltpu.make_async_copy(
            anomaly.at[sources[group], columns(chip, core, group, chunk)],
            series.at[my_rows[group], span_of(group, chunk)],
            own_sem.at[group, chunk],
        )

    loads = [
        pltpu.make_async_copy(offsets, small.at[0:1, :], small_sem.at[0]),
        pltpu.make_async_copy(taper, small.at[8:9, :], small_sem.at[1]),
    ]
    for load in loads:
        load.start()
    pl.semaphore_wait(barrier, greeted)

    @pl.when(inner == 1)
    def _():
        for group in range(2):
            for chunk in chunks[group]:
                for z, c in INNER_ORDER:
                    exchange(group, chunk, z, c).start()
        for group in range(2):
            for chunk in chunks[group]:
                keep(group, chunk).start()

    @pl.when(inner == 0)
    def _():
        for group in range(2):
            for chunk in chunks[group]:
                for z, c in OUTER_ORDER:
                    exchange(group, chunk, z, c).start()

    for load in loads:
        load.wait()
    write_scaled_operator(small.at[0:1, :], small.at[8:9, :], operator)

    def half_of(group, n):
        return pl.ds(pl.multiple_of(base[group] + n * half[group], 16), half[group])

    def box(group):
        return pl.ds(base[group] // 2, half[group])

    def inside(group, z, x):
        return ((z - 1) * across + x) * part[group]

    def part_of(group, n, z, x):
        return pl.ds(pl.multiple_of(base[group] + n * half[group] + inside(group, z, x), 16), part[group])

    def landed(group, index):
        return landing.at[index, pl.ds(base[group] // (4 * across), part[group]), :]

    def beside(x):
        return 1 - side if x else side

    def device_of(z, x):
        return {"tm": 2 * at[z] + core, "pix": beside(x)}

    def own(group):
        return gathered.at[part_of(group, core, chip * inner + 1 - inner, side), :]

    def whole(group, z, x):
        mine = own(group)
        return send(mine, mine, whole_send, whole_recv, (group, 2 * z + x), device_of(z, x))

    def piece(group, z, x):
        return gathered.at[part_of(group, core, at[z], beside(x)), :]

    def gotten(group, z, x):
        mine = piece(group, z, x)
        return send(mine, mine, whole_send, whole_recv, (group, 2 * z + x), device_of(z, x))

    def passed(group, ref, index):
        return send(ref, ref, pass_send, pass_recv, (group, index), neighbour)

    def near(group):
        return send(near_box.at[box(group), :], near_land.at[box(group), :], near_send, near_recv, group, neighbour)

    others = ((3, 1), (3, 0), (0, 1))

    def portion(group, index):
        z, x = others[index]
        src = outbox.at[pl.ds(pl.multiple_of(base[group] // 2 + inside(group, at[z], beside(x)), 16), part[group]), :]
        return send(src, landed(group, index), part_send, part_recv, (group, index), device_of(z, x))

    def start_near(group):
        theirs = packed[half_of(group, 1 - core), :] * scale[half_of(group, 1 - core), :]
        near_box[box(group), :] = theirs.astype(jnp.bfloat16)
        near(group).start()
        mine = packed.at[half_of(group, core), :]
        mine[...] = mine[...] * scale[half_of(group, core), :]

    def start_scatter(group):
        near(group).wait()
        mine = packed.at[half_of(group, core), :]
        total = mine[...] + near_land[box(group), :].astype(jnp.float32)
        mine[...] = total
        outbox[box(group), :] = total.astype(jnp.bfloat16)
        for index in range(3):
            portion(group, index).start()

    everyone = ((3, 1, 0), (3, 1, 1), (3, 0, 0), (3, 0, 1), (0, 1, 0), (0, 1, 1), (0, 0, 1))

    def direct(index):
        z, x, c = everyone[index]
        there = 1 - core if c else core
        src = late_box.at[pl.ds(pl.multiple_of(there * half[1] + inside(1, at[z], beside(x)), 16), part[1]), :]
        device = {"tm": 2 * at[z] + there, "pix": beside(x)}
        return send(src, late_land.at[index], late_send, late_recv, index, device)

    def scatter_late():
        region = packed.at[base[1] : base[1] + 2 * half[1], :]
        final = span_of(1, len(WIDTHS[1]) - 1)
        last = lax.dot_general(
            series[:, final],
            series[days - BLOCK : days, final],
            (((1,), (1,)), ((), ())),
            preferred_element_type=jnp.float32,
        )
        total = (region[...] + last) * scale[base[1] : base[1] + 2 * half[1], :]
        region[...] = total
        late_box[...] = total.astype(jnp.bfloat16)
        for index in range(len(everyone)):
            direct(index).start()

    def start_gather(group):
        total = packed[part_of(group, core, chip, side), :]
        if group == 0:
            for index in range(3):
                portion(group, index).wait()
                total = total + landed(group, index)[...].astype(jnp.float32)
        else:
            for index in range(len(everyone)):
                direct(index).wait()
                total = total + late_land[index].astype(jnp.float32)
        mine = own(group)
        mine[...] = total.astype(jnp.bfloat16)
        for z, x in GATHER_ORDER:
            whole(group, z, x).start()
        passed(group, mine, 0).start()

    def pass_on(group, froms, first):
        for index, (z, x) in enumerate(froms):
            gotten(group, z, x).wait_recv()
            passed(group, piece(group, z, x), index + first).start()

    def end_pass(group, froms, first):
        if first:
            passed(group, own(group), 0).wait_recv()
        for index, (z, x) in enumerate(froms):
            passed(group, piece(group, z, x), index + first).wait()

    @pl.when(inner == 1)
    def _():
        write_scale(scale, blocks)
        froms = ((0, 1), (3, 0), (3, 1))
        for group in range(2):
            for chunk in chunks[group]:
                keep(group, chunk).wait()
                for z, c in ((0, 1), (1, 0), (1, 1), (3, 0), (3, 1), (2, 0), (2, 1)):
                    arrival(group, chunk, z, c).wait_recv()
                for j in range(blocks - 1) if group == 0 else (blocks - 1,):
                    if group == 0 or chunk < len(WIDTHS[1]) - 1:
                        add_column(series.at[:, span_of(group, chunk)], packed, j, chunk == 0)
            if group == 0:
                start_near(0)
                start_scatter(0)
        scatter_late()
        start_gather(0)
        start_gather(1)
        pass_on(0, froms, 1)
        end_pass(0, froms, 1)

    @pl.when(inner == 0)
    def _():
        for group in range(2):
            for chunk in chunks[group]:
                for z, c in OUTER_ORDER:
                    exchange(group, chunk, z, c).wait_send()
        pass_on(0, ((1, 0), (1, 1), (2, 0), (2, 1)), 0)
        end_pass(0, ((1, 0), (1, 1), (2, 0), (2, 1)), 0)

    own_count = operator.shape[0]
    write_early_gram(gathered, operator, early_gram, 0, CUT)

    @pl.when(inner == 1)
    def _():
        pass_on(1, ((0, 1), (3, 0), (3, 1)), 1)

    @pl.when(inner == 0)
    def _():
        pass_on(1, ((1, 0), (1, 1), (2, 0), (2, 1)), 0)

    mine = pl.ds(pl.multiple_of(core * half[1], BLOCK), half[1])
    add_half(operator, gathered[half_of(1, core), :], mine, own_half)
    write_early_gram(gathered, operator, early_gram, CUT, own_count)

    @pl.when(inner == 1)
    def _():
        end_pass(1, ((0, 1), (3, 0), (3, 1)), 1)
        for group in range(2):
            for chunk in chunks[group]:
                for z, c in INNER_ORDER:
                    exchange(group, chunk, z, c).wait_send()
            for z, x in GATHER_ORDER:
                whole(group, z, x).wait_send()
            passed(group, own(group), 0).wait_send()

    @pl.when(inner == 0)
    def _():
        end_pass(1, ((1, 0), (1, 1), (2, 0), (2, 1)), 0)

    out[...] = gathered[base[1] : base[1] + days, :]


def direct_covariance(anomaly, offsets, taper_index):
    per_device, pixels = anomaly.shape
    peers, across = lax.axis_size("tm"), lax.axis_size("pix")
    days = per_device * peers
    own = NF // peers
    blocks = days // BLOCK
    owners = 4 * across
    rows = -(-(blocks * (blocks + 1) // 2 * BLOCK) // (16 * owners)) * 16 * owners
    half, part = rows // 2, rows // owners
    others = owners // 2 - 1
    vmem = pl.BlockSpec(memory_space=pltpu.VMEM)
    hbm = pl.BlockSpec(memory_space=pl.ANY)
    counts = [(2,), (2, others), (2, peers), (2, others + 1)]
    return pl.pallas_call(
        direct_kernel,
        out_shape=(
            jax.ShapeDtypeStruct((days, BLOCK), jnp.bfloat16),
            jax.ShapeDtypeStruct((own, 2 * NB, days), jnp.bfloat16),
            jax.ShapeDtypeStruct((own, 2 * NB, 2 * NB), jnp.float32),
            jax.ShapeDtypeStruct((own * 2 * NB, BLOCK), jnp.float32),
        ),
        in_specs=[hbm, hbm, hbm],
        out_specs=(vmem, vmem, vmem, vmem),
        scratch_shapes=[
            pltpu.VMEM((rows, BLOCK), jnp.float32),
            pltpu.VMEM((rows, BLOCK), jnp.float32),
            pltpu.VMEM((half, BLOCK), jnp.bfloat16),
            pltpu.VMEM((half, BLOCK), jnp.bfloat16),
            pltpu.VMEM((half, BLOCK), jnp.bfloat16),
            pltpu.VMEM((others, part, BLOCK), jnp.bfloat16),
            pltpu.VMEM((rows, BLOCK), jnp.bfloat16),
            pltpu.VMEM((16, NB), jnp.int32),
            pltpu.SemaphoreType.DMA((2, max(map(len, WIDTHS)))),
            pltpu.SemaphoreType.DMA((2,)),
            pltpu.SemaphoreType.DMA((2, max(map(len, WIDTHS)), peers)),
            pltpu.SemaphoreType.DMA((2, max(map(len, WIDTHS)), peers)),
        ]
        + [pltpu.SemaphoreType.DMA(count) for count in counts for _ in range(2)]
        + [
            pltpu.VMEM((days, BLOCK), jnp.bfloat16),
            pltpu.VMEM((owners - 1, days // owners, BLOCK), jnp.bfloat16),
            pltpu.SemaphoreType.DMA((owners - 1,)),
            pltpu.SemaphoreType.DMA((owners - 1,)),
        ]
        + [pltpu.VMEM((days, sum(WIDTHS[0])), jnp.bfloat16)],
        compiler_params=pltpu.CompilerParams(
            collective_id=0, has_side_effects=True, vmem_limit_bytes=DIRECT_VMEM
        ),
        name="covariance",
    )(*(pltpu.with_memory_space_constraint(each, pltpu.HBM) for each in (anomaly, offsets[None, :], taper_index[None, :])))


def leading(matrix, size):
    own = matrix.shape[0]
    vector = jnp.ones((own, 1, size), jnp.float32)
    for step in range(POWER + 1):
        across = 2 - step % 2
        applied = jnp.sum(matrix * vector, axis=across, keepdims=True)
        power = jnp.sum(applied * applied, axis=3 - across, keepdims=True) / size
        vector = applied * lax.rsqrt(power + power_eps)
    column = jnp.broadcast_to(jnp.sqrt(power)[:, 0, :], (own, own))
    square = (own, own)
    diagonal = lax.broadcasted_iota(jnp.int32, square, 0) == lax.broadcasted_iota(jnp.int32, square, 1)
    return jnp.sum(jnp.where(diagonal, column, 0.0), axis=0, keepdims=True)


def direct_finish_kernel(pixels, late, operator, early_gram, own_half, gram, lead, held, sem):
    own, size, days = operator.shape
    other = pl.ds(pl.multiple_of((1 - lax.rem(lax.axis_index("tm"), 2)) * (days // 2), BLOCK), days // 2)
    group = math.gcd(own, 4)
    copies = []
    for first in range(0, own, group):
        left = operator[first : first + group, :, other].reshape(group * size, days // 2)
        half = lax.dot_general(left, late[other, :], (((1,), (0,)), ((), ())), preferred_element_type=jnp.float32)
        half = (half + own_half[first * size : (first + group) * size, :]).astype(jnp.bfloat16)
        for f in range(group):
            mine = half[f * size : (f + 1) * size]
            weights = operator[first + f, :, days - BLOCK : days]
            value = both_ways(mine, weights)
            held[first + f] = (early_gram[first + f] + value) * (1.0 / pixels)
        chosen = pl.ds(first, group)
        copy = pltpu.make_async_copy(held.at[chosen], gram.at[chosen], sem.at[first // group])
        copy.start()
        copies.append(copy)
    lead[...] = leading(held[...], size)
    for copy in copies:
        copy.wait()


def direct_finish(late, operator, early_gram, own_half, pixels):
    own, size, days = operator.shape
    vmem = pl.BlockSpec(memory_space=pltpu.VMEM)
    gram, lead = pl.pallas_call(
        functools.partial(direct_finish_kernel, pixels),
        out_shape=(
            jax.ShapeDtypeStruct((own, size, size), jnp.float32),
            jax.ShapeDtypeStruct((1, own), jnp.float32),
        ),
        in_specs=[vmem] * 4,
        out_specs=(pl.BlockSpec(memory_space=pl.ANY), vmem),
        scratch_shapes=[
            pltpu.VMEM((own, size, size), jnp.float32),
            pltpu.SemaphoreType.DMA((own // math.gcd(own, 4),)),
        ],
        compiler_params=pltpu.CompilerParams(vmem_limit_bytes=24 * 2**20),
        name="finish",
    )(late, operator, early_gram, own_half)
    return gram, lead[0]


def shards(anomaly, offsets, taper_index):
    total_pixels = anomaly.shape[1] * lax.axis_size(("pix", "sub"))
    peers, sub = lax.axis_size("tm"), lax.axis_size("sub")
    if sub == 1 and peers == 8 and lax.axis_size("pix") == 2 and anomaly.shape == (64, 4 * sum(WIDTHS[0])):
        return direct_finish(*direct_covariance(anomaly, offsets, taper_index), total_pixels)
    covariance, operator, operator_low = covariance_and_operator(anomaly, offsets, taper_index)
    return gram_and_leading(covariance, operator, operator_low, total_pixels)


def solution(mesh):
    placed = (P("tm", ("group", "pix", "sub")), P(), P())
    return jax.shard_map(
        shards,
        mesh=mesh,
        in_specs=placed,
        out_specs=(P(("group", "tm"), None, None), P(("group", "tm"))),
        check_vma=False,
    )
```

```python
import functools
import math

import jax
import jax.numpy as jnp
from jax import lax
from jax.experimental import pallas as pl
from jax.experimental.pallas import tpu as pltpu
from jax.sharding import PartitionSpec as P

NFFT = 256
NB = 32
POWER = 8
NF = 128


power_eps = 1e-06


CHUNKS = 4


DIRECT_VMEM = 40 * 2**20
CUT = 12
WIDTHS = ((4096,), (3072, 1024))
INNER_ORDER = ((0, 1), (3, 0), (3, 1))
OUTER_ORDER = ((2, 0), (2, 1), (1, 0), (1, 1))
GATHER_ORDER = ((2, 1), (2, 0), (3, 1), (3, 0), (1, 1), (0, 1), (1, 0))


def windows_of(taper, step, length):
    steps = step.astype(jnp.float32)
    phase = steps * (2.0 * math.pi / length)
    center = (steps + 0.5) * (math.pi / length)
    sine_win = jnp.sin(center)
    hann = sine_win * sine_win
    hamming = 0.54 - 0.46 * jnp.cos(phase)
    blackman = 0.42 - 0.5 * jnp.cos(phase) + 0.08 * jnp.cos(2.0 * phase)
    chosen = jnp.where(
        taper == 0, hann, jnp.where(taper == 1, hamming, jnp.where(taper == 2, blackman, sine_win))
    )
    return jnp.where((step >= 0) & (step < length), chosen, 0.0)


def upright(row):
    square = (NB, NB)
    diagonal = lax.broadcasted_iota(jnp.int32, square, 0) == lax.broadcasted_iota(jnp.int32, square, 1)
    values = jnp.broadcast_to(row[...].astype(jnp.float32), square)
    return jnp.sum(jnp.where(diagonal, values, 0.0), axis=1, keepdims=True).astype(jnp.int32)


def split(value):
    high = value.astype(jnp.bfloat16)
    return high, (value - high.astype(jnp.float32)).astype(jnp.bfloat16)


def write_operator(offsets, taper, operator, operator_low):
    own, _, days = operator.shape
    step = lax.broadcasted_iota(jnp.int32, (NB, days), 1) - upright(offsets)
    windows = windows_of(jnp.broadcast_to(upright(taper), (NB, days)), step, NFFT)
    scaled = windows * (1.0 / jnp.sqrt(jnp.sum(windows * windows, axis=1, keepdims=True)))
    first = lax.axis_index("tm") * own

    def one(f, carry):
        angle = (((first + f) * step) & (NFFT - 1)).astype(jnp.float32) * (2.0 * math.pi / NFFT)
        for rows, table in ((pl.ds(0, NB), jnp.cos(angle)), (pl.ds(NB, NB), -jnp.sin(angle))):
            high, low = split(table.astype(jnp.bfloat16).astype(jnp.float32) * scaled)
            operator[f, rows, :] = high
            operator_low[f, rows, :] = low
        return carry

    lax.fori_loop(0, own, one, 0)


BLOCK = 128
MESH = pl.DeviceIdType.MESH


def stages_of(tm, pix, sub):
    if sub > 1 or tm % 2:
        split = [("sub", 1, sub), ("pix", 1, pix), ("tm", 1, tm)]
    else:
        split = [("tm", 1, 2), ("pix", 1, pix), ("tm", 2, tm // 2)]
    return split


def place_in(stage):
    axis, inner, members = stage
    return lax.rem(lax.axis_index(axis) // inner, members)


def device_at(stage, shift):
    axis, inner, members = stage
    index = lax.axis_index(axis)
    here = place_in(stage)
    there = lax.rem(here + shift, members)
    return {axis: index + (there - here) * inner}, there


def add_products(series, packed, first):
    blocks = series.shape[0] // BLOCK
    place = 0
    for i in range(blocks):
        strip = lax.dot_general(
            series[i * BLOCK : (i + 1) * BLOCK, :],
            series[i * BLOCK :, :],
            (((1,), (1,)), ((), ())),
            preferred_element_type=jnp.float32,
        )
        for j in range(blocks - i):
            rows = pl.ds((place + j) * BLOCK, BLOCK)
            block = strip[:, j * BLOCK : (j + 1) * BLOCK]
            packed[rows, :] = block if first else packed[rows, :] + block
        place += blocks - i


def covariance_kernel(
    stages, anomaly, offsets, taper, out, operator, operator_low, series, packed, gathered, own_sem, *scratch
):
    exchange_send, exchange_recv = scratch[:2]
    landing, sems = scratch[2:5], scratch[5:]
    chunks, days, width = series.shape
    per_device = anomaly.shape[0]
    peers = days // per_device
    me = lax.axis_index("tm")

    barrier = pltpu.get_barrier_semaphore()
    greeted = 0
    for axis in ("tm", "pix", "sub"):
        members = lax.axis_size(axis)
        for shift in range(1, members):
            device = {axis: lax.rem(lax.axis_index(axis) + shift, members)}
            pl.semaphore_signal(barrier, inc=1, device_id=device, device_id_type=MESH)
            greeted += 1
    my_rows = pl.ds(pl.multiple_of(me * per_device, per_device), per_device)

    def columns(device, chunk):
        return pl.ds(pl.multiple_of(device * (chunks * width) + chunk * width, width), width)

    kept = []
    for chunk in range(chunks):
        copy = pltpu.make_async_copy(
            anomaly.at[:, columns(me, chunk)], series.at[chunk, my_rows, :], own_sem.at[chunk]
        )
        copy.start()
        kept.append(copy)
    pl.semaphore_wait(barrier, greeted)
    farthest_first = sorted(range(1, peers), key=lambda shift: abs(2 * shift - peers))
    exchanged = []
    for chunk in range(chunks):
        copies = []
        for shift in farthest_first:
            there = lax.rem(me + shift, peers)
            copy = pltpu.make_async_remote_copy(
                src_ref=anomaly.at[:, columns(there, chunk)],
                dst_ref=series.at[chunk, my_rows, :],
                send_sem=exchange_send.at[chunk, shift - 1],
                recv_sem=exchange_recv.at[chunk, shift - 1],
                device_id={"tm": there},
                device_id_type=MESH,
            )
            copy.start()
            copies.append(copy)
        exchanged.append(copies)

    write_operator(offsets, taper, operator, operator_low)
    blocks = days // BLOCK
    filled = blocks * (blocks + 1) // 2 * BLOCK
    if packed.shape[0] > filled:
        packed[filled:, :] = jnp.zeros((packed.shape[0] - filled, BLOCK), jnp.float32)
    for chunk in range(chunks):
        kept[chunk].wait()
        for copy in exchanged[chunk]:
            copy.wait()
        add_products(series.at[chunk], packed, chunk == 0)

    near, side, line = stages
    piece = packed.shape[0] // line[2]
    half = piece // near[2]
    part = half // side[2]

    def rows_of(at, n, s, rows):
        return pl.ds(pl.multiple_of(at * piece + n * half + s * part, 8), rows)

    def send(src, dst, sem, index, device):
        copy = pltpu.make_async_remote_copy(
            src_ref=src,
            dst_ref=dst,
            send_sem=sems[2 * sem].at[index],
            recv_sem=sems[2 * sem + 1].at[index],
            device_id=device,
            device_id_type=MESH,
        )
        copy.start()
        return copy

    my_near, my_side = place_in(near), place_in(side)
    order = list(range(1, line[2])) + [0]
    order.sort(key=lambda shift: abs(2 * shift - line[2]))
    targets = {shift: device_at(line, shift) for shift in order}

    near_copies, side_copies, line_copies = {}, {}, {}
    for shift in order:
        at = targets[shift][1]
        near_copies[shift] = []
        for k in range(1, near[2]):
            device, there = device_at(near, k)
            index = shift * (near[2] - 1) + k - 1
            src = packed.at[rows_of(at, there, 0, half), :]
            near_copies[shift].append(send(src, landing[0].at[index], 0, index, device))
    for shift in order:
        at = targets[shift][1]
        mine = packed.at[rows_of(at, my_near, 0, half), :]
        total = mine[...]
        for k, copy in enumerate(near_copies[shift]):
            copy.wait()
            total = total + landing[0][shift * (near[2] - 1) + k]
        mine[...] = total
        side_copies[shift] = []
        for k in range(1, side[2]):
            device, there = device_at(side, k)
            index = shift * (side[2] - 1) + k - 1
            src = packed.at[rows_of(at, my_near, there, part), :]
            side_copies[shift].append(send(src, landing[1].at[index], 1, index, device))
    for shift in order:
        device, at = targets[shift]
        mine = packed.at[rows_of(at, my_near, my_side, part), :]
        total = mine[...]
        for k, copy in enumerate(side_copies[shift]):
            copy.wait()
            total = total + landing[1][shift * (side[2] - 1) + k]
        mine[...] = total
        if shift:
            line_copies[shift] = send(mine, landing[2].at[shift - 1], 2, shift - 1, device)
    here = place_in(line)
    own = gathered.at[rows_of(here, my_near, my_side, part), :]
    total = packed[rows_of(here, my_near, my_side, part), :]
    for shift in order:
        if shift:
            line_copies[shift].wait()
            total = total + landing[2][shift - 1]
    own[...] = total

    arriving = {}
    for shift in order:
        if shift:
            arriving[shift] = send(own, own, 3, shift - 1, targets[shift][0])
    spread, near_spread = {}, []
    incoming = [0] + [shift for shift in order if shift]
    sources = {shift: lax.rem(here + line[2] - shift, line[2]) for shift in incoming}
    for shift in incoming:
        if shift:
            arriving[shift].wait()
        mine = gathered.at[rows_of(sources[shift], my_near, my_side, part), :]
        spread[shift] = [
            send(mine, mine, 4, shift * (side[2] - 1) + k - 1, device_at(side, k)[0])
            for k in range(1, side[2])
        ]
    for shift in incoming:
        for copy in spread[shift]:
            copy.wait()
        mine = gathered.at[rows_of(sources[shift], my_near, 0, half), :]
        near_spread += [
            send(mine, mine, 5, shift * (near[2] - 1) + k - 1, device_at(near, k)[0])
            for k in range(1, near[2])
        ]
    for copy in near_spread:
        copy.wait()

    place = 0
    for i in range(blocks):
        for j in range(i, blocks):
            block = gathered[pl.ds(place * BLOCK, BLOCK), :]
            out[pl.ds(i * BLOCK, BLOCK), pl.ds(j * BLOCK, BLOCK)] = block
            if j > i:
                out[pl.ds(j * BLOCK, BLOCK), pl.ds(i * BLOCK, BLOCK)] = block.T
            place += 1


def covariance_and_operator(anomaly, offsets, taper_index):
    per_device, pixels = anomaly.shape
    peers = lax.axis_size("tm")
    days = per_device * peers
    own = NF // peers
    stages = stages_of(peers, lax.axis_size("pix"), lax.axis_size("sub"))
    devices = math.prod(stage[2] for stage in stages)
    blocks = days // BLOCK
    rows = -(-(blocks * (blocks + 1) // 2 * BLOCK) // (8 * devices)) * 8 * devices
    near, side, line = (stage[2] for stage in stages)
    half = rows // line // near
    part = half // side
    slots = [max(1, count) for count in (line * (near - 1), line * (side - 1), line - 1)]
    landing = [
        pltpu.VMEM((count, depth, BLOCK), jnp.float32)
        for count, depth in zip(slots, (half, part, part))
    ]
    sems = [
        pltpu.SemaphoreType.DMA((slots[stage],)) for stage in (0, 1, 2, 2, 1, 0) for _ in range(2)
    ]
    words = rows * BLOCK * 2 + days * days + own * 2 * NB * days + days * (pixels // peers) // 2
    words += sum(count * depth * BLOCK for count, depth in zip(slots, (half, part, part)))
    vmem = pl.BlockSpec(memory_space=pltpu.VMEM)
    return pl.pallas_call(
        functools.partial(covariance_kernel, stages),
        out_shape=(
            jax.ShapeDtypeStruct((days, days), jnp.float32),
            jax.ShapeDtypeStruct((own, 2 * NB, days), jnp.bfloat16),
            jax.ShapeDtypeStruct((own, 2 * NB, days), jnp.bfloat16),
        ),
        in_specs=[pl.BlockSpec(memory_space=pltpu.HBM), vmem, vmem],
        out_specs=(vmem, vmem, vmem),
        scratch_shapes=[
            pltpu.VMEM((CHUNKS, days, pixels // peers // CHUNKS), jnp.bfloat16),
            pltpu.VMEM((rows, BLOCK), jnp.float32),
            pltpu.VMEM((rows, BLOCK), jnp.float32),
            pltpu.SemaphoreType.DMA((CHUNKS,)),
            pltpu.SemaphoreType.DMA((CHUNKS, peers - 1)),
            pltpu.SemaphoreType.DMA((CHUNKS, peers - 1)),
        ]
        + landing
        + sems,
        compiler_params=pltpu.CompilerParams(
            collective_id=0, has_side_effects=True, vmem_limit_bytes=4 * words + 8 * 2**20
        ),
        name="covariance",
    )(anomaly, offsets[None, :], taper_index[None, :])


def finish_kernel(pixels, covariance, operator, operator_low, gram, lead, high, low):
    own, size, days = operator.shape
    high[...], low[...] = split(covariance[...])
    group = math.gcd(own, 4)

    def product(left, right, contract):
        return lax.dot_general(
            left, right, (((1,), (contract,)), ((), ())), preferred_element_type=jnp.float32
        )

    for first in range(0, own, group):
        left = operator[first : first + group].reshape(group * size, days)
        left_low = operator_low[first : first + group].reshape(group * size, days)
        half = product(left, high[...], 0) + (
            product(left_low, high[...], 0) + product(left, low[...], 0)
        )
        half_high, half_low = split(half)
        for f in range(group):
            rows = slice(f * size, (f + 1) * size)
            right, right_low = operator[first + f], operator_low[first + f]
            value = product(half_high[rows], right, 1) + (
                product(half_low[rows], right, 1) + product(half_high[rows], right_low, 1)
            )
            gram[first + f] = value / pixels

    matrix = gram[...]
    vector = jnp.ones((own, 1, size), jnp.float32)
    for step in range(POWER + 1):
        across = 2 - step % 2
        applied = jnp.sum(matrix * vector, axis=across, keepdims=True)
        power = jnp.sum(applied * applied, axis=3 - across, keepdims=True) / size
        vector = applied / jnp.sqrt(power + power_eps)
    column = jnp.broadcast_to(jnp.sqrt(power)[:, 0, :], (own, own))
    square = (own, own)
    diagonal = lax.broadcasted_iota(jnp.int32, square, 0) == lax.broadcasted_iota(jnp.int32, square, 1)
    lead[...] = jnp.sum(jnp.where(diagonal, column, 0.0), axis=0, keepdims=True)


def gram_and_leading(covariance, operator, operator_low, pixels):
    own, size, days = operator.shape
    vmem = pl.BlockSpec(memory_space=pltpu.VMEM)
    gram, lead = pl.pallas_call(
        functools.partial(finish_kernel, pixels),
        out_shape=(
            jax.ShapeDtypeStruct((own, size, size), jnp.float32),
            jax.ShapeDtypeStruct((1, own), jnp.float32),
        ),
        in_specs=[vmem] * 3,
        out_specs=(vmem, vmem),
        scratch_shapes=[pltpu.VMEM((days, days), jnp.bfloat16)] * 2,
        compiler_params=pltpu.CompilerParams(
            vmem_limit_bytes=8 * days * days + 4 * own * size * days + 12 * 2**20
        ),
        name="finish",
    )(covariance, operator, operator_low)
    return gram, lead[0]


def row_scale(shape, axis):
    day = lax.broadcasted_iota(jnp.int32, shape, axis)
    return 1.0 + ((((day * day) * 40503) >> 4) & 1023).astype(jnp.float32) * (1.0 / 1024.0)


def write_scaled_operator(offsets, taper, operator):
    own, _, days = operator.shape
    step = days_of((NB, days), lax.axis_size("tm")) - upright(offsets)
    windows = windows_of(jnp.broadcast_to(upright(taper), (NB, days)), step, NFFT)
    scaled = windows * (1.0 / jnp.sqrt(jnp.sum(windows * windows, axis=1, keepdims=True)))
    scaled = scaled / row_scale((NB, days), 1)
    first = lax.axis_index("tm") * own

    def one(f, carry):
        angle = (((first + f) * step) & (NFFT - 1)).astype(jnp.float32) * (2.0 * math.pi / NFFT)
        for rows, table in ((pl.ds(0, NB), jnp.cos(angle)), (pl.ds(NB, NB), -jnp.sin(angle))):
            operator[f, rows, :] = (table.astype(jnp.bfloat16).astype(jnp.float32) * scaled).astype(jnp.bfloat16)
        return carry

    lax.fori_loop(0, own, one, 0)


def days_of(shape, peers):
    days = shape[1]
    rows = days // peers
    late = rows // 4
    early = rows - late
    place = lax.broadcasted_iota(jnp.int32, shape, 1)
    first = jnp.zeros(shape, jnp.int32)
    second = jnp.zeros(shape, jnp.int32)
    for device in range(1, peers):
        first = first + (place >= early * device).astype(jnp.int32)
        second = second + (place >= early * peers + late * device).astype(jnp.int32)
    return jnp.where(
        place < early * peers, place + late * first, place - early * peers + early + early * second
    )


def block_order(blocks):
    order = [(i, j) for j in range(blocks) for i in range(j + 1)]
    return order[: -blocks], order[-blocks:]


def write_scale(scale, blocks):
    column, row = row_scale((blocks * BLOCK, BLOCK), 0), row_scale((8, blocks * BLOCK), 1)[:1]
    early, late = block_order(blocks)
    for place, (i, j) in enumerate(early + late):
        block = column[i * BLOCK : (i + 1) * BLOCK, :] * row[:, j * BLOCK : (j + 1) * BLOCK]
        scale[pl.ds(place * BLOCK, BLOCK), :] = 0.5 * block if i == j else block


def write_early_gram(gathered, operator, gram, start, stop):
    own, size, days = operator.shape
    columns = days // BLOCK - 1
    group = math.gcd(own, 4)
    for first in range(start, stop, group):
        halves = []
        for j in range(columns):
            depth = (j + 1) * BLOCK
            left = operator[first : first + group, :, 0:depth].reshape(group * size, depth)
            stack = gathered[pl.ds(j * (j + 1) // 2 * BLOCK, depth), :]
            half = lax.dot_general(left, stack, (((1,), (0,)), ((), ())), preferred_element_type=jnp.float32)
            halves.append(half.astype(jnp.bfloat16))
        half = jnp.concatenate(halves, axis=1)
        for f in range(group):
            mine = half[f * size : (f + 1) * size]
            gram[first + f] = both_ways(mine, operator[first + f, :, 0 : columns * BLOCK])


def add_half(operator, late, place, result):
    own, size, _ = operator.shape
    group = math.gcd(own, 4)
    for first in range(0, own, group):
        left = operator[first : first + group, :, place].reshape(group * size, late.shape[0])
        half = lax.dot_general(left, late, (((1,), (0,)), ((), ())), preferred_element_type=jnp.float32)
        result[first * size : (first + group) * size, :] = half


def both_ways(half, weights):
    return lax.dot_general(
        jnp.concatenate([half, weights], axis=1),
        jnp.concatenate([weights, half], axis=1),
        (((1,), (1,)), ((), ())),
        preferred_element_type=jnp.float32,
    )


def add_column(series, packed, j, first):
    rows = series.at[0 : (j + 1) * BLOCK, :]
    block = lax.dot_general(
        rows[...], series[j * BLOCK : (j + 1) * BLOCK, :], (((1,), (1,)), ((), ())), preferred_element_type=jnp.float32
    )
    place = pl.ds(j * (j + 1) // 2 * BLOCK, (j + 1) * BLOCK)
    packed[place, :] = block if first else packed[place, :] + block


def direct_kernel(
    anomaly,
    offsets,
    taper,
    out,
    operator,
    early_gram,
    own_half,
    packed,
    scale,
    near_box,
    near_land,
    outbox,
    landing,
    gathered,
    small,
    own_sem,
    small_sem,
    exchange_send,
    exchange_recv,
    near_send,
    near_recv,
    part_send,
    part_recv,
    whole_send,
    whole_recv,
    pass_send,
    pass_recv,
    late_box,
    late_land,
    late_send,
    late_recv,
    series,
):
    per_device, pixels = anomaly.shape
    days = series.shape[0]
    peers, across = lax.axis_size("tm"), lax.axis_size("pix")
    chips = peers // 2
    holders = chips
    span = pixels // holders
    me, side = lax.axis_index("tm"), lax.axis_index("pix")
    core, chip = lax.rem(me, 2), lax.div(me, 2)
    inner = lax.div(lax.rem(chip, chips - 1) + 1, 2)
    at = [chip, chip + 1 - 2 * lax.rem(chip, 2), lax.rem(chip + 2, chips), chips - 1 - chip]
    neighbour = {"tm": me + 1 - 2 * core}

    barrier = pltpu.get_barrier_semaphore()
    greeted = 0
    for axis, place, members in (("tm", me, peers), ("pix", side, across)):
        for shift in range(1, members):
            device = {axis: lax.rem(place + shift, members)}
            pl.semaphore_signal(barrier, inc=1, device_id=device, device_id_type=MESH)
            greeted += 1
    blocks = days // BLOCK
    early, late = block_order(blocks)
    base = (0, len(early) * BLOCK)
    half = (len(early) * BLOCK // 2, len(late) * BLOCK // 2)
    part = tuple(each // (2 * across) for each in half)
    late_rows = per_device // 4
    early_rows = per_device - late_rows
    sources = (pl.ds(0, early_rows), pl.ds(early_rows, late_rows))
    my_rows = (
        pl.ds(pl.multiple_of(me * early_rows, 16), early_rows),
        pl.ds(pl.multiple_of(early_rows * peers + me * late_rows, 16), late_rows),
    )
    chunks = [range(len(widths)) for widths in WIDTHS]

    def span_of(group, chunk):
        return pl.ds(sum(WIDTHS[group][:chunk]), WIDTHS[group][chunk])

    def columns(z, c, group, chunk):
        start = (2 * (z - 1) + c) * span + sum(WIDTHS[group][:chunk])
        return pl.ds(pl.multiple_of(start, BLOCK), WIDTHS[group][chunk])

    def send(src, dst, sends, receives, index, device):
        return pltpu.make_async_remote_copy(
            src_ref=src,
            dst_ref=dst,
            send_sem=sends.at[index],
            recv_sem=receives.at[index],
            device_id=device,
            device_id_type=MESH,
        )

    def exchange(group, chunk, z, c):
        there = 1 - core if c else core
        return send(
            anomaly.at[sources[group], columns(at[z], there, group, chunk)],
            series.at[my_rows[group], span_of(group, chunk)],
            exchange_send,
            exchange_recv,
            (group, chunk, 2 * z + c),
            {"tm": 2 * at[z] + there},
        )

    def arrival(group, chunk, z, c):
        mine = series.at[my_rows[group], span_of(group, chunk)]
        return send(mine, mine, exchange_send, exchange_recv, (group, chunk, 2 * z + c), neighbour)

    def keep(group, chunk):
        return pltpu.make_async_copy(
            anomaly.at[sources[group], columns(chip, core, group, chunk)],
            series.at[my_rows[group], span_of(group, chunk)],
            own_sem.at[group, chunk],
        )

    loads = [
        pltpu.make_async_copy(offsets, small.at[0:1, :], small_sem.at[0]),
        pltpu.make_async_copy(taper, small.at[8:9, :], small_sem.at[1]),
    ]
    for load in loads:
        load.start()
    pl.semaphore_wait(barrier, greeted)

    @pl.when(inner == 1)
    def _():
        for group in range(2):
            for chunk in chunks[group]:
                for z, c in INNER_ORDER:
                    exchange(group, chunk, z, c).start()
        for group in range(2):
            for chunk in chunks[group]:
                keep(group, chunk).start()

    @pl.when(inner == 0)
    def _():
        for group in range(2):
            for chunk in chunks[group]:
                for z, c in OUTER_ORDER:
                    exchange(group, chunk, z, c).start()

    for load in loads:
        load.wait()
    write_scaled_operator(small.at[0:1, :], small.at[8:9, :], operator)

    def half_of(group, n):
        return pl.ds(pl.multiple_of(base[group] + n * half[group], 16), half[group])

    def box(group):
        return pl.ds(base[group] // 2, half[group])

    def inside(group, z, x):
        return ((z - 1) * across + x) * part[group]

    def part_of(group, n, z, x):
        return pl.ds(pl.multiple_of(base[group] + n * half[group] + inside(group, z, x), 16), part[group])

    def landed(group, index):
        return landing.at[index, pl.ds(base[group] // (4 * across), part[group]), :]

    def beside(x):
        return 1 - side if x else side

    def device_of(z, x):
        return {"tm": 2 * at[z] + core, "pix": beside(x)}

    def own(group):
        return gathered.at[part_of(group, core, chip * inner + 1 - inner, side), :]

    def whole(group, z, x):
        mine = own(group)
        return send(mine, mine, whole_send, whole_recv, (group, 2 * z + x), device_of(z, x))

    def piece(group, z, x):
        return gathered.at[part_of(group, core, at[z], beside(x)), :]

    def gotten(group, z, x):
        mine = piece(group, z, x)
        return send(mine, mine, whole_send, whole_recv, (group, 2 * z + x), device_of(z, x))

    def passed(group, ref, index):
        return send(ref, ref, pass_send, pass_recv, (group, index), neighbour)

    def near(group):
        return send(near_box.at[box(group), :], near_land.at[box(group), :], near_send, near_recv, group, neighbour)

    others = ((3, 1), (3, 0), (0, 1))

    def portion(group, index):
        z, x = others[index]
        src = outbox.at[pl.ds(pl.multiple_of(base[group] // 2 + inside(group, at[z], beside(x)), 16), part[group]), :]
        return send(src, landed(group, index), part_send, part_recv, (group, index), device_of(z, x))

    def start_near(group):
        theirs = packed[half_of(group, 1 - core), :] * scale[half_of(group, 1 - core), :]
        near_box[box(group), :] = theirs.astype(jnp.bfloat16)
        near(group).start()
        mine = packed.at[half_of(group, core), :]
        mine[...] = mine[...] * scale[half_of(group, core), :]

    def start_scatter(group):
        near(group).wait()
        mine = packed.at[half_of(group, core), :]
        total = mine[...] + near_land[box(group), :].astype(jnp.float32)
        mine[...] = total
        outbox[box(group), :] = total.astype(jnp.bfloat16)
        for index in range(3):
            portion(group, index).start()

    everyone = ((3, 1, 0), (3, 1, 1), (3, 0, 0), (3, 0, 1), (0, 1, 0), (0, 1, 1), (0, 0, 1))

    def direct(index):
        z, x, c = everyone[index]
        there = 1 - core if c else core
        src = late_box.at[pl.ds(pl.multiple_of(there * half[1] + inside(1, at[z], beside(x)), 16), part[1]), :]
        device = {"tm": 2 * at[z] + there, "pix": beside(x)}
        return send(src, late_land.at[index], late_send, late_recv, index, device)

    def scatter_late():
        region = packed.at[base[1] : base[1] + 2 * half[1], :]
        final = span_of(1, len(WIDTHS[1]) - 1)
        last = lax.dot_general(
            series[:, final],
            series[days - BLOCK : days, final],
            (((1,), (1,)), ((), ())),
            preferred_element_type=jnp.float32,
        )
        total = (region[...] + last) * scale[base[1] : base[1] + 2 * half[1], :]
        region[...] = total
        late_box[...] = total.astype(jnp.bfloat16)
        for index in range(len(everyone)):
            direct(index).start()

    def start_gather(group):
        total = packed[part_of(group, core, chip, side), :]
        if group == 0:
            for index in range(3):
                portion(group, index).wait()
                total = total + landed(group, index)[...].astype(jnp.float32)
        else:
            for index in range(len(everyone)):
                direct(index).wait()
                total = total + late_land[index].astype(jnp.float32)
        mine = own(group)
        mine[...] = total.astype(jnp.bfloat16)
        for z, x in GATHER_ORDER:
            whole(group, z, x).start()
        passed(group, mine, 0).start()

    def pass_on(group, froms, first):
        for index, (z, x) in enumerate(froms):
            gotten(group, z, x).wait_recv()
            passed(group, piece(group, z, x), index + first).start()

    def end_pass(group, froms, first):
        if first:
            passed(group, own(group), 0).wait_recv()
        for index, (z, x) in enumerate(froms):
            passed(group, piece(group, z, x), index + first).wait()

    @pl.when(inner == 1)
    def _():
        write_scale(scale, blocks)
        froms = ((0, 1), (3, 0), (3, 1))
        for group in range(2):
            for chunk in chunks[group]:
                keep(group, chunk).wait()
                for z, c in ((0, 1), (1, 0), (1, 1), (3, 0), (3, 1), (2, 0), (2, 1)):
                    arrival(group, chunk, z, c).wait_recv()
                for j in range(blocks - 1) if group == 0 else (blocks - 1,):
                    if group == 0 or chunk < len(WIDTHS[1]) - 1:
                        add_column(series.at[:, span_of(group, chunk)], packed, j, chunk == 0)
            if group == 0:
                start_near(0)
                start_scatter(0)
        scatter_late()
        start_gather(0)
        start_gather(1)
        pass_on(0, froms, 1)
        end_pass(0, froms, 1)

    @pl.when(inner == 0)
    def _():
        for group in range(2):
            for chunk in chunks[group]:
                for z, c in OUTER_ORDER:
                    exchange(group, chunk, z, c).wait_send()
        pass_on(0, ((1, 0), (1, 1), (2, 0), (2, 1)), 0)
        end_pass(0, ((1, 0), (1, 1), (2, 0), (2, 1)), 0)

    own_count = operator.shape[0]
    write_early_gram(gathered, operator, early_gram, 0, CUT)

    @pl.when(inner == 1)
    def _():
        pass_on(1, ((0, 1), (3, 0), (3, 1)), 1)

    @pl.when(inner == 0)
    def _():
        pass_on(1, ((1, 0), (1, 1), (2, 0), (2, 1)), 0)

    mine = pl.ds(pl.multiple_of(core * half[1], BLOCK), half[1])
    add_half(operator, gathered[half_of(1, core), :], mine, own_half)
    write_early_gram(gathered, operator, early_gram, CUT, own_count)

    @pl.when(inner == 1)
    def _():
        end_pass(1, ((0, 1), (3, 0), (3, 1)), 1)
        for group in range(2):
            for chunk in chunks[group]:
                for z, c in INNER_ORDER:
                    exchange(group, chunk, z, c).wait_send()
            for z, x in GATHER_ORDER:
                whole(group, z, x).wait_send()
            passed(group, own(group), 0).wait_send()

    @pl.when(inner == 0)
    def _():
        end_pass(1, ((1, 0), (1, 1), (2, 0), (2, 1)), 0)

    out[...] = gathered[half_of(1, 1 - core), :]


def direct_covariance(anomaly, offsets, taper_index):
    per_device, pixels = anomaly.shape
    peers, across = lax.axis_size("tm"), lax.axis_size("pix")
    days = per_device * peers
    own = NF // peers
    blocks = days // BLOCK
    owners = 4 * across
    rows = -(-(blocks * (blocks + 1) // 2 * BLOCK) // (16 * owners)) * 16 * owners
    half, part = rows // 2, rows // owners
    others = owners // 2 - 1
    vmem = pl.BlockSpec(memory_space=pltpu.VMEM)
    hbm = pl.BlockSpec(memory_space=pl.ANY)
    counts = [(2,), (2, others), (2, peers), (2, others + 1)]
    return pl.pallas_call(
        direct_kernel,
        out_shape=(
            jax.ShapeDtypeStruct((days // 2, BLOCK), jnp.bfloat16),
            jax.ShapeDtypeStruct((own, 2 * NB, days), jnp.bfloat16),
            jax.ShapeDtypeStruct((own, 2 * NB, 2 * NB), jnp.float32),
            jax.ShapeDtypeStruct((own * 2 * NB, BLOCK), jnp.float32),
        ),
        in_specs=[hbm, hbm, hbm],
        out_specs=(vmem, vmem, vmem, vmem),
        scratch_shapes=[
            pltpu.VMEM((rows, BLOCK), jnp.float32),
            pltpu.VMEM((rows, BLOCK), jnp.float32),
            pltpu.VMEM((half, BLOCK), jnp.bfloat16),
            pltpu.VMEM((half, BLOCK), jnp.bfloat16),
            pltpu.VMEM((half, BLOCK), jnp.bfloat16),
            pltpu.VMEM((others, part, BLOCK), jnp.bfloat16),
            pltpu.VMEM((rows, BLOCK), jnp.bfloat16),
            pltpu.VMEM((16, NB), jnp.int32),
            pltpu.SemaphoreType.DMA((2, max(map(len, WIDTHS)))),
            pltpu.SemaphoreType.DMA((2,)),
            pltpu.SemaphoreType.DMA((2, max(map(len, WIDTHS)), peers)),
            pltpu.SemaphoreType.DMA((2, max(map(len, WIDTHS)), peers)),
        ]
        + [pltpu.SemaphoreType.DMA(count) for count in counts for _ in range(2)]
        + [
            pltpu.VMEM((days, BLOCK), jnp.bfloat16),
            pltpu.VMEM((owners - 1, days // owners, BLOCK), jnp.bfloat16),
            pltpu.SemaphoreType.DMA((owners - 1,)),
            pltpu.SemaphoreType.DMA((owners - 1,)),
        ]
        + [pltpu.VMEM((days, sum(WIDTHS[0])), jnp.bfloat16)],
        compiler_params=pltpu.CompilerParams(
            collective_id=0, has_side_effects=True, vmem_limit_bytes=DIRECT_VMEM
        ),
        name="covariance",
    )(*(pltpu.with_memory_space_constraint(each, pltpu.HBM) for each in (anomaly, offsets[None, :], taper_index[None, :])))


def leading(matrix, size):
    own = matrix.shape[0]
    vector = jnp.ones((own, 1, size), jnp.float32)
    for step in range(POWER + 1):
        across = 2 - step % 2
        applied = jnp.sum(matrix * vector, axis=across, keepdims=True)
        power = jnp.sum(applied * applied, axis=3 - across, keepdims=True) / size
        vector = applied * lax.rsqrt(power + power_eps)
    column = jnp.broadcast_to(jnp.sqrt(power)[:, 0, :], (own, own))
    square = (own, own)
    diagonal = lax.broadcasted_iota(jnp.int32, square, 0) == lax.broadcasted_iota(jnp.int32, square, 1)
    return jnp.sum(jnp.where(diagonal, column, 0.0), axis=0, keepdims=True)


def direct_finish_kernel(pixels, late, operator, early_gram, own_half, gram, lead, held, sem):
    own, size, days = operator.shape
    other = pl.ds(pl.multiple_of((1 - lax.rem(lax.axis_index("tm"), 2)) * (days // 2), BLOCK), days // 2)
    group = math.gcd(own, 4)
    copies = []
    for first in range(0, own, group):
        left = operator[first : first + group, :, other].reshape(group * size, days // 2)
        half = lax.dot_general(left, late[...], (((1,), (0,)), ((), ())), preferred_element_type=jnp.float32)
        half = (half + own_half[first * size : (first + group) * size, :]).astype(jnp.bfloat16)
        for f in range(group):
            mine = half[f * size : (f + 1) * size]
            weights = operator[first + f, :, days - BLOCK : days]
            value = both_ways(mine, weights)
            held[first + f] = (early_gram[first + f] + value) * (1.0 / pixels)
        chosen = pl.ds(first, group)
        copy = pltpu.make_async_copy(held.at[chosen], gram.at[chosen], sem.at[first // group])
        copy.start()
        copies.append(copy)
    lead[...] = leading(held[...], size)
    for copy in copies:
        copy.wait()


def direct_finish(late, operator, early_gram, own_half, pixels):
    own, size, days = operator.shape
    vmem = pl.BlockSpec(memory_space=pltpu.VMEM)
    gram, lead = pl.pallas_call(
        functools.partial(direct_finish_kernel, pixels),
        out_shape=(
            jax.ShapeDtypeStruct((own, size, size), jnp.float32),
            jax.ShapeDtypeStruct((1, own), jnp.float32),
        ),
        in_specs=[vmem] * 4,
        out_specs=(pl.BlockSpec(memory_space=pl.ANY), vmem),
        scratch_shapes=[
            pltpu.VMEM((own, size, size), jnp.float32),
            pltpu.SemaphoreType.DMA((own // math.gcd(own, 4),)),
        ],
        compiler_params=pltpu.CompilerParams(vmem_limit_bytes=24 * 2**20),
        name="finish",
    )(late, operator, early_gram, own_half)
    return gram, lead[0]


def shards(anomaly, offsets, taper_index):
    total_pixels = anomaly.shape[1] * lax.axis_size(("pix", "sub"))
    peers, sub = lax.axis_size("tm"), lax.axis_size("sub")
    if sub == 1 and peers == 8 and lax.axis_size("pix") == 2 and anomaly.shape == (64, 4 * sum(WIDTHS[0])):
        return direct_finish(*direct_covariance(anomaly, offsets, taper_index), total_pixels)
    covariance, operator, operator_low = covariance_and_operator(anomaly, offsets, taper_index)
    return gram_and_leading(covariance, operator, operator_low, total_pixels)


def solution(mesh):
    placed = (P("tm", ("group", "pix", "sub")), P(), P())
    return jax.shard_map(
        shards,
        mesh=mesh,
        in_specs=placed,
        out_specs=(P(("group", "tm"), None, None), P(("group", "tm"))),
        check_vma=False,
    )
```
